32 devices in a mesh: dp: 8 (over z, x), tensor: 4 (over y, core).
Axes of the slice: x: 2, y: 2, z: 4, core: 2. Of those that a mesh axis runs over, the one named last changes fastest.
Arguments:
- tokens: bfloat16 [8192, 1024], P('dp'), may hold values from -6 to 6
- cotangent: bfloat16 [8192, 1024], P('dp'), may hold values from -6 to 6
- segments: int32 [8, 1024], P('dp'), may hold values from 0 to 3, never falling along the last dimension, each value on 1 to 512 neighbouring positions
- norm_gain: float32 [1024], replicated, may hold values from 0.5 to 1.5
- gate_proj: bfloat16 [1024, 2048], P(None, 'tensor'), may hold values from -0.1875 to 0.1875
- value_proj: bfloat16 [1024, 2048], P(None, 'tensor'), may hold values from -0.1875 to 0.1875
- shared_proj: bfloat16 [1024, 256], replicated, may hold values from -0.1875 to 0.1875
- step_proj: bfloat16 [1024, 32], P(None, 'tensor'), may hold values from -0.1875 to 0.1875
- conv_value: float32 [4, 2048], P(None, 'tensor'), may hold values from -3 to 3
- bias_value: float32 [2048], P('tensor'), may hold values from -3 to 3
- conv_shared: float32 [4, 256], replicated, may hold values from -3 to 3
- bias_shared: float32 [256], replicated, may hold values from -3 to 3
- step_bias: float32 [32], P('tensor'), may hold values from -3 to -1
- decay_log: float32 [32], P('tensor'), may hold values from -4 to 0.5
- skip_gain: float32 [32], P('tensor'), may hold values from 0.5 to 1.5
- gate_gain: float32 [2048], P('tensor'), may hold values from 0.5 to 1.5
- out_proj: bfloat16 [1024, 2048], P(None, 'tensor'), may hold values from -0.125 to 0.125
Outputs:
- result: bfloat16 [8192, 1024], P('dp')
- grad_tokens: bfloat16 [8192, 1024], P('dp')
- grad_norm_gain: float32 [1024], P('tensor')
- grad_gate_proj: float32 [1024, 2048], P('dp', 'tensor')
- grad_value_proj: float32 [1024, 2048], P('dp', 'tensor')
- grad_shared_proj: float32 [1024, 256], P('dp')
- grad_step_proj: float32 [1024, 32], P('dp', 'tensor')
- grad_conv_value: float32 [4, 2048], P(None, 'tensor')
- grad_bias_value: float32 [2048], P('tensor')
- grad_conv_shared: float32 [4, 256], replicated
- grad_bias_shared: float32 [256], replicated
- grad_step_bias: float32 [32], P('tensor')
- grad_decay_log: float32 [32], P('tensor')
- grad_skip_gain: float32 [32], P('tensor')
- grad_gate_gain: float32 [2048], P('tensor')
- grad_out_proj: float32 [1024, 2048], P('dp', 'tensor')
The draws below stay inside these ranges and needn't reach their ends.
Inputs may be any that keep to these rules, and one draw needn't show every extreme that they name: `segments`: within a row of 1024 tokens the numbers never fall; a segment holds 1 to 512 tokens.
All inputs are finite; a program needn't handle non-finite values.
Results may differ from the reference program's by a relative error of at most 0.012.
Values may be sent and summed in bfloat16 or wider, within the bound.
A program may use at most 192 MiB of HBM per device.

```python
import math
from functools import partial
import jax
import jax.numpy as jnp
import numpy as np
from jax import lax

D = 1024
H = 32
HSIZE = 64
N = 128
DI = 2048
CONV = 4
SPAN = 256
SEQ = 1024
ROWS = 8
TOKENS = 8192


def block_scale(rng, dims, cuts, smallest, largest):
    def one(position, shards_of):
        steps = jax.random.uniform(jax.random.fold_in(jax.random.fold_in(rng, 6), position), (shards_of,), jnp.float32, smallest / len(cuts), largest / len(cuts))
        return jnp.repeat(jnp.exp(steps), dims[position] // shards_of).reshape((-1,) + (1,) * (len(dims) - position - 1))

    level = one(*cuts[0])
    for cut in cuts[1:]:
        level = level * one(*cut)
    return level


def split_up(count, total, bound, lean):
    loads = [(1 << 20) // math.isqrt(rank ** lean) + 1 for rank in range(2, count + 1)]
    surplus, holding = total - bound - (count - 1), [1] * (count - 1)
    while surplus > 0:
        movable = [i for i in range(count - 1) if holding[i] < bound]
        mass, remaining = sum([loads[i] for i in movable]), surplus
        for i in movable:
            addition = min(bound - holding[i], max(1, remaining * loads[i] // mass), surplus)
            holding[i] = holding[i] + addition
            surplus = surplus - addition
    return np.array([bound] + holding)


def uneven_parts(own_key, amount, total, most, slope):
    if amount == 2:
        one = jax.random.randint(own_key, (), max(1, total - most), min(most, total - 1) + 1)
        return jnp.stack([one, total - one])
    lengths = jnp.asarray(split_up(amount, total, most, slope), jnp.int32)
    pairs = (amount - 1) // 2
    giver, taker = lengths[1:1 + 2 * pairs:2], lengths[2:2 + 2 * pairs:2]
    room = jnp.minimum(giver - 1, most - taker)
    passed = jax.random.randint(jax.random.fold_in(own_key, 1), (pairs,), 0, 1 << 20) % (room + 1)
    lengths = lengths.at[1:1 + 2 * pairs:2].set(giver - passed).at[2:2 + 2 * pairs:2].set(taker + passed)
    return lengths[jax.random.permutation(jax.random.fold_in(own_key, 2), amount)]


def bell_draw(stream_key, shape, spread, bound, cuts=(), held_as=jnp.bfloat16):
    loudness = block_scale(stream_key, shape, cuts, -0.22, 0.18) if cuts else 1.0
    values = jax.random.normal(stream_key, shape, jnp.float32) * spread * loudness
    return jnp.minimum(jnp.maximum(values, -bound), bound).astype(held_as)


def setup_inputs(seed: int = 0) -> dict:
    arg_keys = jax.random.split(jax.random.key(seed), 18)
    return {
        "tokens": bell_draw(arg_keys[0], (TOKENS, D), 1.0, 6.0, ((0, 8),)),
        "cotangent": bell_draw(arg_keys[1], (TOKENS, D), 1.0, 6.0, ((0, 8),)),
        "segments": jax.vmap(lambda own: jnp.searchsorted(jnp.cumsum(uneven_parts(own, 4, SEQ, SEQ // 2, 2)), jnp.arange(SEQ), side="right"))(jax.random.split(arg_keys[2], ROWS)).reshape((ROWS, SEQ)).astype(jnp.int32),
        "norm_gain": jnp.clip(1.0 + 0.1 * jax.random.normal(arg_keys[3], (D,), jnp.float32), 0.5, 1.5),
        "gate_proj": bell_draw(arg_keys[4], (D, DI), D ** -0.5, 0.1875, ((1, 4),)),
        "value_proj": bell_draw(arg_keys[5], (D, DI), D ** -0.5, 0.1875, ((1, 4),)),
        "shared_proj": bell_draw(arg_keys[6], (D, 2 * N), D ** -0.5, 0.1875),
        "step_proj": bell_draw(arg_keys[7], (D, H), D ** -0.5, 0.1875, ((1, 4),)),
        "conv_value": bell_draw(arg_keys[8], (CONV, DI), CONV ** -0.5, 3.0, ((1, 4),), jnp.float32),
        "bias_value": bell_draw(arg_keys[9], (DI,), 0.5, 3.0, ((0, 4),), jnp.float32),
        "conv_shared": bell_draw(arg_keys[10], (CONV, 2 * N), CONV ** -0.5, 3.0, (), jnp.float32),
        "bias_shared": bell_draw(arg_keys[11], (2 * N,), 0.5, 3.0, (), jnp.float32),
        "step_bias": jnp.clip(-3.0 + 2.0 * jax.random.uniform(arg_keys[12], (H,), jnp.float32) ** block_scale(arg_keys[12], (H,), ((0, 4),), -0.2, 0.2), -3.0, -1.0),
        "decay_log": jnp.clip(-4.0 + 4.5 * jax.random.uniform(arg_keys[13], (H,), jnp.float32) ** block_scale(arg_keys[13], (H,), ((0, 4),), -0.2, 0.2), -4.0, 0.5),
        "skip_gain": jnp.clip(0.5 + 1.0 * jax.random.uniform(arg_keys[14], (H,), jnp.float32) ** block_scale(arg_keys[14], (H,), ((0, 4),), -0.2, 0.2), 0.5, 1.5),
        "gate_gain": jnp.clip(1.0 + 0.1 * jax.random.normal(arg_keys[15], (DI,), jnp.float32), 0.5, 1.5),
        "out_proj": bell_draw(arg_keys[16], (D, DI), DI ** -0.5, 0.125, ((1, 4),)),
    }


EPSILON = 1e-05
NEG_FILL = -1e+30
EXACT = lax.Precision.HIGHEST

def silu_grad(inputs):
    sigmoid = jax.nn.sigmoid(inputs)
    return sigmoid * (1.0 + inputs * (1.0 - sigmoid))

def causal_conv(inputs, kernel, shift_bias, seg_ids):
    kernel_len = kernel.shape[0]
    length = inputs.shape[0]
    padded = jnp.pad(inputs, ((kernel_len - 1, 0), (0, 0)))
    padded_ids = jnp.pad(seg_ids, (kernel_len - 1, 0), constant_values=-1)
    result = jnp.zeros_like(inputs) + shift_bias[None, :]
    for offset in range(kernel_len):
        shifted = padded[offset:offset + length]
        same_doc = (padded_ids[offset:offset + length] == seg_ids)[:, None]
        result = result + jnp.where(same_doc, shifted, 0.0) * kernel[offset][None, :]
    return result

def state_scan(values, step_sizes, decay_rates, write_in, read_out, seg_ids):
    length, head_count, head_size = values.shape
    state_size = write_in.shape[1]
    blocks = length // SPAN

    def one_block(carried, pieces):
        memory, last_id = carried
        block_vals, block_steps, block_write, block_read, block_ids = pieces
        log_decay = jnp.cumsum(block_steps * decay_rates[None, :], axis=0)
        intersections = jnp.dot(block_read, block_write.T, precision=EXACT, preferred_element_type=jnp.float32)
        causal = jnp.arange(SPAN)[:, None] >= jnp.arange(SPAN)[None, :]
        allowed = causal & (block_ids[:, None] == block_ids[None, :])
        gaps = log_decay[:, None, :] - log_decay[None, :, :]
        weights = jnp.exp(jnp.where(allowed[:, :, None], gaps, NEG_FILL)) * intersections[:, :, None]
        scaled = block_vals * block_steps[:, :, None]
        within = jnp.einsum('tsh,shp->thp', weights, scaled, precision=EXACT)
        entering = (block_ids == last_id).astype(jnp.float32)
        carried_in = jnp.einsum('tn,hnp->thp', block_read, memory, precision=EXACT)
        carried_in = carried_in * (jnp.exp(log_decay) * entering[:, None])[:, :, None]
        leaving = (block_ids == block_ids[-1]).astype(jnp.float32)
        to_end = jnp.exp(log_decay[-1][None, :] - log_decay) * leaving[:, None]
        fresh = jnp.einsum('sn,shp->hnp', block_write, scaled * to_end[:, :, None], precision=EXACT)
        continued = (block_ids[-1] == last_id).astype(jnp.float32)
        memory = memory * (continued * jnp.exp(log_decay[-1]))[:, None, None] + fresh
        return ((memory, block_ids[-1]), within + carried_in)
    pieces = (values.reshape(blocks, SPAN, head_count, head_size), step_sizes.reshape(blocks, SPAN, head_count), write_in.reshape(blocks, SPAN, state_size), read_out.reshape(blocks, SPAN, state_size), seg_ids.reshape(blocks, SPAN))
    initial = (jnp.zeros((head_count, state_size, head_size), values.dtype), jnp.array(-1, seg_ids.dtype))
    final_state, outputs = lax.scan(one_block, initial, pieces)
    return outputs.reshape(length, head_count, head_size)

def value_path(value_pre, step_pre, conv_value, bias_value, step_bias, decay_log, skip_gain, write_in, read_out, seg_ids):
    activated = jax.nn.silu(causal_conv(value_pre, conv_value, bias_value, seg_ids))
    step_sizes = jax.nn.softplus(step_pre + step_bias[None, :])
    decay_rates = -jnp.exp(decay_log)
    length = activated.shape[0]
    head_count = step_pre.shape[1]
    values = activated.reshape(length, head_count, HSIZE)
    mixed = state_scan(values, step_sizes, decay_rates, write_in, read_out, seg_ids) + values * skip_gain[None, :, None]
    return mixed.reshape(length, head_count * HSIZE)

def shared_path(shared_pre, conv_shared, bias_shared, seg_ids):
    activated = jax.nn.silu(causal_conv(shared_pre, conv_shared, bias_shared, seg_ids))
    half_width = activated.shape[1] // 2
    return (activated[:, :half_width], activated[:, half_width:])

def back_dot(left, right):
    return lax.dot_general(left, right, (((1,), (1,)), ((), ())), preferred_element_type=jnp.float32)

def left_dot(left, right):
    return lax.dot_general(left, right, (((0,), (0,)), ((), ())), preferred_element_type=jnp.float32)

def reference(tokens, cotangent, segments, norm_gain, gate_proj, value_proj, shared_proj, step_proj, conv_value, bias_value, conv_shared, bias_shared, step_bias, decay_log, skip_gain, gate_gain, out_proj):
    row_count = segments.shape[0]
    row_len = segments.shape[1]
    token_rows = tokens.reshape(row_count, row_len, D)
    cot_rows = cotangent.reshape(row_count, row_len, D)

    def row_pass(totals, row_data):
        row_tokens, row_cot, seg_ids = row_data
        inputs_f = row_tokens.astype(jnp.float32)
        inv_in = lax.rsqrt(lax.optimization_barrier(jnp.mean(inputs_f * inputs_f, axis=1, keepdims=True)) + EPSILON)
        normed = inputs_f * inv_in
        hidden = (normed * norm_gain[None, :]).astype(jnp.bfloat16)
        gate_pre = jnp.dot(hidden, gate_proj, preferred_element_type=jnp.float32)
        value_pre = jnp.dot(hidden, value_proj, preferred_element_type=jnp.float32)
        shared_pre = jnp.dot(hidden, shared_proj, preferred_element_type=jnp.float32)
        step_pre = jnp.dot(hidden, step_proj, preferred_element_type=jnp.float32)
        (write_in, read_out), shared_back = jax.vjp(partial(shared_path, seg_ids=seg_ids), shared_pre, conv_shared, bias_shared)
        mixer, mixer_back = jax.vjp(partial(value_path, seg_ids=seg_ids), value_pre, step_pre, conv_value, bias_value, step_bias, decay_log, skip_gain, write_in, read_out)
        gate_act = jax.nn.silu(gate_pre)
        gated = mixer * gate_act
        inv_gate = lax.rsqrt(lax.optimization_barrier(jnp.sum(gated * gated, axis=1)) / DI + EPSILON)[:, None]
        normal_out = (gated * inv_gate * gate_gain[None, :]).astype(jnp.bfloat16)
        mixed = back_dot(normal_out, out_proj)
        row_result = (inputs_f + mixed).astype(jnp.bfloat16)
        upstream = row_cot.astype(jnp.float32)
        grad_normal = jnp.dot(row_cot, out_proj, preferred_element_type=jnp.float32)
        grad_gate_gain = lax.optimization_barrier(jnp.sum(grad_normal * gated * inv_gate, axis=0))
        weighted = grad_normal * gate_gain[None, :]
        dots_gate = lax.optimization_barrier(jnp.sum(weighted * gated, axis=1))
        grad_gated = inv_gate * weighted - gated * (inv_gate * inv_gate * inv_gate) * (dots_gate / DI)[:, None]
        grad_mixer = grad_gated * gate_act
        grad_gate_pre = grad_gated * mixer * silu_grad(gate_pre)
        grad_value_pre, grad_step_pre, grad_conv_value, grad_bias_value, grad_step_bias, grad_decay_log, grad_skip_gain, write_grad, read_grad = mixer_back(grad_mixer)
        grad_shared_pre, grad_conv_shared, grad_bias_shared = shared_back((write_grad, read_grad))
        gate_low = grad_gate_pre.astype(jnp.bfloat16)
        value_low = grad_value_pre.astype(jnp.bfloat16)
        step_low = grad_step_pre.astype(jnp.bfloat16)
        shared_low = grad_shared_pre.astype(jnp.bfloat16)
        grad_hidden = back_dot(gate_low, gate_proj) + back_dot(value_low, value_proj) + back_dot(step_low, step_proj)
        grad_hidden = grad_hidden + back_dot(shared_low, shared_proj)
        grad_norm_gain = lax.optimization_barrier(jnp.sum(grad_hidden * normed, axis=0))
        scaled = grad_hidden * norm_gain[None, :]
        grad_row = inv_in * (scaled - normed * lax.optimization_barrier(jnp.mean(scaled * normed, axis=1, keepdims=True))) + upstream
        grad_row = grad_row.astype(jnp.bfloat16)
        terms = (grad_norm_gain, left_dot(hidden, gate_low), left_dot(hidden, value_low), left_dot(hidden, shared_low), left_dot(hidden, step_low), grad_conv_value, grad_bias_value, grad_conv_shared, grad_bias_shared, grad_step_bias, grad_decay_log, grad_skip_gain, grad_gate_gain, left_dot(row_cot, normal_out))
        totals = tuple((total + term for total, term in zip(totals, terms)))
        return (totals, (row_result, grad_row))
    params = (norm_gain, gate_proj, value_proj, shared_proj, step_proj, conv_value, bias_value, conv_shared, bias_shared, step_bias, decay_log, skip_gain, gate_gain, out_proj)
    initial = tuple((jnp.zeros(param.shape, jnp.float32) for param in params))
    finals, (result_rows, grad_rows) = lax.scan(row_pass, initial, (token_rows, cot_rows, segments))
    return (result_rows.reshape(tokens.shape), grad_rows.reshape(tokens.shape), finals[0], finals[1], finals[2], finals[3], finals[4], finals[5], finals[6], finals[7], finals[8], finals[9], finals[10], finals[11], finals[12], finals[13])
```

```python
import jax
import jax.numpy as jnp
from jax import lax
from jax.experimental import pallas as pl
from jax.experimental.pallas import tpu as pltpu
from jax.sharding import PartitionSpec as P

SPAN = 256
HSIZE = 64
LANES = 128
EPSILON = 1e-05
NEG_FILL = -1e30
EXACT = lax.Precision.HIGHEST
F32 = jnp.float32
BF16 = jnp.bfloat16


def mm(left, right):
    return jnp.dot(left, right, preferred_element_type=F32)


def mm_t(left, right):
    return lax.dot_general(left, right, (((1,), (1,)), ((), ())), preferred_element_type=F32)


def t_mm(left, right):
    return lax.dot_general(left, right, (((0,), (0,)), ((), ())), preferred_element_type=F32)


def exact(left, right):
    return jnp.dot(left, right, precision=EXACT, preferred_element_type=F32)


def sigmoid(v):
    return 1.0 / (1.0 + jnp.exp(-v))


def spread(cols, pairs):
    low = lax.broadcasted_iota(jnp.int32, (cols.shape[0], LANES), 1) < HSIZE
    parts = [
        jnp.where(low, cols[:, 2 * p : 2 * p + 1], cols[:, 2 * p + 1 : 2 * p + 2])
        for p in range(pairs)
    ]
    return jnp.concatenate(parts, axis=1)


def gather_mat(inner):
    channel = lax.broadcasted_iota(jnp.int32, (inner, LANES), 0) // HSIZE
    head = lax.broadcasted_iota(jnp.int32, (inner, LANES), 1)
    return (channel == head).astype(F32)


def grid_masks():
    row = lax.broadcasted_iota(jnp.int32, (SPAN, SPAN), 0)
    col = lax.broadcasted_iota(jnp.int32, (SPAN, SPAN), 1)
    return row, col


def conv_fwd(buf, pack, aux):
    out = pack[4:5, :] + buf[8 : 8 + SPAN, :] * pack[3:4, :]
    for j in range(1, 4):
        out = out + buf[8 - j : 8 - j + SPAN, :] * (aux[:, j : j + 1] * pack[3 - j : 4 - j, :])
    return out


def fwd_kernel(
    tok, cot, aux_ref, segr, ng, wg, wv, ws, wst, wo, chp, shp, hp,
    hidden_o, gate_o, vpre_o, cv_o, spre_o, scv_o, z_o, ld_o, ldt_o, yn_o, sin_o, gn_o, stat_o,
    vbuf, sbuf, state,
):
    inner = wg.shape[1]
    pairs = inner // LANES
    state_size = ws.shape[1] // 2

    @pl.when(pl.program_id(0) == 0)
    def _():
        vbuf[0:8, :] = jnp.zeros((8, inner), F32)
        sbuf[0:8, :] = jnp.zeros((8, 2 * state_size), F32)
        state[...] = jnp.zeros_like(state)

    aux = aux_ref[...]
    x = tok[...].astype(F32)
    inv = lax.rsqrt(jnp.mean(x * x, axis=1, keepdims=True) + EPSILON)
    hid = (x * inv * ng[...]).astype(BF16)
    hidden_o[...] = hid
    gate = mm(hid, wg[...])
    gate_o[...] = gate
    vp = mm(hid, wv[...])
    vpre_o[...] = vp
    vbuf[8 : 8 + SPAN, :] = vp
    sp = mm(hid, ws[...])
    spre_o[...] = sp
    sbuf[8 : 8 + SPAN, :] = sp
    z = mm(hid, wst[...]) + hp[0:1, :]
    z_o[...] = z
    gn = mm(cot[...], wo[...])
    gn_o[...] = gn
    scv = conv_fwd(sbuf, shp, aux)
    scv_o[...] = scv
    bc = (scv * sigmoid(scv)).astype(BF16)
    b_low, c_low = bc[:, :state_size], bc[:, state_size:]
    cv = conv_fwd(vbuf, chp, aux)
    cv_o[...] = cv
    vbuf[0:8, :] = vbuf[SPAN : SPAN + 8, :]
    sbuf[0:8, :] = sbuf[SPAN : SPAN + 8, :]
    values = cv * sigmoid(cv)
    dt = jnp.maximum(z, 0.0) + jnp.log1p(jnp.exp(-jnp.abs(z)))
    row, col = grid_masks()
    tri = (row >= col).astype(F32)
    ld = exact(tri, dt * hp[1:2, :])
    ld_o[...] = ld
    ldt = jnp.transpose(ld)[0:8, :]
    ldt_o[...] = ldt
    allowed = (row >= col) & (aux[:, 0:1] == segr[...])
    scores = jnp.where(allowed, mm_t(c_low, b_low), 0.0)
    xs = values * spread(dt, pairs)
    xs_low = xs.astype(BF16)
    ein = jnp.exp(ld) * aux[:, 4:5]
    eout = jnp.exp(ld[SPAN - 1 : SPAN, :] - ld) * aux[:, 5:6]
    ein_x = spread(ein, pairs)
    eout_x = spread(eout, pairs)
    old = state[...]
    sin_o[...] = old
    carried = mm(c_low, old.astype(BF16)) * ein_x
    state[...] = old * ein_x[SPAN - 1 : SPAN, :] + t_mm(b_low, (xs * eout_x).astype(BF16))
    low = lax.broadcasted_iota(jnp.int32, (SPAN, LANES), 1) < HSIZE
    parts = []
    for p in range(pairs):
        pair = xs_low[:, p * LANES : (p + 1) * LANES]
        outs = []
        for h in (2 * p, 2 * p + 1):
            gap = jnp.minimum(ld[:, h : h + 1] - ldt[h : h + 1, :], 0.0)
            outs.append(mm((jnp.exp(gap) * scores).astype(BF16), pair))
        parts.append(jnp.where(low, outs[0], outs[1]))
    yn = jnp.concatenate(parts, axis=1) + carried
    yn_o[...] = yn
    gated = (yn + chp[6:7, :] * values) * (gate * sigmoid(gate))
    squares = jnp.sum(gated * gated, axis=1, keepdims=True)
    dots = jnp.sum(gn * chp[5:6, :] * gated, axis=1, keepdims=True)
    lane = lax.broadcasted_iota(jnp.int32, (SPAN, LANES), 1)
    both = jnp.where(lane == 0, squares, jnp.where(lane == 1, dots, 0.0))
    stat_o[...] = jnp.transpose(both)[0:8, :]


def gate_kernel(
    width, gate_ref, cv_ref, yn, gn_ref, stat, chp, wo, normal_o, dy_o, low_o, gain_o, mixed_o
):
    both = jnp.transpose(jnp.concatenate([stat[...]] * (LANES // 8), axis=0))
    inv = lax.rsqrt(both[:, 0:1] / width + EPSILON)
    mean_dots = both[:, 1:2] / width
    gate = gate_ref[...]
    cv = cv_ref[...]
    gn = gn_ref[...]
    sig = sigmoid(gate)
    act = gate * sig
    mixer = yn[...] + chp[6:7, :] * (cv * sigmoid(cv))
    gated = mixer * act
    normed = gated * inv
    normal = (normed * chp[5:6, :]).astype(BF16)
    normal_o[...] = normal
    mixed_o[...] = mm_t(normal, wo[...]).astype(BF16)
    part = jnp.sum(gn * normed, axis=0, keepdims=True)

    @pl.when(pl.program_id(0) == 0)
    def _():
        gain_o[...] = jnp.zeros_like(gain_o)

    gain_o[0:1, :] += part
    grad_gated = inv * (gn * chp[5:6, :]) - gated * (inv * inv * inv) * mean_dots
    dy_o[...] = grad_gated * act
    low_o[...] = (grad_gated * mixer * (sig * (1.0 + gate * (1.0 - sig)))).astype(BF16)


def bwd_kernel(
    dy_ref, cv_ref, vpre, scv_ref, z_ref, ld_ref, ldt_ref, yn, sin, aux_ref, segr, glow,
    wg, wv, wst, chp, hp,
    vlow_o, slow_o, heads_o, dbc_o, chg_o, hg_o,
    dbuf, dstate,
):
    inner = wg.shape[1]
    pairs = inner // LANES
    state_size = sin.shape[0]

    @pl.when(pl.program_id(0) == 0)
    def _():
        dbuf[SPAN : SPAN + 8, :] = jnp.zeros((8, inner), F32)
        dstate[...] = jnp.zeros_like(dstate)
        chg_o[...] = jnp.zeros_like(chg_o)
        hg_o[...] = jnp.zeros_like(hg_o)

    aux = aux_ref[...]
    dy = dy_ref[...]
    dy_low = dy.astype(BF16)
    scv = scv_ref[...]
    bc = (scv * sigmoid(scv)).astype(BF16)
    b_low, c_low = bc[:, :state_size], bc[:, state_size:]
    cv = cv_ref[...]
    csig = sigmoid(cv)
    values = cv * csig
    z = z_ref[...]
    dt = jnp.maximum(z, 0.0) + jnp.log1p(jnp.exp(-jnp.abs(z)))
    ld = ld_ref[...]
    ldt = ldt_ref[...]
    dt_x = spread(dt, pairs)
    xs = values * dt_x
    xs_low = xs.astype(BF16)
    ein = jnp.exp(ld) * aux[:, 4:5]
    eout = jnp.exp(ld[SPAN - 1 : SPAN, :] - ld) * aux[:, 5:6]
    ein_x = spread(ein, pairs)
    eout_x = spread(eout, pairs)
    row, col = grid_masks()
    allowed = (col >= row) & (aux[:, 0:1] == segr[...])
    mask = allowed.astype(F32)
    scores_t = mm_t(b_low, c_low) * mask
    low = lax.broadcasted_iota(jnp.int32, (SPAN, LANES), 1) < HSIZE
    parts = []
    dscores_t = jnp.zeros((SPAN, SPAN), F32)
    for p in range(pairs):
        cols = slice(p * LANES, (p + 1) * LANES)
        dy_pair = dy_low[:, cols]
        xs_pair = xs_low[:, cols]
        zero = jnp.zeros_like(xs_pair)
        outs = []
        for side, h in enumerate((2 * p, 2 * p + 1)):
            gap = jnp.minimum(ldt[h : h + 1, :] - ld[:, h : h + 1], 0.0)
            decay = jnp.exp(gap)
            outs.append(mm((decay * scores_t).astype(BF16), dy_pair))
            mine = jnp.where(low, xs_pair, zero) if side == 0 else jnp.where(low, zero, xs_pair)
            dscores_t = dscores_t + mm_t(mine, dy_pair) * decay
        parts.append(jnp.where(low, outs[0], outs[1]))
    inside = jnp.concatenate(parts, axis=1)
    dscores_low = (dscores_t * mask).astype(BF16)
    old = sin[...]
    dst = dstate[...]
    dst_low = dst.astype(BF16)
    dye_low = (dy * ein_x).astype(BF16)
    xse_low = (xs * eout_x).astype(BF16)
    db = mm(dscores_low, c_low) + mm_t(xse_low, dst_low)
    dc = t_mm(dscores_low, b_low) + mm_t(dye_low, old.astype(BF16))
    late = mm(b_low, dst_low) * eout_x
    keep = ein_x[SPAN - 1 : SPAN, :]
    dstate[...] = dst * keep + t_mm(c_low, dye_low)
    dxs = inside + late
    collect = gather_mat(inner)
    q = dy_low.astype(F32) * yn[...] - xs_low.astype(F32) * inside
    u = xs * late
    kappa = exact(jnp.sum(old * dst, axis=0, keepdims=True) * keep + jnp.zeros((8, inner), F32), collect)
    da = (
        exact((col >= row).astype(F32), exact(q, collect))
        + exact((row > col).astype(F32), exact(u, collect))
        + kappa[0:1, :]
    )
    rates = hp[1:2, :]
    ddt = da * rates + exact(dxs * values, collect)
    dz = ddt * sigmoid(z)
    slow = dz.astype(BF16)
    slow_o[...] = slow
    skip = exact(jnp.sum(dy * values, axis=0, keepdims=True) + jnp.zeros((8, inner), F32), collect)
    hg_o[0:1, :] += jnp.sum(dz, axis=0, keepdims=True)
    hg_o[1:2, :] += jnp.sum(da * dt, axis=0, keepdims=True) * rates
    hg_o[2:3, :] += skip[0:1, :]
    dcv = (dxs * dt_x + chp[6:7, :] * dy) * (csig * (1.0 + cv * (1.0 - csig)))
    dbuf[0:SPAN, :] = dcv
    vp = vpre[...]
    dv = dcv * chp[3:4, :]
    chg_o[3:4, :] += jnp.sum(dcv * vp, axis=0, keepdims=True)
    chg_o[4:5, :] += jnp.sum(dcv, axis=0, keepdims=True)
    for j in range(1, 4):
        moved = dbuf[j : j + SPAN, :] * aux[:, 8 + j : 9 + j]
        dv = dv + moved * chp[3 - j : 4 - j, :]
        chg_o[3 - j : 4 - j, :] += jnp.sum(moved * vp, axis=0, keepdims=True)
    dbuf[SPAN : SPAN + 8, :] = dbuf[0:8, :]
    vlow = dv.astype(BF16)
    vlow_o[...] = vlow
    back = mm_t(glow[...], wg[...]) + mm_t(vlow, wv[...]) + mm_t(slow, wst[...])
    heads_o[...] = back.astype(BF16)
    dbc_o[...] = jnp.concatenate([db, dc], axis=1)


MESH = pl.DeviceIdType.MESH
PIECES = 4


def prep_kernel(
    seg, stepw, conv_v, bias_v, gate_g, skip_g, conv_s, bias_s, step_b, decay,
    aux_o, segr_o, wst_o, chp_o, shp_o, hp_o,
):
    length = seg.shape[1]
    ids = seg[...].astype(F32)
    segr_o[...] = ids
    wide = ids + jnp.zeros((8, length), F32)
    lane = lax.broadcasted_iota(jnp.int32, (8, length), 1)
    row = lax.broadcasted_iota(jnp.int32, (8, length), 0)
    ends = [
        ids[:, start + SPAN - 1 : start + SPAN] + jnp.zeros((8, SPAN), F32)
        for start in range(0, length, SPAN)
    ]
    last = jnp.concatenate(ends, axis=1)
    before = jnp.concatenate([jnp.full((8, SPAN), -1.0, F32)] + ends[:-1], axis=1)
    first = jnp.where(row == 0, wide, 0.0)
    first = jnp.where((row == 4) & (wide == before), 1.0, first)
    first = jnp.where((row == 5) & (wide == last), 1.0, first)
    second = jnp.zeros((8, length), F32)
    for j in range(1, 4):
        back = (pltpu.roll(wide, j, 1) == wide) & (lane >= j)
        ahead = (pltpu.roll(wide, length - j, 1) == wide) & (lane < length - j)
        first = jnp.where((row == j) & back, 1.0, first)
        second = jnp.where((row == j) & ahead, 1.0, second)
    rest = jnp.zeros((LANES - 16, length), F32)
    aux_o[...] = jnp.transpose(jnp.concatenate([first, second, rest], axis=0))
    heads, width = stepw.shape
    steps = jnp.concatenate([stepw[...].astype(F32), jnp.zeros((LANES - heads, width), F32)], axis=0)
    wst_o[...] = jnp.transpose(steps).astype(BF16)
    hp_o[...] = jnp.zeros_like(hp_o)
    hp_o[0:1, 0:heads] = step_b[...]
    hp_o[1:2, 0:heads] = -jnp.exp(decay[...])
    hp_o[2:3, 0:heads] = skip_g[...]
    inner = chp_o.shape[1]
    repeated = lax.dot_general(
        hp_o[...], gather_mat(inner), (((1,), (1,)), ((), ())), precision=EXACT,
        preferred_element_type=F32,
    )
    chp_o[0:4, :] = conv_v[...]
    chp_o[4:5, :] = bias_v[...]
    chp_o[5:6, :] = gate_g[...]
    chp_o[6:7, :] = repeated[2:3, :]
    chp_o[7:8, :] = jnp.zeros((1, inner), F32)
    shp_o[...] = jnp.zeros_like(shp_o)
    shp_o[0:4, :] = conv_s[...]
    shp_o[4:5, :] = bias_s[...]


def small_sum(x, axis, collective_id):
    count = lax.axis_size(axis)

    def body(x_ref, out_ref, slots, send, recv):
        me = lax.axis_index(axis)
        barrier = pltpu.get_barrier_semaphore()
        for k in range(1, count):
            peer = lax.rem(me + k, count)
            pl.semaphore_signal(barrier, inc=1, device_id={axis: peer}, device_id_type=MESH)
        pl.semaphore_wait(barrier, count - 1)
        copies = []
        for k in range(1, count):
            copies.append(
                pltpu.make_async_remote_copy(
                    src_ref=x_ref,
                    dst_ref=slots.at[k],
                    send_sem=send.at[k],
                    recv_sem=recv.at[k],
                    device_id={axis: lax.rem(me + k, count)},
                    device_id_type=MESH,
                )
            )
            copies[-1].start()
        slots[0] = x_ref[...]
        for copy in copies:
            copy.wait()
        total = slots[me]
        for source in range(1, count):
            total = total + slots[lax.rem(me - source + count, count)]
        out_ref[...] = total

    return pl.pallas_call(
        body,
        in_specs=[pl.BlockSpec(memory_space=pltpu.VMEM)],
        out_specs=pl.BlockSpec(memory_space=pltpu.VMEM),
        out_shape=jax.ShapeDtypeStruct(x.shape, x.dtype),
        scratch_shapes=[
            pltpu.VMEM((count,) + x.shape, x.dtype),
            pltpu.SemaphoreType.DMA((count,)),
            pltpu.SemaphoreType.DMA((count,)),
        ],
        compiler_params=pltpu.CompilerParams(collective_id=collective_id, has_side_effects=True),
        name="small_sum_" + axis,
    )(x)


def cost(micros):
    return pl.CostEstimate(
        flops=int(micros * 1e9), bytes_accessed=int(micros * 3.6e6), transcendentals=0
    )


def call(body, blocks, ins, outs, scratch, backward, name, micros):
    def spec(shape, kind):
        if kind == "whole":
            return pl.BlockSpec(shape, lambda i: (0,) * len(shape))
        if kind == "lanes":
            block = (shape[0], shape[1] // blocks)
            return pl.BlockSpec(block, (lambda i: (0, blocks - 1 - i)) if backward else (lambda i: (0, i)))
        block = (shape[0] // blocks, shape[1])
        return pl.BlockSpec(block, (lambda i: (blocks - 1 - i, 0)) if backward else (lambda i: (i, 0)))

    return pl.pallas_call(
        body,
        grid=(blocks,),
        in_specs=[spec(a.shape, kind) for a, kind in ins],
        out_specs=[spec(shape, kind) for shape, _, kind in outs],
        out_shape=[jax.ShapeDtypeStruct(shape, dtype) for shape, dtype, _ in outs],
        scratch_shapes=scratch,
        compiler_params=pltpu.CompilerParams(
            dimension_semantics=("arbitrary",), vmem_limit_bytes=60 * 1024 * 1024
        ),
        cost_estimate=cost(micros),
        name=name,
    )(*[a for a, _ in ins])


def signal_all(groups):
    barrier = pltpu.get_barrier_semaphore()
    for axis, peers in groups:
        for peer in peers:
            pl.semaphore_signal(barrier, inc=1, device_id={axis: peer}, device_id_type=MESH)
    pl.semaphore_wait(barrier, sum(len(peers) for _, peers in groups))


def push(src, dst, send, recv, axis, peer):
    copy = pltpu.make_async_remote_copy(
        src_ref=src, dst_ref=dst, send_sem=send, recv_sem=recv, device_id={axis: peer},
        device_id_type=MESH,
    )
    copy.start()
    return copy


def span(start, size):
    return pl.ds(pl.multiple_of(start, size), size)


def split_dp(count):
    small = 1
    while 2 * small * 2 * small * 2 <= count:
        small *= 2
    return small, count // small


def mid_step(mixed, hidden, gate_low, cotangent, normal, collective_id, micros):
    length, width = mixed.shape
    inner = gate_low.shape[1]
    nd = lax.axis_size("dp")
    nx, nz = split_dp(nd)
    rows = width // nd
    half = length // 2
    chunk = 256

    def body(mixed_r, hid, low, cot, nor, half_o, keep_o, *rest):
        sends, (near, buf, send, recv) = rest[: nx - 1], rest[nx - 1 :]
        me = lax.axis_index("tensor")
        side = lax.rem(me, 2)
        sibling = me + 1 - 2 * side
        x = lax.rem(lax.axis_index("dp"), nx)
        signal_all([("tensor", [sibling])])
        copy = push(
            mixed_r.at[span((1 - side) * half, half)], near, send.at[0], recv.at[0], "tensor", sibling
        )
        for c in range(width // chunk):
            cols = slice(c * chunk, (c + 1) * chunk)
            left = t_mm(hid[:, cols], low[...]).astype(BF16)
            right = t_mm(cot[:, cols], nor[...]).astype(BF16)
            for d in range(c * chunk // rows, (c + 1) * chunk // rows):
                at = slice(d * rows - c * chunk, (d + 1) * rows - c * chunk)
                place = slice((d // nx) * rows, (d // nx + 1) * rows)
                buf[d % nx, place, :inner] = left[at]
                buf[d % nx, place, inner:] = right[at]
        keep_o[...] = buf[x]
        for q in range(1, nx):
            sends[q - 1][...] = buf[lax.rem(x + q, nx)]
        copy.wait()
        mine = mixed_r[span(side * half, half), :].astype(F32) + near[...].astype(F32)
        half_o[...] = mine.astype(BF16)

    vm = pl.BlockSpec(memory_space=pltpu.VMEM)
    part = jax.ShapeDtypeStruct((nz * rows, 2 * inner), BF16)
    return pl.pallas_call(
        body,
        in_specs=[vm] * 5,
        out_specs=[vm] * (1 + nx),
        out_shape=[jax.ShapeDtypeStruct((half, width), BF16)] + [part] * nx,
        scratch_shapes=[
            pltpu.VMEM((half, width), BF16),
            pltpu.VMEM((nx, nz * rows, 2 * inner), BF16),
            pltpu.SemaphoreType.DMA((1,)),
            pltpu.SemaphoreType.DMA((1,)),
        ],
        compiler_params=pltpu.CompilerParams(
            collective_id=collective_id, has_side_effects=True, vmem_limit_bytes=60 * 1024 * 1024
        ),
        cost_estimate=cost(micros),
        name="mid_step",
    )(mixed, hidden, gate_low, cotangent, normal)


def tail_step(
    heads_part, dbc_part, hidden, value_low, step_low, shared_conv, shared_pre, aux, tokens, cotangent,
    ng, shared_proj, shp, mixed_half, mixed_far, keep, far, ch_grads, head_grads, gain_part,
    heads, collective_id, micros,
):
    length, width = tokens.shape
    inner = value_low.shape[1]
    shared_width = shared_proj.shape[1]
    nt, nd = lax.axis_size("tensor"), lax.axis_size("dp")
    ng_chips = nt // 2
    nx, nz = split_dp(nd)
    rows = width // nd
    quarter, half = length // nt, length // 2
    piece = quarter // PIECES
    part = nz * rows
    low_width = inner + LANES
    norm_width = width // nt
    early_width = 2 * inner + LANES
    late_width = shared_width + norm_width
    blocks = length // SPAN
    chunk = 256
    n_mixed, n_far = len(mixed_far), len(far)
    n_late = 10 + n_mixed + n_far

    def body(*refs):
        refs = list(refs)

        def take(n):
            out = refs[:n]
            del refs[:n]
            return out

        heads_r, dbc, aux_r, ng_r, ws, shp_r, chg, hg, gain = take(9)
        hid_h, vlow_h, slow_h, scv_h, spre_h, tok_h, cot_h, mix_h = take(8)
        mixfar_h, (keep_h,), far_h = take(n_mixed), take(1), take(n_far)
        (
            result_o, gtok_o, dgate_o, dvalue_o, dshared_o, dstep_o, dout_o,
            convv_o, biasv_o, convs_o, biass_o, h0_o, h1_o, h2_o, gain_o, norm_o,
        ) = take(16)
        hid, low, scv, spre, tokh, tokq, cotq, mix, gk = take(9)
        mixfar, fars = take(n_mixed), take(n_far)
        (
            dnear, dslots, dtot, dbuf, shlow, hnear, fsrc, ffar, hacc, vbuf, vslot, sbuf, sslot,
            zg, zgslot, zv, zvslot, zs, zsslot, eslots, lslots, nbuf, nslot,
        ) = take(23)
        (
            loc, a_s, a_r, d_s, d_r, n_s, n_r, f_s, f_r, g_s, g_r, h_s, h_r, r_s, r_r,
            zg_s, zg_r, zv_s, zv_r, zs_s, zs_r, xv_s, xv_r, xs_s, xs_r, e_s, e_r, l_s, l_r, m_s, m_r,
        ) = take(31)

        me = lax.axis_index("tensor")
        side, chip = lax.rem(me, 2), me // 2
        sibling = 2 * chip + 1 - side
        md = lax.axis_index("dp")
        x, z = lax.rem(md, nx), md // nx

        def chip_at(q):
            return lax.rem(chip + q, ng_chips)

        def mate(q):
            return 2 * chip_at(q) + side

        def x_peer(q):
            return z * nx + lax.rem(x + q, nx)

        def z_peer(k):
            return lax.rem(z + k, nz) * nx + x

        count = [0]

        def fetch(src, dst):
            copy = pltpu.make_async_copy(src, dst, loc.at[count[0]])
            count[0] += 1
            copy.start()
            return copy

        my_rows = span(me * quarter, quarter)
        my_half = span(side * half, half)
        sib_half = span((1 - side) * half, half)
        got_keep = [fetch(keep_h, gk)] + [fetch(a, b) for a, b in zip(far_h, fars)]
        got_low = [
            fetch(hid_h, hid), fetch(vlow_h, low.at[:, 0:inner]),
            fetch(slow_h, low.at[:, inner : inner + LANES]),
        ]
        got_mix = [fetch(mix_h, mix), fetch(tok_h.at[my_half], tokh)]
        got_mix += [fetch(a, b) for a, b in zip(mixfar_h, mixfar)]
        got_shared = [fetch(scv_h, scv), fetch(spre_h, spre)]
        got_end = [fetch(tok_h.at[my_rows], tokq), fetch(cot_h.at[my_rows], cotq)]

        signal_all([
            ("tensor", [lax.rem(me + k, nt) for k in range(1, nt)]),
            ("dp", [lax.rem(md + k, nd) for k in range(1, nd)]),
        ])
        sent = []

        def send(*args):
            copy = push(*args)
            sent.append(copy)
            return copy

        dn = send(dbc.at[sib_half], dnear, a_s.at[0], a_r.at[0], "tensor", sibling)
        order = list(range(1, ng_chips)) + [0]
        near = {}
        for q in order:
            for p in range(PIECES):
                at = (2 * chip_at(q) + 1 - side) * quarter + p * piece
                near[q, p] = send(
                    heads_r.at[span(at, piece)], hnear.at[q, p], n_s.at[q, p], n_r.at[q, p],
                    "tensor", sibling,
                )
        eslots[md, :, :inner] = chg[...]
        eslots[md, :, inner : 2 * inner] = gain[...]
        eslots[md, :, 2 * inner :] = hg[...]

        for copy in got_keep:
            copy.wait()
        total = gk[...].astype(F32)
        for b in fars:
            total = total + b[...].astype(F32)
        zg[...] = total.astype(BF16)

        dn.wait_recv()
        dslots[chip] = (dbc[my_half, :] + dnear[...]).astype(BF16)
        dmates = [
            send(dslots.at[chip], dslots.at[chip], d_s.at[q], d_r.at[q], "tensor", mate(q))
            for q in range(1, ng_chips)
        ]
        zgs = [
            send(
                zg.at[span(lax.rem(z + k, nz) * rows, rows)], zgslot.at[k], zg_s.at[k], zg_r.at[k],
                "dp", z_peer(k),
            )
            for k in range(1, nz)
        ]
        fwd = {}
        for q in order:
            for p in range(PIECES):
                near[q, p].wait_recv()
                at = (2 * chip_at(q) + side) * quarter + p * piece
                both = heads_r[span(at, piece), :].astype(F32) + hnear[q, p].astype(F32)
                if q:
                    fsrc[q, p] = both.astype(BF16)
                    fwd[q, p] = send(
                        fsrc.at[q, p], ffar.at[q, p], f_s.at[q, p], f_r.at[q, p], "tensor", mate(q)
                    )
                else:
                    hacc[p * piece : (p + 1) * piece, :] = both
        es = [
            send(
                eslots.at[md], eslots.at[md], e_s.at[k], e_r.at[k], "dp", lax.rem(md + k, nd)
            )
            for k in range(1, nd)
        ]

        for copy in got_low:
            copy.wait()
        for c in range(width // chunk):
            prod = t_mm(hid[:, c * chunk : (c + 1) * chunk], low[...]).astype(BF16)
            for d in range(c * chunk // rows, (c + 1) * chunk // rows):
                at = slice(d * rows - c * chunk, (d + 1) * rows - c * chunk)
                vbuf[d % nx, (d // nx) * rows : (d // nx + 1) * rows, :] = prod[at]
        xvs = [
            send(
                vbuf.at[lax.rem(x + q, nx)], vslot.at[q], xv_s.at[q], xv_r.at[q], "dp", x_peer(q)
            )
            for q in range(1, nx)
        ]

        for copy in got_shared:
            copy.wait()
        for copy in dmates:
            copy.wait_recv()
        total = dslots[0].astype(F32)
        for g in range(1, ng_chips):
            total = total + dslots[g].astype(F32)
        dtot[my_half, :] = total
        dt_copy = send(
            dtot.at[my_half], dtot.at[my_half], a_s.at[1], a_r.at[1], "tensor", sibling
        )

        for copy in got_mix:
            copy.wait()
        mixed = mix[...].astype(F32)
        if n_mixed == 1:
            mixed = mixed + mixfar[0][...].astype(F32)
        else:
            terms = [mix] + list(mixfar)
            mixed = jnp.zeros((half, width), F32)
            for g in range(ng_chips):
                for q in range(ng_chips):
                    mine = (lax.rem(chip - q + ng_chips, ng_chips) == g).astype(F32)
                    mixed = mixed + terms[q][...].astype(F32) * mine
        result_o[my_half, :] = (tokh[...].astype(F32) + mixed).astype(BF16)
        res = send(
            result_o.at[my_half], result_o.at[my_half], r_s.at[0], r_r.at[0], "tensor", sibling
        )

        dt_copy.wait_recv()
        dbuf[length : length + 8, :] = jnp.zeros((8, shared_width), F32)
        sums = [jnp.zeros((1, shared_width), F32)] * 5
        for b in reversed(range(blocks)):
            base = b * SPAN
            at = slice(base, base + SPAN)
            sc = scv[at, :]
            csig = sigmoid(sc)
            dcv = dtot[at, :] * (csig * (1.0 + sc * (1.0 - csig)))
            dbuf[at, :] = dcv
            sp = spre[at, :]
            mask = aux_r[at, :]
            ds = dcv * shp_r[3:4, :]
            sums[3] = sums[3] + jnp.sum(dcv * sp, axis=0, keepdims=True)
            sums[4] = sums[4] + jnp.sum(dcv, axis=0, keepdims=True)
            for j in range(1, 4):
                moved = dbuf[base + j : base + j + SPAN, :] * mask[:, 8 + j : 9 + j]
                ds = ds + moved * shp_r[3 - j : 4 - j, :]
                sums[3 - j] = sums[3 - j] + jnp.sum(moved * sp, axis=0, keepdims=True)
            shlow[at, :] = ds.astype(BF16)
        for c in range(width // chunk):
            prod = t_mm(hid[:, c * chunk : (c + 1) * chunk], shlow[...]).astype(BF16)
            for d in range(c * chunk // rows, (c + 1) * chunk // rows):
                at = slice(d * rows - c * chunk, (d + 1) * rows - c * chunk)
                sbuf[d % nx, (d // nx) * rows : (d // nx + 1) * rows, :] = prod[at]
        xss = [
            send(
                sbuf.at[lax.rem(x + q, nx)], sslot.at[q], xs_s.at[q], xs_r.at[q], "dp", x_peer(q)
            )
            for q in range(1, nx)
        ]
        hacc[...] = hacc[...] + mm_t(shlow[my_rows, :], ws[...])

        for copy in got_end:
            copy.wait()
        norm = jnp.zeros((1, width), F32)
        gather, own = {}, []
        for p in range(PIECES):
            at = slice(p * piece, (p + 1) * piece)
            grad_hidden = hacc[at, :]
            for q in range(1, ng_chips):
                fwd[q, p].wait_recv()
                grad_hidden = grad_hidden + ffar[q, p].astype(F32)
            v = tokq[at, :].astype(F32)
            inv = lax.rsqrt(jnp.mean(v * v, axis=1, keepdims=True) + EPSILON)
            normed = v * inv
            scaled = grad_hidden * ng_r[...]
            norm = norm + jnp.sum(grad_hidden * normed, axis=0, keepdims=True)
            mean = jnp.mean(scaled * normed, axis=1, keepdims=True)
            place = span(me * quarter + p * piece, piece)
            gtok_o[place, :] = (inv * (scaled - normed * mean) + cotq[at, :].astype(F32)).astype(BF16)
            for q in range(1, ng_chips):
                gather[q, p] = send(
                    gtok_o.at[place], gtok_o.at[place], g_s.at[q, p], g_r.at[q, p], "tensor", mate(q)
                )
            own.append(
                send(gtok_o.at[place], gtok_o.at[place], h_s.at[0, p], h_r.at[0, p], "tensor", sibling)
            )
        for q in range(nt):
            nbuf[q] = norm[:, q * norm_width : (q + 1) * norm_width] + jnp.zeros((8, norm_width), F32)
        norms = [
            send(
                nbuf.at[lax.rem(me + k, nt)], nslot.at[k], m_s.at[k], m_r.at[k], "tensor",
                lax.rem(me + k, nt),
            )
            for k in range(1, nt)
        ]

        for copy in xvs:
            copy.wait_recv()
        total = vbuf[x].astype(F32)
        for q in range(1, nx):
            total = total + vslot[q].astype(F32)
        zv[...] = total.astype(BF16)
        zvs = [
            send(
                zv.at[span(lax.rem(z + k, nz) * rows, rows)], zvslot.at[k], zv_s.at[k], zv_r.at[k],
                "dp", z_peer(k),
            )
            for k in range(1, nz)
        ]
        for copy in xss:
            copy.wait_recv()
        total = sbuf[x].astype(F32)
        for q in range(1, nx):
            total = total + sslot[q].astype(F32)
        zs[...] = total.astype(BF16)
        zss = [
            send(
                zs.at[span(lax.rem(z + k, nz) * rows, rows)], zsslot.at[k], zs_s.at[k], zs_r.at[k],
                "dp", z_peer(k),
            )
            for k in range(1, nz)
        ]

        for copy in norms:
            copy.wait_recv()
        total = nbuf[me]
        for k in range(1, nt):
            total = total + nslot[k]
        lslots[md, :, shared_width:] = total
        packed = jnp.concatenate(sums + [jnp.zeros((3, shared_width), F32)], axis=0)
        lslots[md, :, :shared_width] = packed
        ls = [
            send(
                lslots.at[md], lslots.at[md], l_s.at[k], l_r.at[k], "dp", lax.rem(md + k, nd)
            )
            for k in range(1, nd)
        ]

        for copy in zgs:
            copy.wait_recv()
        total = zg[span(z * rows, rows), :].astype(F32)
        for k in range(1, nz):
            total = total + zgslot[k].astype(F32)
        dgate_o[...] = total[:, :inner]
        dout_o[...] = total[:, inner:]

        for copy in es:
            copy.wait_recv()
        total = eslots[0]
        for s in range(1, nd):
            total = total + eslots[s]
        convv_o[...] = total[0:4, :inner]
        biasv_o[...] = total[4:5, :inner]
        gain_o[...] = total[0:1, inner : 2 * inner]
        h0_o[...] = total[0:1, 2 * inner : 2 * inner + heads]
        h1_o[...] = total[1:2, 2 * inner : 2 * inner + heads]
        h2_o[...] = total[2:3, 2 * inner : 2 * inner + heads]

        for p in range(PIECES):
            for q in range(1, ng_chips):
                gather[q, p].wait_recv()
                came = 2 * lax.rem(chip - q + ng_chips, ng_chips) + side
                place = span(came * quarter + p * piece, piece)
                own.append(
                    send(
                        gtok_o.at[place], gtok_o.at[place], h_s.at[q, p], h_r.at[q, p],
                        "tensor", sibling,
                    )
                )

        for copy in zvs:
            copy.wait_recv()
        total = zv[span(z * rows, rows), :].astype(F32)
        for k in range(1, nz):
            total = total + zvslot[k].astype(F32)
        dvalue_o[...] = total[:, :inner]
        dstep_o[...] = total[:, inner : inner + heads]
        for copy in zss:
            copy.wait_recv()
        total = zs[span(z * rows, rows), :].astype(F32)
        for k in range(1, nz):
            total = total + zsslot[k].astype(F32)
        dshared_o[...] = total

        for copy in ls:
            copy.wait_recv()
        total = lslots[0]
        for s in range(1, nd):
            total = total + lslots[s]
        convs_o[...] = total[0:4, :shared_width]
        biass_o[...] = total[4:5, :shared_width]
        norm_o[...] = total[0:1, shared_width:]

        res.wait_recv()
        for copy in own:
            copy.wait_recv()
        for copy in sent:
            copy.wait_send()

    vm = pl.BlockSpec(memory_space=pltpu.VMEM)
    hbm = pl.BlockSpec(memory_space=pl.ANY)
    dma = pltpu.SemaphoreType.DMA

    def f32(*shape):
        return pltpu.VMEM(shape, F32)

    def bf16(*shape):
        return pltpu.VMEM(shape, BF16)

    def out(*shape):
        return jax.ShapeDtypeStruct(shape, F32)

    early = [heads_part, dbc_part, aux, ng, shared_proj, shp, ch_grads, head_grads, gain_part]
    late = [hidden, value_low, step_low, shared_conv, shared_pre, tokens, cotangent, mixed_half]
    late += list(mixed_far) + [keep] + list(far)
    return pl.pallas_call(
        body,
        in_specs=[vm] * len(early) + [hbm] * len(late),
        out_specs=[vm] * 16,
        out_shape=[
            jax.ShapeDtypeStruct((length, width), BF16), jax.ShapeDtypeStruct((length, width), BF16),
            out(rows, inner), out(rows, inner), out(rows, shared_width), out(rows, heads),
            out(rows, inner), out(4, inner), out(1, inner), out(4, shared_width),
            out(1, shared_width), out(1, heads), out(1, heads), out(1, heads), out(1, inner),
            out(1, norm_width),
        ],
        scratch_shapes=[
            bf16(length, width), bf16(length, low_width), f32(length, shared_width),
            f32(length, shared_width), bf16(half, width), bf16(quarter, width), bf16(quarter, width),
            bf16(half, width), bf16(part, 2 * inner),
        ]
        + [bf16(half, width)] * n_mixed
        + [bf16(part, 2 * inner)] * n_far
        + [
            f32(half, shared_width), bf16(ng_chips, half, shared_width), f32(length, shared_width),
            f32(length + 8, shared_width), bf16(length, shared_width),
            bf16(ng_chips, PIECES, piece, width), bf16(ng_chips, PIECES, piece, width),
            bf16(ng_chips, PIECES, piece, width), f32(quarter, width),
            bf16(nx, part, low_width), bf16(nx, part, low_width),
            bf16(nx, part, shared_width), bf16(nx, part, shared_width),
            bf16(part, 2 * inner), bf16(nz, rows, 2 * inner),
            bf16(part, low_width), bf16(nz, rows, low_width),
            bf16(part, shared_width), bf16(nz, rows, shared_width),
            f32(nd, 8, early_width), f32(nd, 8, late_width),
            f32(nt, 8, norm_width), f32(nt, 8, norm_width),
        ]
        + [dma((n_late + 1,)), dma((2,)), dma((2,)), dma((ng_chips,)), dma((ng_chips,))]
        + [dma((ng_chips, PIECES))] * 8
        + [dma((1,)), dma((1,))]
        + [dma((nz,))] * 6
        + [dma((nx,))] * 4
        + [dma((nd,))] * 4
        + [dma((nt,))] * 2,
        compiler_params=pltpu.CompilerParams(
            collective_id=collective_id, has_side_effects=True, vmem_limit_bytes=60 * 1024 * 1024
        ),
        cost_estimate=cost(micros),
        name="tail_step",
    )(*early, *late)


def per_device(
    tokens, cotangent, segments, norm_gain, gate_proj, value_proj, shared_proj, step_proj,
    conv_value, bias_value, conv_shared, bias_shared, step_bias, decay_log, skip_gain,
    gate_gain, out_proj,
):
    tp_count = lax.axis_size("tensor")
    dp_count = lax.axis_size("dp")
    chips = tp_count // 2
    nx, nz = split_dp(dp_count)
    length, width = tokens.shape
    inner = gate_proj.shape[1]
    heads = step_proj.shape[1]
    shared_width = shared_proj.shape[1]
    state_size = shared_width // 2
    blocks = length // SPAN
    aux, segr, wst, chp, shp, hp = pl.pallas_call(
        prep_kernel,
        out_shape=[
            jax.ShapeDtypeStruct((length, LANES), F32),
            jax.ShapeDtypeStruct((1, length), F32),
            jax.ShapeDtypeStruct((width, LANES), BF16),
            jax.ShapeDtypeStruct((8, inner), F32),
            jax.ShapeDtypeStruct((8, shared_width), F32),
            jax.ShapeDtypeStruct((8, LANES), F32),
        ],
        name="prep_step",
    )(
        segments, step_proj.T, conv_value, bias_value[None], gate_gain[None], skip_gain[None],
        conv_shared, bias_shared[None], step_bias[None], decay_log[None],
    )
    ng = norm_gain[None, :]

    (
        hidden, gate_pre, value_pre, conv_out, shared_pre, shared_conv, z, ld, ldt, yn, sin, gn, stat,
    ) = call(
        fwd_kernel,
        blocks,
        [
            (tokens, "rows"), (cotangent, "rows"), (aux, "rows"), (segr, "lanes"), (ng, "whole"),
            (gate_proj, "whole"), (value_proj, "whole"), (shared_proj, "whole"), (wst, "whole"),
            (out_proj, "whole"), (chp, "whole"), (shp, "whole"), (hp, "whole"),
        ],
        [
            ((length, width), BF16, "rows"),
            ((length, inner), F32, "rows"),
            ((length, inner), F32, "rows"),
            ((length, inner), F32, "rows"),
            ((length, shared_width), F32, "rows"),
            ((length, shared_width), F32, "rows"),
            ((length, LANES), F32, "rows"),
            ((length, LANES), F32, "rows"),
            ((8, length), F32, "lanes"),
            ((length, inner), F32, "rows"),
            ((blocks * state_size, inner), F32, "rows"),
            ((length, inner), F32, "rows"),
            ((8, length), F32, "lanes"),
        ],
        [
            pltpu.VMEM((SPAN + 8, inner), F32),
            pltpu.VMEM((SPAN + 8, shared_width), F32),
            pltpu.VMEM((state_size, inner), F32),
        ],
        False,
        "fwd_scan",
        20,
    )
    stat = small_sum(stat, "tensor", 0)
    total_inner = float(inner * tp_count)

    def gate_body(*refs):
        gate_kernel(total_inner, *refs)

    normal_out, dy, gate_low, gain_part, mixed_part = call(
        gate_body,
        blocks,
        [
            (gate_pre, "rows"), (conv_out, "rows"), (yn, "rows"), (gn, "rows"), (stat, "lanes"),
            (chp, "whole"), (out_proj, "whole"),
        ],
        [
            ((length, inner), BF16, "rows"),
            ((length, inner), F32, "rows"),
            ((length, inner), BF16, "rows"),
            ((8, inner), F32, "whole"),
            ((length, width), BF16, "rows"),
        ],
        [],
        False,
        "gate_step",
        9,
    )
    mixed_half, keep, *sends = mid_step(mixed_part, hidden, gate_low, cotangent, normal_out, 1, 6)
    mixed_far = [
        lax.ppermute(
            mixed_half, "tensor",
            [(2 * c + s, 2 * ((c + q) % chips) + s) for c in range(chips) for s in range(2)],
        )
        for q in range(1, chips)
    ]
    far = [
        lax.ppermute(
            sends[q - 1], "dp",
            [(d, d // nx * nx + (d + q) % nx) for d in range(dp_count)],
        )
        for q in range(1, nx)
    ]
    value_low, step_low, heads_part, dbc_part, ch_grads, head_grads = call(
        bwd_kernel,
        blocks,
        [
            (dy, "rows"), (conv_out, "rows"), (value_pre, "rows"), (shared_conv, "rows"),
            (z, "rows"), (ld, "rows"), (ldt, "lanes"), (yn, "rows"), (sin, "rows"),
            (aux, "rows"), (segr, "lanes"), (gate_low, "rows"), (gate_proj, "whole"),
            (value_proj, "whole"), (wst, "whole"), (chp, "whole"), (hp, "whole"),
        ],
        [
            ((length, inner), BF16, "rows"),
            ((length, LANES), BF16, "rows"),
            ((length, width), BF16, "rows"),
            ((length, shared_width), F32, "rows"),
            ((8, inner), F32, "whole"),
            ((8, LANES), F32, "whole"),
        ],
        [pltpu.VMEM((SPAN + 8, inner), F32), pltpu.VMEM((state_size, inner), F32)],
        True,
        "bwd_scan",
        27,
    )
    (
        result, grad_tokens, dgate, dvalue, dshared, dstep, dout,
        convv, biasv, convs, biass, h0, h1, h2, gain, norm,
    ) = tail_step(
        heads_part, dbc_part, hidden, value_low, step_low, shared_conv, shared_pre, aux, tokens,
        cotangent, ng, shared_proj, shp, mixed_half, mixed_far, keep, far, ch_grads, head_grads,
        gain_part, heads, 2, 40,
    )
    return (
        result, grad_tokens, norm[0], dgate, dvalue, dshared, dstep, convv, biasv[0], convs, biass[0],
        h0[0], h1[0], h2[0], gain[0], dout,
    )


def solution(mesh):
    rows, cols, vec = P("dp", None), P(None, "tensor"), P("tensor")
    return jax.shard_map(
        per_device,
        mesh=mesh,
        in_specs=(
            rows, rows, rows, P(), cols, cols, P(), cols, cols, vec, P(), P(), vec, vec, vec, vec, cols,
        ),
        out_specs=(
            rows, rows, vec, P("dp", "tensor"), P("dp", "tensor"), rows, P("dp", "tensor"), cols, vec,
            P(), P(), vec, vec, vec, vec, P("dp", "tensor"),
        ),
        check_vma=False,
    )
```

```python
import jax
import jax.numpy as jnp
from jax import lax
from jax.experimental import pallas as pl
from jax.experimental.pallas import tpu as pltpu
from jax.sharding import PartitionSpec as P

SPAN = 256
HSIZE = 64
LANES = 128
EPSILON = 1e-05
NEG_FILL = -1e30
EXACT = lax.Precision.HIGHEST
F32 = jnp.float32
BF16 = jnp.bfloat16


def mm(left, right):
    return jnp.dot(left, right, preferred_element_type=F32)


def mm_t(left, right):
    return lax.dot_general(left, right, (((1,), (1,)), ((), ())), preferred_element_type=F32)


def t_mm(left, right):
    return lax.dot_general(left, right, (((0,), (0,)), ((), ())), preferred_element_type=F32)


def exact(left, right):
    return jnp.dot(left, right, precision=EXACT, preferred_element_type=F32)


def sigmoid(v):
    return 1.0 / (1.0 + jnp.exp(-v))


def spread(cols, pairs):
    low = lax.broadcasted_iota(jnp.int32, (cols.shape[0], LANES), 1) < HSIZE
    parts = [
        jnp.where(low, cols[:, 2 * p : 2 * p + 1], cols[:, 2 * p + 1 : 2 * p + 2])
        for p in range(pairs)
    ]
    return jnp.concatenate(parts, axis=1)


def gather_mat(inner):
    channel = lax.broadcasted_iota(jnp.int32, (inner, LANES), 0) // HSIZE
    head = lax.broadcasted_iota(jnp.int32, (inner, LANES), 1)
    return (channel == head).astype(F32)


def grid_masks():
    row = lax.broadcasted_iota(jnp.int32, (SPAN, SPAN), 0)
    col = lax.broadcasted_iota(jnp.int32, (SPAN, SPAN), 1)
    return row, col


def conv_fwd(buf, pack, aux):
    out = pack[4:5, :] + buf[8 : 8 + SPAN, :] * pack[3:4, :]
    for j in range(1, 4):
        out = out + buf[8 - j : 8 - j + SPAN, :] * (aux[:, j : j + 1] * pack[3 - j : 4 - j, :])
    return out


def fwd_kernel(
    tok, cot, aux_ref, segr, ng, wg, wv, ws, wst, wo, chp, shp, hp,
    hidden_o, gate_o, vpre_o, cv_o, spre_o, scv_o, z_o, ld_o, ldt_o, yn_o, sin_o, gn_o, stat_o,
    vbuf, sbuf, state,
):
    inner = wg.shape[1]
    pairs = inner // LANES
    state_size = ws.shape[1] // 2

    @pl.when(pl.program_id(0) == 0)
    def _():
        vbuf[0:8, :] = jnp.zeros((8, inner), F32)
        sbuf[0:8, :] = jnp.zeros((8, 2 * state_size), F32)
        state[...] = jnp.zeros_like(state)

    aux = aux_ref[...]
    x = tok[...].astype(F32)
    inv = lax.rsqrt(jnp.mean(x * x, axis=1, keepdims=True) + EPSILON)
    hid = (x * inv * ng[...]).astype(BF16)
    hidden_o[...] = hid
    gate = mm(hid, wg[...])
    gate_o[...] = gate
    vp = mm(hid, wv[...])
    vpre_o[...] = vp
    vbuf[8 : 8 + SPAN, :] = vp
    sp = mm(hid, ws[...])
    spre_o[...] = sp
    sbuf[8 : 8 + SPAN, :] = sp
    z = mm(hid, wst[...]) + hp[0:1, :]
    z_o[...] = z
    gn = mm(cot[...], wo[...])
    gn_o[...] = gn
    scv = conv_fwd(sbuf, shp, aux)
    scv_o[...] = scv
    bc = (scv * sigmoid(scv)).astype(BF16)
    b_low, c_low = bc[:, :state_size], bc[:, state_size:]
    cv = conv_fwd(vbuf, chp, aux)
    cv_o[...] = cv
    vbuf[0:8, :] = vbuf[SPAN : SPAN + 8, :]
    sbuf[0:8, :] = sbuf[SPAN : SPAN + 8, :]
    values = cv * sigmoid(cv)
    dt = jnp.maximum(z, 0.0) + jnp.log1p(jnp.exp(-jnp.abs(z)))
    row, col = grid_masks()
    tri = (row >= col).astype(F32)
    ld = exact(tri, dt * hp[1:2, :])
    ld_o[...] = ld
    ldt = jnp.transpose(ld)[0:8, :]
    ldt_o[...] = ldt
    allowed = (row >= col) & (aux[:, 0:1] == segr[...])
    scores = jnp.where(allowed, mm_t(c_low, b_low), 0.0)
    xs = values * spread(dt, pairs)
    xs_low = xs.astype(BF16)
    ein = jnp.exp(ld) * aux[:, 4:5]
    eout = jnp.exp(ld[SPAN - 1 : SPAN, :] - ld) * aux[:, 5:6]
    ein_x = spread(ein, pairs)
    eout_x = spread(eout, pairs)
    old = state[...]
    sin_o[...] = old
    carried = mm(c_low, old.astype(BF16)) * ein_x
    state[...] = old * ein_x[SPAN - 1 : SPAN, :] + t_mm(b_low, (xs * eout_x).astype(BF16))
    low = lax.broadcasted_iota(jnp.int32, (SPAN, LANES), 1) < HSIZE
    parts = []
    for p in range(pairs):
        pair = xs_low[:, p * LANES : (p + 1) * LANES]
        outs = []
        for h in (2 * p, 2 * p + 1):
            gap = jnp.minimum(ld[:, h : h + 1] - ldt[h : h + 1, :], 0.0)
            outs.append(mm((jnp.exp(gap) * scores).astype(BF16), pair))
        parts.append(jnp.where(low, outs[0], outs[1]))
    yn = jnp.concatenate(parts, axis=1) + carried
    yn_o[...] = yn
    gated = (yn + chp[6:7, :] * values) * (gate * sigmoid(gate))
    squares = jnp.sum(gated * gated, axis=1, keepdims=True)
    dots = jnp.sum(gn * chp[5:6, :] * gated, axis=1, keepdims=True)
    lane = lax.broadcasted_iota(jnp.int32, (SPAN, LANES), 1)
    both = jnp.where(lane == 0, squares, jnp.where(lane == 1, dots, 0.0))
    stat_o[...] = jnp.transpose(both)[0:8, :]


def gate_kernel(
    width, gate_ref, cv_ref, yn, gn_ref, stat, chp, wo, normal_o, dy_o, low_o, gain_o, mixed_o
):
    both = jnp.transpose(jnp.concatenate([stat[...]] * (LANES // 8), axis=0))
    inv = lax.rsqrt(both[:, 0:1] / width + EPSILON)
    mean_dots = both[:, 1:2] / width
    gate = gate_ref[...]
    cv = cv_ref[...]
    gn = gn_ref[...]
    sig = sigmoid(gate)
    act = gate * sig
    mixer = yn[...] + chp[6:7, :] * (cv * sigmoid(cv))
    gated = mixer * act
    normed = gated * inv
    normal = (normed * chp[5:6, :]).astype(BF16)
    normal_o[...] = normal
    mixed_o[...] = mm_t(normal, wo[...]).astype(BF16)
    part = jnp.sum(gn * normed, axis=0, keepdims=True)

    @pl.when(pl.program_id(0) == 0)
    def _():
        gain_o[...] = jnp.zeros_like(gain_o)

    gain_o[0:1, :] += part
    grad_gated = inv * (gn * chp[5:6, :]) - gated * (inv * inv * inv) * mean_dots
    dy_o[...] = grad_gated * act
    low_o[...] = (grad_gated * mixer * (sig * (1.0 + gate * (1.0 - sig)))).astype(BF16)


def bwd_kernel(
    dy_ref, cv_ref, vpre, scv_ref, z_ref, ld_ref, ldt_ref, yn, sin, aux_ref, segr, glow,
    wg, wv, wst, chp, hp,
    vlow_o, slow_o, heads_o, dbc_o, chg_o, hg_o,
    dbuf, dstate,
):
    inner = wg.shape[1]
    pairs = inner // LANES
    state_size = sin.shape[0]

    @pl.when(pl.program_id(0) == 0)
    def _():
        dbuf[SPAN : SPAN + 8, :] = jnp.zeros((8, inner), F32)
        dstate[...] = jnp.zeros_like(dstate)
        chg_o[...] = jnp.zeros_like(chg_o)
        hg_o[...] = jnp.zeros_like(hg_o)

    aux = aux_ref[...]
    dy = dy_ref[...]
    dy_low = dy.astype(BF16)
    scv = scv_ref[...]
    bc = (scv * sigmoid(scv)).astype(BF16)
    b_low, c_low = bc[:, :state_size], bc[:, state_size:]
    cv = cv_ref[...]
    csig = sigmoid(cv)
    values = cv * csig
    z = z_ref[...]
    dt = jnp.maximum(z, 0.0) + jnp.log1p(jnp.exp(-jnp.abs(z)))
    ld = ld_ref[...]
    ldt = ldt_ref[...]
    dt_x = spread(dt, pairs)
    xs = values * dt_x
    xs_low = xs.astype(BF16)
    ein = jnp.exp(ld) * aux[:, 4:5]
    eout = jnp.exp(ld[SPAN - 1 : SPAN, :] - ld) * aux[:, 5:6]
    ein_x = spread(ein, pairs)
    eout_x = spread(eout, pairs)
    row, col = grid_masks()
    allowed = (col >= row) & (aux[:, 0:1] == segr[...])
    mask = allowed.astype(F32)
    scores_t = mm_t(b_low, c_low) * mask
    low = lax.broadcasted_iota(jnp.int32, (SPAN, LANES), 1) < HSIZE
    parts = []
    dscores_t = jnp.zeros((SPAN, SPAN), F32)
    for p in range(pairs):
        cols = slice(p * LANES, (p + 1) * LANES)
        dy_pair = dy_low[:, cols]
        xs_pair = xs_low[:, cols]
        zero = jnp.zeros_like(xs_pair)
        outs = []
        for side, h in enumerate((2 * p, 2 * p + 1)):
            gap = jnp.minimum(ldt[h : h + 1, :] - ld[:, h : h + 1], 0.0)
            decay = jnp.exp(gap)
            outs.append(mm((decay * scores_t).astype(BF16), dy_pair))
            mine = jnp.where(low, xs_pair, zero) if side == 0 else jnp.where(low, zero, xs_pair)
            dscores_t = dscores_t + mm_t(mine, dy_pair) * decay
        parts.append(jnp.where(low, outs[0], outs[1]))
    inside = jnp.concatenate(parts, axis=1)
    dscores_low = (dscores_t * mask).astype(BF16)
    old = sin[...]
    dst = dstate[...]
    dst_low = dst.astype(BF16)
    dye_low = (dy * ein_x).astype(BF16)
    xse_low = (xs * eout_x).astype(BF16)
    db = mm(dscores_low, c_low) + mm_t(xse_low, dst_low)
    dc = t_mm(dscores_low, b_low) + mm_t(dye_low, old.astype(BF16))
    late = mm(b_low, dst_low) * eout_x
    keep = ein_x[SPAN - 1 : SPAN, :]
    dstate[...] = dst * keep + t_mm(c_low, dye_low)
    dxs = inside + late
    collect = gather_mat(inner)
    q = dy_low.astype(F32) * yn[...] - xs_low.astype(F32) * inside
    u = xs * late
    kappa = exact(jnp.sum(old * dst, axis=0, keepdims=True) * keep + jnp.zeros((8, inner), F32), collect)
    da = (
        exact((col >= row).astype(F32), exact(q, collect))
        + exact((row > col).astype(F32), exact(u, collect))
        + kappa[0:1, :]
    )
    rates = hp[1:2, :]
    ddt = da * rates + exact(dxs * values, collect)
    dz = ddt * sigmoid(z)
    slow = dz.astype(BF16)
    slow_o[...] = slow
    skip = exact(jnp.sum(dy * values, axis=0, keepdims=True) + jnp.zeros((8, inner), F32), collect)
    hg_o[0:1, :] += jnp.sum(dz, axis=0, keepdims=True)
    hg_o[1:2, :] += jnp.sum(da * dt, axis=0, keepdims=True) * rates
    hg_o[2:3, :] += skip[0:1, :]
    dcv = (dxs * dt_x + chp[6:7, :] * dy) * (csig * (1.0 + cv * (1.0 - csig)))
    dbuf[0:SPAN, :] = dcv
    vp = vpre[...]
    dv = dcv * chp[3:4, :]
    chg_o[3:4, :] += jnp.sum(dcv * vp, axis=0, keepdims=True)
    chg_o[4:5, :] += jnp.sum(dcv, axis=0, keepdims=True)
    for j in range(1, 4):
        moved = dbuf[j : j + SPAN, :] * aux[:, 8 + j : 9 + j]
        dv = dv + moved * chp[3 - j : 4 - j, :]
        chg_o[3 - j : 4 - j, :] += jnp.sum(moved * vp, axis=0, keepdims=True)
    dbuf[SPAN : SPAN + 8, :] = dbuf[0:8, :]
    vlow = dv.astype(BF16)
    vlow_o[...] = vlow
    back = mm_t(glow[...], wg[...]) + mm_t(vlow, wv[...]) + mm_t(slow, wst[...])
    heads_o[...] = back.astype(BF16)
    dbc_o[...] = jnp.concatenate([db, dc], axis=1)


MESH = pl.DeviceIdType.MESH
PIECES = 4


def prep_kernel(
    seg, stepw, conv_v, bias_v, gate_g, skip_g, conv_s, bias_s, step_b, decay,
    aux_o, segr_o, wst_o, chp_o, shp_o, hp_o,
):
    length = seg.shape[1]
    ids = seg[...].astype(F32)
    segr_o[...] = ids
    wide = ids + jnp.zeros((8, length), F32)
    lane = lax.broadcasted_iota(jnp.int32, (8, length), 1)
    row = lax.broadcasted_iota(jnp.int32, (8, length), 0)
    ends = [
        ids[:, start + SPAN - 1 : start + SPAN] + jnp.zeros((8, SPAN), F32)
        for start in range(0, length, SPAN)
    ]
    last = jnp.concatenate(ends, axis=1)
    before = jnp.concatenate([jnp.full((8, SPAN), -1.0, F32)] + ends[:-1], axis=1)
    first = jnp.where(row == 0, wide, 0.0)
    first = jnp.where((row == 4) & (wide == before), 1.0, first)
    first = jnp.where((row == 5) & (wide == last), 1.0, first)
    second = jnp.zeros((8, length), F32)
    for j in range(1, 4):
        back = (pltpu.roll(wide, j, 1) == wide) & (lane >= j)
        ahead = (pltpu.roll(wide, length - j, 1) == wide) & (lane < length - j)
        first = jnp.where((row == j) & back, 1.0, first)
        second = jnp.where((row == j) & ahead, 1.0, second)
    rest = jnp.zeros((LANES - 16, length), F32)
    aux_o[...] = jnp.transpose(jnp.concatenate([first, second, rest], axis=0))
    heads, width = stepw.shape
    steps = jnp.concatenate([stepw[...].astype(F32), jnp.zeros((LANES - heads, width), F32)], axis=0)
    wst_o[...] = jnp.transpose(steps).astype(BF16)
    hp_o[...] = jnp.zeros_like(hp_o)
    hp_o[0:1, 0:heads] = step_b[...]
    hp_o[1:2, 0:heads] = -jnp.exp(decay[...])
    hp_o[2:3, 0:heads] = skip_g[...]
    inner = chp_o.shape[1]
    repeated = lax.dot_general(
        hp_o[...], gather_mat(inner), (((1,), (1,)), ((), ())), precision=EXACT,
        preferred_element_type=F32,
    )
    chp_o[0:4, :] = conv_v[...]
    chp_o[4:5, :] = bias_v[...]
    chp_o[5:6, :] = gate_g[...]
    chp_o[6:7, :] = repeated[2:3, :]
    chp_o[7:8, :] = jnp.zeros((1, inner), F32)
    shp_o[...] = jnp.zeros_like(shp_o)
    shp_o[0:4, :] = conv_s[...]
    shp_o[4:5, :] = bias_s[...]


def small_sum(x, axis, collective_id):
    count = lax.axis_size(axis)

    def body(x_ref, out_ref, slots, send, recv):
        me = lax.axis_index(axis)
        barrier = pltpu.get_barrier_semaphore()
        for k in range(1, count):
            peer = lax.rem(me + k, count)
            pl.semaphore_signal(barrier, inc=1, device_id={axis: peer}, device_id_type=MESH)
        pl.semaphore_wait(barrier, count - 1)
        copies = []
        for k in range(1, count):
            copies.append(
                pltpu.make_async_remote_copy(
                    src_ref=x_ref,
                    dst_ref=slots.at[k],
                    send_sem=send.at[k],
                    recv_sem=recv.at[k],
                    device_id={axis: lax.rem(me + k, count)},
                    device_id_type=MESH,
                )
            )
            copies[-1].start()
        slots[0] = x_ref[...]
        for copy in copies:
            copy.wait()
        total = slots[me]
        for source in range(1, count):
            total = total + slots[lax.rem(me - source + count, count)]
        out_ref[...] = total

    return pl.pallas_call(
        body,
        in_specs=[pl.BlockSpec(memory_space=pltpu.VMEM)],
        out_specs=pl.BlockSpec(memory_space=pltpu.VMEM),
        out_shape=jax.ShapeDtypeStruct(x.shape, x.dtype),
        scratch_shapes=[
            pltpu.VMEM((count,) + x.shape, x.dtype),
            pltpu.SemaphoreType.DMA((count,)),
            pltpu.SemaphoreType.DMA((count,)),
        ],
        compiler_params=pltpu.CompilerParams(collective_id=collective_id, has_side_effects=True),
        name="small_sum_" + axis,
    )(x)


def cost(micros):
    return pl.CostEstimate(
        flops=int(micros * 1e9), bytes_accessed=int(micros * 3.6e6), transcendentals=0
    )


def block_specs(blocks, backward):
    def spec(shape, kind):
        if kind == "whole":
            return pl.BlockSpec(shape, lambda i: (0,) * len(shape))
        if kind == "lanes":
            block = (shape[0], shape[1] // blocks)
            return pl.BlockSpec(block, (lambda i: (0, blocks - 1 - i)) if backward else (lambda i: (0, i)))
        block = (shape[0] // blocks, shape[1])
        return pl.BlockSpec(block, (lambda i: (blocks - 1 - i, 0)) if backward else (lambda i: (i, 0)))

    return spec


def call(body, blocks, ins, outs, scratch, backward, name, micros):
    spec = block_specs(blocks, backward)
    return pl.pallas_call(
        body,
        grid=(blocks,),
        in_specs=[spec(a.shape, kind) for a, kind in ins],
        out_specs=[spec(shape, kind) for shape, _, kind in outs],
        out_shape=[jax.ShapeDtypeStruct(shape, dtype) for shape, dtype, _ in outs],
        scratch_shapes=scratch,
        compiler_params=pltpu.CompilerParams(
            dimension_semantics=("arbitrary",), vmem_limit_bytes=60 * 1024 * 1024
        ),
        cost_estimate=cost(micros),
        name=name,
    )(*[a for a, _ in ins])


def signal_all(groups):
    barrier = pltpu.get_barrier_semaphore()
    for axis, peers in groups:
        for peer in peers:
            pl.semaphore_signal(barrier, inc=1, device_id={axis: peer}, device_id_type=MESH)
    pl.semaphore_wait(barrier, sum(len(peers) for _, peers in groups))


def push(src, dst, send, recv, axis, peer):
    copy = pltpu.make_async_remote_copy(
        src_ref=src, dst_ref=dst, send_sem=send, recv_sem=recv, device_id={axis: peer},
        device_id_type=MESH,
    )
    copy.start()
    return copy


def span(start, size):
    return pl.ds(pl.multiple_of(start, size), size)


def split_dp(count):
    small = 1
    while 2 * small * 2 * small * 2 <= count:
        small *= 2
    return small, count // small


def mid_step(mixed, hidden, gate_low, cotangent, normal, collective_id, micros):
    length, width = mixed.shape
    inner = gate_low.shape[1]
    nd = lax.axis_size("dp")
    nx, nz = split_dp(nd)
    rows = width // nd
    half = length // 2
    chunk = 256

    def body(mixed_r, hid, low, cot, nor, half_o, buf, near, send, recv):
        me = lax.axis_index("tensor")
        side = lax.rem(me, 2)
        sibling = me + 1 - 2 * side
        signal_all([("tensor", [sibling])])
        copy = push(
            mixed_r.at[span((1 - side) * half, half)], near, send.at[0], recv.at[0], "tensor", sibling
        )
        for c in range(width // chunk):
            cols = slice(c * chunk, (c + 1) * chunk)
            left = t_mm(hid[:, cols], low[...]).astype(BF16)
            right = t_mm(cot[:, cols], nor[...]).astype(BF16)
            for d in range(c * chunk // rows, (c + 1) * chunk // rows):
                at = slice(d * rows - c * chunk, (d + 1) * rows - c * chunk)
                place = slice((d // nx) * rows, (d // nx + 1) * rows)
                buf[d % nx, place, :inner] = left[at]
                buf[d % nx, place, inner:] = right[at]
        copy.wait()
        mine = mixed_r[span(side * half, half), :].astype(F32) + near[...].astype(F32)
        half_o[...] = mine.astype(BF16)

    vm = pl.BlockSpec(memory_space=pltpu.VMEM)
    return pl.pallas_call(
        body,
        in_specs=[vm] * 5,
        out_specs=[vm] * 2,
        out_shape=[
            jax.ShapeDtypeStruct((half, width), BF16),
            jax.ShapeDtypeStruct((nx, nz * rows, 2 * inner), BF16),
        ],
        scratch_shapes=[
            pltpu.VMEM((half, width), BF16),
            pltpu.SemaphoreType.DMA((1,)),
            pltpu.SemaphoreType.DMA((1,)),
        ],
        compiler_params=pltpu.CompilerParams(
            collective_id=collective_id, has_side_effects=True, vmem_limit_bytes=60 * 1024 * 1024
        ),
        cost_estimate=cost(micros),
        name="mid_step",
    )(mixed, hidden, gate_low, cotangent, normal)


def bwd_step(ins, outs, scratch, dw, mixed_half, blocks, collective_id, micros):
    nt, nd = lax.axis_size("tensor"), lax.axis_size("dp")
    chips = nt // 2
    nx, nz = split_dp(nd)
    part, cols = dw.shape[1:]
    rows = part // nz
    per = -(-(nz - 1) // (blocks - 1))

    def body(*refs):
        refs = list(refs)

        def take(n):
            out = refs[:n]
            del refs[:n]
            return out

        plain_in = take(len(ins))
        dw_h, mix_h = take(2)
        plain_out = take(len(outs))
        sum_o, far_o = take(2)
        plain_scratch = take(len(scratch))
        keep, xslot, zsrc, zslot, loc, m_s, m_r, x_s, x_r, z_s, z_r = refs
        step = pl.program_id(0)
        me, md = lax.axis_index("tensor"), lax.axis_index("dp")
        side, chip = lax.rem(me, 2), me // 2
        x, z = lax.rem(md, nx), md // nx

        def remote(src, dst, send, recv, axis, peer):
            return pltpu.make_async_remote_copy(
                src_ref=src, dst_ref=dst, send_sem=send, recv_sem=recv, device_id={axis: peer},
                device_id_type=MESH,
            )

        def mate(q):
            return 2 * lax.rem(chip + q, chips) + side

        def x_peer(q):
            return z * nx + lax.rem(x + q, nx)

        def z_peer(k):
            return lax.rem(z + k, nz) * nx + x

        def place(p):
            return span(lax.rem(z + 1 + p, nz) * rows, rows)

        def mix_copy(q):
            return remote(mix_h, far_o.at[q - 1], m_s.at[q - 1], m_r.at[q - 1], "tensor", mate(q))

        def x_copy(q, p):
            return remote(
                dw_h.at[lax.rem(x + q, nx), place(p)], xslot.at[q - 1, p], x_s.at[q - 1, p],
                x_r.at[q - 1, p], "dp", x_peer(q),
            )

        def z_copy(p):
            return remote(
                zsrc.at[p], zslot.at[p], z_s.at[p], z_r.at[p], "dp", z_peer(p + 1)
            )

        def keep_copy():
            return pltpu.make_async_copy(dw_h.at[x], keep, loc.at[0])

        def gather_piece(p):
            for q in range(1, nx):
                x_copy(q, p).wait_recv()
            total = keep[place(p), :].astype(F32)
            for q in range(1, nx):
                total = total + xslot[q - 1, p].astype(F32)
            return total

        @pl.when(step == 0)
        def _():
            keep_copy().start()
            signal_all([
                ("tensor", [mate(q) for q in range(1, chips)]),
                ("dp", [x_peer(q) for q in range(1, nx)] + [z_peer(k) for k in range(1, nz)]),
            ])
            for p in range(nz):
                for q in range(1, nx):
                    x_copy(q, p).start()
            for q in range(1, chips):
                mix_copy(q).start()

        for s in range(1, blocks):

            @pl.when(step == s)
            def _(s=s):
                if s == 1:
                    keep_copy().wait()
                for p in range((s - 1) * per, min(s * per, nz - 1)):
                    zsrc[p] = gather_piece(p).astype(BF16)
                    z_copy(p).start()

        bwd_kernel(*plain_in, *plain_out, *plain_scratch)

        @pl.when(step == blocks - 1)
        def _():
            total = gather_piece(nz - 1)
            for p in range(nz - 1):
                z_copy(p).wait_recv()
                total = total + zslot[p].astype(F32)
            sum_o[...] = total
            for q in range(1, chips):
                mix_copy(q).wait()
            for p in range(nz - 1):
                z_copy(p).wait_send()
            for p in range(nz):
                for q in range(1, nx):
                    x_copy(q, p).wait_send()

    spec = block_specs(blocks, True)
    hbm = pl.BlockSpec(memory_space=pl.ANY)
    dma = pltpu.SemaphoreType.DMA
    return pl.pallas_call(
        body,
        grid=(blocks,),
        in_specs=[spec(a.shape, kind) for a, kind in ins] + [hbm, hbm],
        out_specs=[spec(shape, kind) for shape, _, kind in outs] + [spec((rows, cols), "whole"), hbm],
        out_shape=[jax.ShapeDtypeStruct(shape, dtype) for shape, dtype, _ in outs]
        + [
            jax.ShapeDtypeStruct((rows, cols), F32),
            jax.ShapeDtypeStruct((chips - 1,) + mixed_half.shape, BF16),
        ],
        scratch_shapes=scratch
        + [
            pltpu.VMEM((part, cols), BF16),
            pltpu.VMEM((nx - 1, nz, rows, cols), BF16),
            pltpu.VMEM((nz - 1, rows, cols), BF16),
            pltpu.VMEM((nz - 1, rows, cols), BF16),
            dma((1,)), dma((chips - 1,)), dma((chips - 1,)), dma((nx - 1, nz)), dma((nx - 1, nz)),
            dma((nz - 1,)), dma((nz - 1,)),
        ],
        compiler_params=pltpu.CompilerParams(
            dimension_semantics=("arbitrary",), collective_id=collective_id, has_side_effects=True,
            vmem_limit_bytes=60 * 1024 * 1024,
        ),
        cost_estimate=cost(micros),
        name="bwd_scan",
    )(*[a for a, _ in ins], dw, mixed_half)


def finish_kernel(
    heads, result, gtok, gate_out, value_step, shared, early, late,
    result_o, gtok_o, dgate_o, dvalue_o, dshared_o, dstep_o, dout_o,
    convv_o, biasv_o, convs_o, biass_o, h0_o, h1_o, h2_o, gain_o, norm_o,
):
    inner = dgate_o.shape[1]
    result_o[...] = result[...]
    gtok_o[...] = gtok[...]

    @pl.when(pl.program_id(0) == 0)
    def _():
        dgate_o[...] = gate_out[:, :inner]
        dout_o[...] = gate_out[:, inner:]
        dvalue_o[...] = value_step[:, :inner]
        dstep_o[...] = value_step[:, inner : inner + heads]
        dshared_o[...] = shared[...]
        convv_o[...] = early[0:4, :inner]
        biasv_o[...] = early[4:5, :inner]
        gain_o[...] = early[5:6, :inner]
        h0_o[...] = early[0:1, inner : inner + heads]
        h1_o[...] = early[1:2, inner : inner + heads]
        h2_o[...] = early[2:3, inner : inner + heads]
        convs_o[...] = late[0:4, :]
        biass_o[...] = late[4:5, :]
        norm_o[...] = late[5:6, : norm_o.shape[1]]


def tail_step(
    heads_part, dbc_part, hidden, value_low, step_low, shared_conv, shared_pre, aux, tokens, cotangent,
    ng, shared_proj, shp, mixed_half, mixed_far, ch_grads, head_grads, gain_part,
    collective_id, micros,
):
    length, width = tokens.shape
    inner = value_low.shape[1]
    shared_width = shared_proj.shape[1]
    nt, nd = lax.axis_size("tensor"), lax.axis_size("dp")
    ng_chips = nt // 2
    nx, nz = split_dp(nd)
    rows = width // nd
    quarter, half = length // nt, length // 2
    piece = quarter // PIECES
    part = nz * rows
    low_width = inner + LANES
    norm_width = width // nt
    early_width = inner + LANES
    late_width = shared_width
    blocks = length // SPAN
    chunk = 256
    n_mixed = ng_chips - 1
    n_late = 9 + n_mixed

    def body(*refs):
        refs = list(refs)

        def take(n):
            out = refs[:n]
            del refs[:n]
            return out

        heads_r, dbc, aux_r, ng_r, ws, shp_r, chg, hg, gain = take(9)
        hid_h, vlow_h, slow_h, scv_h, spre_h, tok_h, cot_h, mix_h, mixfar_h = take(9)
        result_o, gtok_o, value_o, shared_o, early_o, late_o = take(6)
        hid, low, scv, spre, tokh, tokq, cotq, mix, mixfar = take(9)
        (
            dnear, dslots, dtot, dbuf, shlow, hnear, fsrc, ffar, hacc, vbuf, vslot, sbuf, sslot,
            zv, zvslot, zs, zsslot, eslots, lslots, nbuf, nslot,
        ) = take(21)
        (
            loc, a_s, a_r, d_s, d_r, n_s, n_r, f_s, f_r, g_s, g_r, h_s, h_r, r_s, r_r,
            zv_s, zv_r, zs_s, zs_r, xv_s, xv_r, xs_s, xs_r, e_s, e_r, l_s, l_r, m_s, m_r,
        ) = take(29)

        me = lax.axis_index("tensor")
        side, chip = lax.rem(me, 2), me // 2
        sibling = 2 * chip + 1 - side
        md = lax.axis_index("dp")
        x, z = lax.rem(md, nx), md // nx

        def chip_at(q):
            return lax.rem(chip + q, ng_chips)

        def mate(q):
            return 2 * chip_at(q) + side

        def x_peer(q):
            return z * nx + lax.rem(x + q, nx)

        def z_peer(k):
            return lax.rem(z + k, nz) * nx + x

        count = [0]

        def fetch(src, dst):
            copy = pltpu.make_async_copy(src, dst, loc.at[count[0]])
            count[0] += 1
            copy.start()
            return copy

        my_rows = span(me * quarter, quarter)
        my_half = span(side * half, half)
        sib_half = span((1 - side) * half, half)
        got_low = [
            fetch(hid_h, hid), fetch(vlow_h, low.at[:, 0:inner]),
            fetch(slow_h, low.at[:, inner : inner + LANES]),
        ]
        got_mix = [fetch(mix_h, mix), fetch(tok_h.at[my_half], tokh)]
        got_mix += [fetch(mixfar_h.at[q], mixfar.at[q]) for q in range(n_mixed)]
        got_shared = [fetch(scv_h, scv), fetch(spre_h, spre)]
        got_end = [fetch(tok_h.at[my_rows], tokq), fetch(cot_h.at[my_rows], cotq)]

        signal_all([
            ("tensor", [lax.rem(me + k, nt) for k in range(1, nt)]),
            ("dp", [lax.rem(md + k, nd) for k in range(1, nd)]),
        ])
        sent = []

        def send(*args):
            copy = push(*args)
            sent.append(copy)
            return copy

        dn = send(dbc.at[sib_half], dnear, a_s.at[0], a_r.at[0], "tensor", sibling)
        order = list(range(1, ng_chips)) + [0]
        near = {}
        for q in order:
            for p in range(PIECES):
                at = (2 * chip_at(q) + 1 - side) * quarter + p * piece
                near[q, p] = send(
                    heads_r.at[span(at, piece)], hnear.at[q, p], n_s.at[q, p], n_r.at[q, p],
                    "tensor", sibling,
                )
        eslots[md, :, :inner] = jnp.concatenate(
            [chg[0:5, :], gain[0:1, :], jnp.zeros((2, inner), F32)], axis=0
        )
        eslots[md, :, inner:] = hg[...]

        dn.wait_recv()
        dslots[chip] = (dbc[my_half, :] + dnear[...]).astype(BF16)
        dmates = [
            send(dslots.at[chip], dslots.at[chip], d_s.at[q], d_r.at[q], "tensor", mate(q))
            for q in range(1, ng_chips)
        ]
        fwd = {}
        for q in order:
            for p in range(PIECES):
                near[q, p].wait_recv()
                at = (2 * chip_at(q) + side) * quarter + p * piece
                both = heads_r[span(at, piece), :].astype(F32) + hnear[q, p].astype(F32)
                if q:
                    fsrc[q, p] = both.astype(BF16)
                    fwd[q, p] = send(
                        fsrc.at[q, p], ffar.at[q, p], f_s.at[q, p], f_r.at[q, p], "tensor", mate(q)
                    )
                else:
                    hacc[p * piece : (p + 1) * piece, :] = both
        es = [
            send(
                eslots.at[md], eslots.at[md], e_s.at[k], e_r.at[k], "dp", lax.rem(md + k, nd)
            )
            for k in range(1, nd)
        ]

        for copy in got_low:
            copy.wait()
        for c in range(width // chunk):
            prod = t_mm(hid[:, c * chunk : (c + 1) * chunk], low[...]).astype(BF16)
            for d in range(c * chunk // rows, (c + 1) * chunk // rows):
                at = slice(d * rows - c * chunk, (d + 1) * rows - c * chunk)
                vbuf[d % nx, (d // nx) * rows : (d // nx + 1) * rows, :] = prod[at]
        xvs = [
            send(
                vbuf.at[lax.rem(x + q, nx)], vslot.at[q], xv_s.at[q], xv_r.at[q], "dp", x_peer(q)
            )
            for q in range(1, nx)
        ]

        for copy in got_shared:
            copy.wait()
        for copy in dmates:
            copy.wait_recv()
        total = dslots[0].astype(F32)
        for g in range(1, ng_chips):
            total = total + dslots[g].astype(F32)
        dtot[my_half, :] = total
        dt_copy = send(
            dtot.at[my_half], dtot.at[my_half], a_s.at[1], a_r.at[1], "tensor", sibling
        )

        for copy in got_mix:
            copy.wait()
        mixed = mix[...].astype(F32)
        if n_mixed == 1:
            mixed = mixed + mixfar[0].astype(F32)
        else:
            terms = [mix] + [mixfar.at[q] for q in range(n_mixed)]
            mixed = jnp.zeros((half, width), F32)
            for g in range(ng_chips):
                for q in range(ng_chips):
                    mine = (lax.rem(chip - q + ng_chips, ng_chips) == g).astype(F32)
                    mixed = mixed + terms[q][...].astype(F32) * mine
        result_o[my_half, :] = (tokh[...].astype(F32) + mixed).astype(BF16)
        res = send(
            result_o.at[my_half], result_o.at[my_half], r_s.at[0], r_r.at[0], "tensor", sibling
        )

        dt_copy.wait_recv()
        dbuf[length : length + 8, :] = jnp.zeros((8, shared_width), F32)
        sums = [jnp.zeros((1, shared_width), F32)] * 5
        for b in reversed(range(blocks)):
            base = b * SPAN
            at = slice(base, base + SPAN)
            sc = scv[at, :]
            csig = sigmoid(sc)
            dcv = dtot[at, :] * (csig * (1.0 + sc * (1.0 - csig)))
            dbuf[at, :] = dcv
            sp = spre[at, :]
            mask = aux_r[at, :]
            ds = dcv * shp_r[3:4, :]
            sums[3] = sums[3] + jnp.sum(dcv * sp, axis=0, keepdims=True)
            sums[4] = sums[4] + jnp.sum(dcv, axis=0, keepdims=True)
            for j in range(1, 4):
                moved = dbuf[base + j : base + j + SPAN, :] * mask[:, 8 + j : 9 + j]
                ds = ds + moved * shp_r[3 - j : 4 - j, :]
                sums[3 - j] = sums[3 - j] + jnp.sum(moved * sp, axis=0, keepdims=True)
            shlow[at, :] = ds.astype(BF16)
        for c in range(width // chunk):
            prod = t_mm(hid[:, c * chunk : (c + 1) * chunk], shlow[...]).astype(BF16)
            for d in range(c * chunk // rows, (c + 1) * chunk // rows):
                at = slice(d * rows - c * chunk, (d + 1) * rows - c * chunk)
                sbuf[d % nx, (d // nx) * rows : (d // nx + 1) * rows, :] = prod[at]
        xss = [
            send(
                sbuf.at[lax.rem(x + q, nx)], sslot.at[q], xs_s.at[q], xs_r.at[q], "dp", x_peer(q)
            )
            for q in range(1, nx)
        ]
        hacc[...] = hacc[...] + mm_t(shlow[my_rows, :], ws[...])

        for copy in got_end:
            copy.wait()
        norm = jnp.zeros((1, width), F32)
        gather, own = {}, []
        for p in range(PIECES):
            at = slice(p * piece, (p + 1) * piece)
            grad_hidden = hacc[at, :]
            for q in range(1, ng_chips):
                fwd[q, p].wait_recv()
                grad_hidden = grad_hidden + ffar[q, p].astype(F32)
            v = tokq[at, :].astype(F32)
            inv = lax.rsqrt(jnp.mean(v * v, axis=1, keepdims=True) + EPSILON)
            normed = v * inv
            scaled = grad_hidden * ng_r[...]
            norm = norm + jnp.sum(grad_hidden * normed, axis=0, keepdims=True)
            mean = jnp.mean(scaled * normed, axis=1, keepdims=True)
            place = span(me * quarter + p * piece, piece)
            gtok_o[place, :] = (inv * (scaled - normed * mean) + cotq[at, :].astype(F32)).astype(BF16)
            for q in range(1, ng_chips):
                gather[q, p] = send(
                    gtok_o.at[place], gtok_o.at[place], g_s.at[q, p], g_r.at[q, p], "tensor", mate(q)
                )
            own.append(
                send(gtok_o.at[place], gtok_o.at[place], h_s.at[0, p], h_r.at[0, p], "tensor", sibling)
            )
        for q in range(nt):
            nbuf[q] = norm[:, q * norm_width : (q + 1) * norm_width] + jnp.zeros((8, norm_width), F32)
        norms = [
            send(
                nbuf.at[lax.rem(me + k, nt)], nslot.at[k], m_s.at[k], m_r.at[k], "tensor",
                lax.rem(me + k, nt),
            )
            for k in range(1, nt)
        ]

        for copy in xvs:
            copy.wait_recv()
        total = vbuf[x].astype(F32)
        for q in range(1, nx):
            total = total + vslot[q].astype(F32)
        zv[...] = total.astype(BF16)
        zvs = [
            send(
                zv.at[span(lax.rem(z + k, nz) * rows, rows)], zvslot.at[k], zv_s.at[k], zv_r.at[k],
                "dp", z_peer(k),
            )
            for k in range(1, nz)
        ]
        for copy in xss:
            copy.wait_recv()
        total = sbuf[x].astype(F32)
        for q in range(1, nx):
            total = total + sslot[q].astype(F32)
        zs[...] = total.astype(BF16)
        zss = [
            send(
                zs.at[span(lax.rem(z + k, nz) * rows, rows)], zsslot.at[k], zs_s.at[k], zs_r.at[k],
                "dp", z_peer(k),
            )
            for k in range(1, nz)
        ]

        for copy in norms:
            copy.wait_recv()
        total = nbuf[me]
        for k in range(1, nt):
            total = total + nslot[k]
        wide = jnp.concatenate(
            [total[0:1, :], jnp.zeros((1, shared_width - norm_width), F32)], axis=1
        ) if norm_width < shared_width else total[0:1, :]
        lslots[md] = jnp.concatenate(sums + [wide, jnp.zeros((2, shared_width), F32)], axis=0)
        ls = [
            send(
                lslots.at[md], lslots.at[md], l_s.at[k], l_r.at[k], "dp", lax.rem(md + k, nd)
            )
            for k in range(1, nd)
        ]

        for copy in es:
            copy.wait_recv()
        total = eslots[0]
        for s in range(1, nd):
            total = total + eslots[s]
        early_o[...] = total

        for p in range(PIECES):
            for q in range(1, ng_chips):
                gather[q, p].wait_recv()
                came = 2 * lax.rem(chip - q + ng_chips, ng_chips) + side
                place = span(came * quarter + p * piece, piece)
                own.append(
                    send(
                        gtok_o.at[place], gtok_o.at[place], h_s.at[q, p], h_r.at[q, p],
                        "tensor", sibling,
                    )
                )

        for copy in zvs:
            copy.wait_recv()
        total = zv[span(z * rows, rows), :].astype(F32)
        for k in range(1, nz):
            total = total + zvslot[k].astype(F32)
        value_o[...] = total
        for copy in zss:
            copy.wait_recv()
        total = zs[span(z * rows, rows), :].astype(F32)
        for k in range(1, nz):
            total = total + zsslot[k].astype(F32)
        shared_o[...] = total

        for copy in ls:
            copy.wait_recv()
        total = lslots[0]
        for s in range(1, nd):
            total = total + lslots[s]
        late_o[...] = total

        res.wait_recv()
        for copy in own:
            copy.wait_recv()
        for copy in sent:
            copy.wait_send()

    vm = pl.BlockSpec(memory_space=pltpu.VMEM)
    hbm = pl.BlockSpec(memory_space=pl.ANY)
    dma = pltpu.SemaphoreType.DMA

    def f32(*shape):
        return pltpu.VMEM(shape, F32)

    def bf16(*shape):
        return pltpu.VMEM(shape, BF16)

    def out(*shape):
        return jax.ShapeDtypeStruct(shape, F32)

    early = [heads_part, dbc_part, aux, ng, shared_proj, shp, ch_grads, head_grads, gain_part]
    late = [hidden, value_low, step_low, shared_conv, shared_pre, tokens, cotangent, mixed_half]
    late += [mixed_far]
    return pl.pallas_call(
        body,
        in_specs=[vm] * len(early) + [hbm] * len(late),
        out_specs=[vm] * 6,
        out_shape=[
            jax.ShapeDtypeStruct((length, width), BF16), jax.ShapeDtypeStruct((length, width), BF16),
            out(rows, low_width), out(rows, shared_width), out(8, early_width), out(8, late_width),
        ],
        scratch_shapes=[
            bf16(length, width), bf16(length, low_width), f32(length, shared_width),
            f32(length, shared_width), bf16(half, width), bf16(quarter, width), bf16(quarter, width),
            bf16(half, width), bf16(n_mixed, half, width),
            f32(half, shared_width), bf16(ng_chips, half, shared_width), f32(length, shared_width),
            f32(length + 8, shared_width), bf16(length, shared_width),
            bf16(ng_chips, PIECES, piece, width), bf16(ng_chips, PIECES, piece, width),
            bf16(ng_chips, PIECES, piece, width), f32(quarter, width),
            bf16(nx, part, low_width), bf16(nx, part, low_width),
            bf16(nx, part, shared_width), bf16(nx, part, shared_width),
            bf16(part, low_width), bf16(nz, rows, low_width),
            bf16(part, shared_width), bf16(nz, rows, shared_width),
            f32(nd, 8, early_width), f32(nd, 8, late_width),
            f32(nt, 8, norm_width), f32(nt, 8, norm_width),
        ]
        + [dma((n_late + 1,)), dma((2,)), dma((2,)), dma((ng_chips,)), dma((ng_chips,))]
        + [dma((ng_chips, PIECES))] * 8
        + [dma((1,)), dma((1,))]
        + [dma((nz,))] * 4
        + [dma((nx,))] * 4
        + [dma((nd,))] * 4
        + [dma((nt,))] * 2,
        compiler_params=pltpu.CompilerParams(
            collective_id=collective_id, has_side_effects=True, vmem_limit_bytes=60 * 1024 * 1024
        ),
        cost_estimate=cost(micros),
        name="tail_step",
    )(*early, *late)


def per_device(
    tokens, cotangent, segments, norm_gain, gate_proj, value_proj, shared_proj, step_proj,
    conv_value, bias_value, conv_shared, bias_shared, step_bias, decay_log, skip_gain,
    gate_gain, out_proj,
):
    tp_count = lax.axis_size("tensor")
    dp_count = lax.axis_size("dp")
    length, width = tokens.shape
    inner = gate_proj.shape[1]
    heads = step_proj.shape[1]
    shared_width = shared_proj.shape[1]
    state_size = shared_width // 2
    blocks = length // SPAN
    aux, segr, wst, chp, shp, hp = pl.pallas_call(
        prep_kernel,
        out_shape=[
            jax.ShapeDtypeStruct((length, LANES), F32),
            jax.ShapeDtypeStruct((1, length), F32),
            jax.ShapeDtypeStruct((width, LANES), BF16),
            jax.ShapeDtypeStruct((8, inner), F32),
            jax.ShapeDtypeStruct((8, shared_width), F32),
            jax.ShapeDtypeStruct((8, LANES), F32),
        ],
        name="prep_step",
    )(
        segments, step_proj.T, conv_value, bias_value[None], gate_gain[None], skip_gain[None],
        conv_shared, bias_shared[None], step_bias[None], decay_log[None],
    )
    ng = norm_gain[None, :]

    (
        hidden, gate_pre, value_pre, conv_out, shared_pre, shared_conv, z, ld, ldt, yn, sin, gn, stat,
    ) = call(
        fwd_kernel,
        blocks,
        [
            (tokens, "rows"), (cotangent, "rows"), (aux, "rows"), (segr, "lanes"), (ng, "whole"),
            (gate_proj, "whole"), (value_proj, "whole"), (shared_proj, "whole"), (wst, "whole"),
            (out_proj, "whole"), (chp, "whole"), (shp, "whole"), (hp, "whole"),
        ],
        [
            ((length, width), BF16, "rows"),
            ((length, inner), F32, "rows"),
            ((length, inner), F32, "rows"),
            ((length, inner), F32, "rows"),
            ((length, shared_width), F32, "rows"),
            ((length, shared_width), F32, "rows"),
            ((length, LANES), F32, "rows"),
            ((length, LANES), F32, "rows"),
            ((8, length), F32, "lanes"),
            ((length, inner), F32, "rows"),
            ((blocks * state_size, inner), F32, "rows"),
            ((length, inner), F32, "rows"),
            ((8, length), F32, "lanes"),
        ],
        [
            pltpu.VMEM((SPAN + 8, inner), F32),
            pltpu.VMEM((SPAN + 8, shared_width), F32),
            pltpu.VMEM((state_size, inner), F32),
        ],
        False,
        "fwd_scan",
        20,
    )
    stat = small_sum(stat, "tensor", 0)
    total_inner = float(inner * tp_count)

    def gate_body(*refs):
        gate_kernel(total_inner, *refs)

    normal_out, dy, gate_low, gain_part, mixed_part = call(
        gate_body,
        blocks,
        [
            (gate_pre, "rows"), (conv_out, "rows"), (yn, "rows"), (gn, "rows"), (stat, "lanes"),
            (chp, "whole"), (out_proj, "whole"),
        ],
        [
            ((length, inner), BF16, "rows"),
            ((length, inner), F32, "rows"),
            ((length, inner), BF16, "rows"),
            ((8, inner), F32, "whole"),
            ((length, width), BF16, "rows"),
        ],
        [],
        False,
        "gate_step",
        9,
    )
    mixed_half, dw = mid_step(mixed_part, hidden, gate_low, cotangent, normal_out, 1, 6)
    value_low, step_low, heads_part, dbc_part, ch_grads, head_grads, gate_out, mixed_far = bwd_step(
        [
            (dy, "rows"), (conv_out, "rows"), (value_pre, "rows"), (shared_conv, "rows"),
            (z, "rows"), (ld, "rows"), (ldt, "lanes"), (yn, "rows"), (sin, "rows"),
            (aux, "rows"), (segr, "lanes"), (gate_low, "rows"), (gate_proj, "whole"),
            (value_proj, "whole"), (wst, "whole"), (chp, "whole"), (hp, "whole"),
        ],
        [
            ((length, inner), BF16, "rows"),
            ((length, LANES), BF16, "rows"),
            ((length, width), BF16, "rows"),
            ((length, shared_width), F32, "rows"),
            ((8, inner), F32, "whole"),
            ((8, LANES), F32, "whole"),
        ],
        [pltpu.VMEM((SPAN + 8, inner), F32), pltpu.VMEM((state_size, inner), F32)],
        dw, mixed_half, blocks, 3, 27,
    )
    result, grad_tokens, value_step, shared_sum, early, late = tail_step(
        heads_part, dbc_part, hidden, value_low, step_low, shared_conv, shared_pre, aux, tokens,
        cotangent, ng, shared_proj, shp, mixed_half, mixed_far, ch_grads, head_grads,
        gain_part, 2, 40,
    )

    def finish_body(*refs):
        finish_kernel(heads, *refs)

    rows = width // dp_count
    (
        result, grad_tokens, dgate, dvalue, dshared, dstep, dout,
        convv, biasv, convs, biass, h0, h1, h2, gain, norm,
    ) = call(
        finish_body,
        blocks,
        [
            (result, "rows"), (grad_tokens, "rows"), (gate_out, "whole"), (value_step, "whole"),
            (shared_sum, "whole"), (early, "whole"), (late, "whole"),
        ],
        [
            ((length, width), BF16, "rows"), ((length, width), BF16, "rows"),
            ((rows, inner), F32, "whole"), ((rows, inner), F32, "whole"),
            ((rows, shared_width), F32, "whole"), ((rows, heads), F32, "whole"),
            ((rows, inner), F32, "whole"), ((4, inner), F32, "whole"), ((1, inner), F32, "whole"),
            ((4, shared_width), F32, "whole"), ((1, shared_width), F32, "whole"),
            ((1, heads), F32, "whole"), ((1, heads), F32, "whole"), ((1, heads), F32, "whole"),
            ((1, inner), F32, "whole"), ((1, width // tp_count), F32, "whole"),
        ],
        [],
        False,
        "finish_step",
        3,
    )
    return (
        result, grad_tokens, norm[0], dgate, dvalue, dshared, dstep, convv, biasv[0], convs, biass[0],
        h0[0], h1[0], h2[0], gain[0], dout,
    )


def solution(mesh):
    rows, cols, vec = P("dp", None), P(None, "tensor"), P("tensor")
    return jax.shard_map(
        per_device,
        mesh=mesh,
        in_specs=(
            rows, rows, rows, P(), cols, cols, P(), cols, cols, vec, P(), P(), vec, vec, vec, vec, cols,
        ),
        out_specs=(
            rows, rows, vec, P("dp", "tensor"), P("dp", "tensor"), rows, P("dp", "tensor"), cols, vec,
            P(), P(), vec, vec, vec, vec, P("dp", "tensor"),
        ),
        check_vma=False,
    )
```

```python
import jax
import jax.numpy as jnp
from jax import lax
from jax.experimental import pallas as pl
from jax.experimental.pallas import tpu as pltpu
from jax.sharding import PartitionSpec as P

SPAN = 256
HSIZE = 64
LANES = 128
EPSILON = 1e-05
NEG_FILL = -1e30
EXACT = lax.Precision.HIGHEST
F32 = jnp.float32
BF16 = jnp.bfloat16


def mm(left, right):
    return jnp.dot(left, right, preferred_element_type=F32)


def mm_t(left, right):
    return lax.dot_general(left, right, (((1,), (1,)), ((), ())), preferred_element_type=F32)


def t_mm(left, right):
    return lax.dot_general(left, right, (((0,), (0,)), ((), ())), preferred_element_type=F32)


def exact(left, right):
    return jnp.dot(left, right, precision=EXACT, preferred_element_type=F32)


def sigmoid(v):
    return 1.0 / (1.0 + jnp.exp(-v))


def spread(cols, pairs):
    low = lax.broadcasted_iota(jnp.int32, (cols.shape[0], LANES), 1) < HSIZE
    parts = [
        jnp.where(low, cols[:, 2 * p : 2 * p + 1], cols[:, 2 * p + 1 : 2 * p + 2])
        for p in range(pairs)
    ]
    return jnp.concatenate(parts, axis=1)


def gather_mat(inner):
    channel = lax.broadcasted_iota(jnp.int32, (inner, LANES), 0) // HSIZE
    head = lax.broadcasted_iota(jnp.int32, (inner, LANES), 1)
    return (channel == head).astype(F32)


def grid_masks():
    row = lax.broadcasted_iota(jnp.int32, (SPAN, SPAN), 0)
    col = lax.broadcasted_iota(jnp.int32, (SPAN, SPAN), 1)
    return row, col


def conv_fwd(buf, pack, aux):
    out = pack[4:5, :] + buf[8 : 8 + SPAN, :] * pack[3:4, :]
    for j in range(1, 4):
        out = out + buf[8 - j : 8 - j + SPAN, :] * (aux[:, j : j + 1] * pack[3 - j : 4 - j, :])
    return out


def fwd_kernel(
    tok, cot, aux_ref, segr, ng, wg, wv, ws, wst, wo, chp, shp, hp,
    hidden_o, gate_o, vpre_o, cv_o, spre_o, scv_o, z_o, ld_o, ldt_o, yn_o, sin_o, gn_o, stat_o,
    vbuf, sbuf, state,
):
    inner = wg.shape[1]
    pairs = inner // LANES
    state_size = ws.shape[1] // 2

    @pl.when(pl.program_id(0) == 0)
    def _():
        vbuf[0:8, :] = jnp.zeros((8, inner), F32)
        sbuf[0:8, :] = jnp.zeros((8, 2 * state_size), F32)
        state[...] = jnp.zeros_like(state)

    aux = aux_ref[...]
    x = tok[...].astype(F32)
    inv = lax.rsqrt(jnp.mean(x * x, axis=1, keepdims=True) + EPSILON)
    hid = (x * inv * ng[...]).astype(BF16)
    hidden_o[...] = hid
    gate = mm(hid, wg[...])
    gate_o[...] = gate
    vp = mm(hid, wv[...])
    vpre_o[...] = vp
    vbuf[8 : 8 + SPAN, :] = vp
    sp = mm(hid, ws[...])
    spre_o[...] = sp
    sbuf[8 : 8 + SPAN, :] = sp
    z = mm(hid, wst[...]) + hp[0:1, :]
    z_o[...] = z
    gn = mm(cot[...], wo[...])
    gn_o[...] = gn
    scv = conv_fwd(sbuf, shp, aux)
    scv_o[...] = scv
    bc = (scv * sigmoid(scv)).astype(BF16)
    b_low, c_low = bc[:, :state_size], bc[:, state_size:]
    cv = conv_fwd(vbuf, chp, aux)
    cv_o[...] = cv
    vbuf[0:8, :] = vbuf[SPAN : SPAN + 8, :]
    sbuf[0:8, :] = sbuf[SPAN : SPAN + 8, :]
    values = cv * sigmoid(cv)
    dt = jnp.maximum(z, 0.0) + jnp.log1p(jnp.exp(-jnp.abs(z)))
    row, col = grid_masks()
    tri = (row >= col).astype(F32)
    ld = exact(tri, dt * hp[1:2, :])
    ld_o[...] = ld
    ldt = jnp.transpose(ld)[0:8, :]
    ldt_o[...] = ldt
    allowed = (row >= col) & (aux[:, 0:1] == segr[...])
    scores = jnp.where(allowed, mm_t(c_low, b_low), 0.0)
    xs = values * spread(dt, pairs)
    xs_low = xs.astype(BF16)
    ein = jnp.exp(ld) * aux[:, 4:5]
    eout = jnp.exp(ld[SPAN - 1 : SPAN, :] - ld) * aux[:, 5:6]
    ein_x = spread(ein, pairs)
    eout_x = spread(eout, pairs)
    old = state[...]
    sin_o[...] = old
    carried = mm(c_low, old.astype(BF16)) * ein_x
    state[...] = old * ein_x[SPAN - 1 : SPAN, :] + t_mm(b_low, (xs * eout_x).astype(BF16))
    low = lax.broadcasted_iota(jnp.int32, (SPAN, LANES), 1) < HSIZE
    parts = []
    for p in range(pairs):
        pair = xs_low[:, p * LANES : (p + 1) * LANES]
        outs = []
        for h in (2 * p, 2 * p + 1):
            gap = jnp.minimum(ld[:, h : h + 1] - ldt[h : h + 1, :], 0.0)
            outs.append(mm((jnp.exp(gap) * scores).astype(BF16), pair))
        parts.append(jnp.where(low, outs[0], outs[1]))
    yn = jnp.concatenate(parts, axis=1) + carried
    yn_o[...] = yn
    gated = (yn + chp[6:7, :] * values) * (gate * sigmoid(gate))
    squares = jnp.sum(gated * gated, axis=1, keepdims=True)
    dots = jnp.sum(gn * chp[5:6, :] * gated, axis=1, keepdims=True)
    lane = lax.broadcasted_iota(jnp.int32, (SPAN, LANES), 1)
    both = jnp.where(lane == 0, squares, jnp.where(lane == 1, dots, 0.0))
    stat_o[...] = jnp.transpose(both)[0:8, :]


def gate_kernel(
    width, gate_ref, cv_ref, yn, gn_ref, stat, chp, wo, normal_o, dy_o, low_o, gain_o, mixed_o
):
    both = jnp.transpose(jnp.concatenate([stat[...]] * (LANES // 8), axis=0))
    inv = lax.rsqrt(both[:, 0:1] / width + EPSILON)
    mean_dots = both[:, 1:2] / width
    gate = gate_ref[...]
    cv = cv_ref[...]
    gn = gn_ref[...]
    sig = sigmoid(gate)
    act = gate * sig
    mixer = yn[...] + chp[6:7, :] * (cv * sigmoid(cv))
    gated = mixer * act
    normed = gated * inv
    normal = (normed * chp[5:6, :]).astype(BF16)
    normal_o[...] = normal
    mixed_o[...] = mm_t(normal, wo[...]).astype(BF16)
    part = jnp.sum(gn * normed, axis=0, keepdims=True)

    @pl.when(pl.program_id(0) == 0)
    def _():
        gain_o[...] = jnp.zeros_like(gain_o)

    gain_o[0:1, :] += part
    grad_gated = inv * (gn * chp[5:6, :]) - gated * (inv * inv * inv) * mean_dots
    dy_o[...] = grad_gated * act
    low_o[...] = (grad_gated * mixer * (sig * (1.0 + gate * (1.0 - sig)))).astype(BF16)


def bwd_kernel(
    dy_ref, cv_ref, vpre, scv_ref, z_ref, ld_ref, ldt_ref, yn, sin, aux_ref, segr, glow,
    wg, wv, wst, chp, hp,
    vlow_o, slow_o, heads_o, dbc_o, chg_o, hg_o,
    dbuf, dstate,
):
    inner = wg.shape[1]
    pairs = inner // LANES
    state_size = sin.shape[0]

    @pl.when(pl.program_id(0) == 0)
    def _():
        dbuf[SPAN : SPAN + 8, :] = jnp.zeros((8, inner), F32)
        dstate[...] = jnp.zeros_like(dstate)
        chg_o[...] = jnp.zeros_like(chg_o)
        hg_o[...] = jnp.zeros_like(hg_o)

    aux = aux_ref[...]
    dy = dy_ref[...]
    dy_low = dy.astype(BF16)
    scv = scv_ref[...]
    bc = (scv * sigmoid(scv)).astype(BF16)
    b_low, c_low = bc[:, :state_size], bc[:, state_size:]
    cv = cv_ref[...]
    csig = sigmoid(cv)
    values = cv * csig
    z = z_ref[...]
    dt = jnp.maximum(z, 0.0) + jnp.log1p(jnp.exp(-jnp.abs(z)))
    ld = ld_ref[...]
    ldt = ldt_ref[...]
    dt_x = spread(dt, pairs)
    xs = values * dt_x
    xs_low = xs.astype(BF16)
    ein = jnp.exp(ld) * aux[:, 4:5]
    eout = jnp.exp(ld[SPAN - 1 : SPAN, :] - ld) * aux[:, 5:6]
    ein_x = spread(ein, pairs)
    eout_x = spread(eout, pairs)
    row, col = grid_masks()
    allowed = (col >= row) & (aux[:, 0:1] == segr[...])
    mask = allowed.astype(F32)
    scores_t = mm_t(b_low, c_low) * mask
    low = lax.broadcasted_iota(jnp.int32, (SPAN, LANES), 1) < HSIZE
    parts = []
    dscores_t = jnp.zeros((SPAN, SPAN), F32)
    for p in range(pairs):
        cols = slice(p * LANES, (p + 1) * LANES)
        dy_pair = dy_low[:, cols]
        xs_pair = xs_low[:, cols]
        zero = jnp.zeros_like(xs_pair)
        outs = []
        for side, h in enumerate((2 * p, 2 * p + 1)):
            gap = jnp.minimum(ldt[h : h + 1, :] - ld[:, h : h + 1], 0.0)
            decay = jnp.exp(gap)
            outs.append(mm((decay * scores_t).astype(BF16), dy_pair))
            mine = jnp.where(low, xs_pair, zero) if side == 0 else jnp.where(low, zero, xs_pair)
            dscores_t = dscores_t + mm_t(mine, dy_pair) * decay
        parts.append(jnp.where(low, outs[0], outs[1]))
    inside = jnp.concatenate(parts, axis=1)
    dscores_low = (dscores_t * mask).astype(BF16)
    old = sin[...]
    dst = dstate[...]
    dst_low = dst.astype(BF16)
    dye_low = (dy * ein_x).astype(BF16)
    xse_low = (xs * eout_x).astype(BF16)
    db = mm(dscores_low, c_low) + mm_t(xse_low, dst_low)
    dc = t_mm(dscores_low, b_low) + mm_t(dye_low, old.astype(BF16))
    late = mm(b_low, dst_low) * eout_x
    keep = ein_x[SPAN - 1 : SPAN, :]
    dstate[...] = dst * keep + t_mm(c_low, dye_low)
    dxs = inside + late
    collect = gather_mat(inner)
    q = dy_low.astype(F32) * yn[...] - xs_low.astype(F32) * inside
    u = xs * late
    kappa = exact(jnp.sum(old * dst, axis=0, keepdims=True) * keep + jnp.zeros((8, inner), F32), collect)
    da = (
        exact((col >= row).astype(F32), exact(q, collect))
        + exact((row > col).astype(F32), exact(u, collect))
        + kappa[0:1, :]
    )
    rates = hp[1:2, :]
    ddt = da * rates + exact(dxs * values, collect)
    dz = ddt * sigmoid(z)
    slow = dz.astype(BF16)
    slow_o[...] = slow
    skip = exact(jnp.sum(dy * values, axis=0, keepdims=True) + jnp.zeros((8, inner), F32), collect)
    hg_o[0:1, :] += jnp.sum(dz, axis=0, keepdims=True)
    hg_o[1:2, :] += jnp.sum(da * dt, axis=0, keepdims=True) * rates
    hg_o[2:3, :] += skip[0:1, :]
    dcv = (dxs * dt_x + chp[6:7, :] * dy) * (csig * (1.0 + cv * (1.0 - csig)))
    dbuf[0:SPAN, :] = dcv
    vp = vpre[...]
    dv = dcv * chp[3:4, :]
    chg_o[3:4, :] += jnp.sum(dcv * vp, axis=0, keepdims=True)
    chg_o[4:5, :] += jnp.sum(dcv, axis=0, keepdims=True)
    for j in range(1, 4):
        moved = dbuf[j : j + SPAN, :] * aux[:, 8 + j : 9 + j]
        dv = dv + moved * chp[3 - j : 4 - j, :]
        chg_o[3 - j : 4 - j, :] += jnp.sum(moved * vp, axis=0, keepdims=True)
    dbuf[SPAN : SPAN + 8, :] = dbuf[0:8, :]
    vlow = dv.astype(BF16)
    vlow_o[...] = vlow
    back = mm_t(glow[...], wg[...]) + mm_t(vlow, wv[...]) + mm_t(slow, wst[...])
    heads_o[...] = back.astype(BF16)
    dbc_o[...] = jnp.concatenate([db, dc], axis=1)


MESH = pl.DeviceIdType.MESH
PIECES = 4


def prep_kernel(
    seg, stepw, conv_v, bias_v, gate_g, skip_g, conv_s, bias_s, step_b, decay,
    aux_o, segr_o, wst_o, chp_o, shp_o, hp_o,
):
    length = seg.shape[1]
    ids = seg[...].astype(F32)
    segr_o[...] = ids
    wide = ids + jnp.zeros((8, length), F32)
    lane = lax.broadcasted_iota(jnp.int32, (8, length), 1)
    row = lax.broadcasted_iota(jnp.int32, (8, length), 0)
    ends = [
        ids[:, start + SPAN - 1 : start + SPAN] + jnp.zeros((8, SPAN), F32)
        for start in range(0, length, SPAN)
    ]
    last = jnp.concatenate(ends, axis=1)
    before = jnp.concatenate([jnp.full((8, SPAN), -1.0, F32)] + ends[:-1], axis=1)
    first = jnp.where(row == 0, wide, 0.0)
    first = jnp.where((row == 4) & (wide == before), 1.0, first)
    first = jnp.where((row == 5) & (wide == last), 1.0, first)
    second = jnp.zeros((8, length), F32)
    for j in range(1, 4):
        back = (pltpu.roll(wide, j, 1) == wide) & (lane >= j)
        ahead = (pltpu.roll(wide, length - j, 1) == wide) & (lane < length - j)
        first = jnp.where((row == j) & back, 1.0, first)
        second = jnp.where((row == j) & ahead, 1.0, second)
    rest = jnp.zeros((LANES - 16, length), F32)
    aux_o[...] = jnp.transpose(jnp.concatenate([first, second, rest], axis=0))
    heads, width = stepw.shape
    steps = jnp.concatenate([stepw[...].astype(F32), jnp.zeros((LANES - heads, width), F32)], axis=0)
    wst_o[...] = jnp.transpose(steps).astype(BF16)
    hp_o[...] = jnp.zeros_like(hp_o)
    hp_o[0:1, 0:heads] = step_b[...]
    hp_o[1:2, 0:heads] = -jnp.exp(decay[...])
    hp_o[2:3, 0:heads] = skip_g[...]
    inner = chp_o.shape[1]
    repeated = lax.dot_general(
        hp_o[...], gather_mat(inner), (((1,), (1,)), ((), ())), precision=EXACT,
        preferred_element_type=F32,
    )
    chp_o[0:4, :] = conv_v[...]
    chp_o[4:5, :] = bias_v[...]
    chp_o[5:6, :] = gate_g[...]
    chp_o[6:7, :] = repeated[2:3, :]
    chp_o[7:8, :] = jnp.zeros((1, inner), F32)
    shp_o[...] = jnp.zeros_like(shp_o)
    shp_o[0:4, :] = conv_s[...]
    shp_o[4:5, :] = bias_s[...]


def small_sum(x, axis, collective_id):
    count = lax.axis_size(axis)

    def body(x_ref, out_ref, slots, send, recv):
        me = lax.axis_index(axis)
        barrier = pltpu.get_barrier_semaphore()
        for k in range(1, count):
            peer = lax.rem(me + k, count)
            pl.semaphore_signal(barrier, inc=1, device_id={axis: peer}, device_id_type=MESH)
        pl.semaphore_wait(barrier, count - 1)
        copies = []
        for k in range(1, count):
            copies.append(
                pltpu.make_async_remote_copy(
                    src_ref=x_ref,
                    dst_ref=slots.at[k],
                    send_sem=send.at[k],
                    recv_sem=recv.at[k],
                    device_id={axis: lax.rem(me + k, count)},
                    device_id_type=MESH,
                )
            )
            copies[-1].start()
        slots[0] = x_ref[...]
        for copy in copies:
            copy.wait()
        total = slots[me]
        for source in range(1, count):
            total = total + slots[lax.rem(me - source + count, count)]
        out_ref[...] = total

    return pl.pallas_call(
        body,
        in_specs=[pl.BlockSpec(memory_space=pltpu.VMEM)],
        out_specs=pl.BlockSpec(memory_space=pltpu.VMEM),
        out_shape=jax.ShapeDtypeStruct(x.shape, x.dtype),
        scratch_shapes=[
            pltpu.VMEM((count,) + x.shape, x.dtype),
            pltpu.SemaphoreType.DMA((count,)),
            pltpu.SemaphoreType.DMA((count,)),
        ],
        compiler_params=pltpu.CompilerParams(collective_id=collective_id, has_side_effects=True),
        name="small_sum_" + axis,
    )(x)


def cost(micros):
    return pl.CostEstimate(
        flops=int(micros * 1e9), bytes_accessed=int(micros * 3.6e6), transcendentals=0
    )


def block_specs(blocks, backward):
    def spec(shape, kind):
        if kind == "whole":
            return pl.BlockSpec(shape, lambda i: (0,) * len(shape))
        if kind == "lanes":
            block = (shape[0], shape[1] // blocks)
            return pl.BlockSpec(block, (lambda i: (0, blocks - 1 - i)) if backward else (lambda i: (0, i)))
        block = (shape[0] // blocks, shape[1])
        return pl.BlockSpec(block, (lambda i: (blocks - 1 - i, 0)) if backward else (lambda i: (i, 0)))

    return spec


def call(body, blocks, ins, outs, scratch, backward, name, micros):
    spec = block_specs(blocks, backward)
    return pl.pallas_call(
        body,
        grid=(blocks,),
        in_specs=[spec(a.shape, kind) for a, kind in ins],
        out_specs=[spec(shape, kind) for shape, _, kind in outs],
        out_shape=[jax.ShapeDtypeStruct(shape, dtype) for shape, dtype, _ in outs],
        scratch_shapes=scratch,
        compiler_params=pltpu.CompilerParams(
            dimension_semantics=("arbitrary",), vmem_limit_bytes=60 * 1024 * 1024
        ),
        cost_estimate=cost(micros),
        name=name,
    )(*[a for a, _ in ins])


def signal_all(groups):
    barrier = pltpu.get_barrier_semaphore()
    for axis, peers in groups:
        for peer in peers:
            pl.semaphore_signal(barrier, inc=1, device_id={axis: peer}, device_id_type=MESH)
    pl.semaphore_wait(barrier, sum(len(peers) for _, peers in groups))


def push(src, dst, send, recv, axis, peer):
    copy = pltpu.make_async_remote_copy(
        src_ref=src, dst_ref=dst, send_sem=send, recv_sem=recv, device_id={axis: peer},
        device_id_type=MESH,
    )
    copy.start()
    return copy


def span(start, size):
    return pl.ds(pl.multiple_of(start, size), size)


def split_dp(count):
    small = 1
    while 2 * small * 2 * small * 2 <= count:
        small *= 2
    return small, count // small


def hops(count):
    return [count // 2] + [k for k in range(1, count) if k != count // 2]


def mid_step(mixed, hidden, gate_low, cotangent, normal, collective_id, micros):
    length, width = mixed.shape
    inner = gate_low.shape[1]
    nd = lax.axis_size("dp")
    nx, nz = split_dp(nd)
    rows = width // nd
    half = length // 2
    chunk = 256

    def body(mixed_r, hid, low, cot, nor, half_o, buf, near, send, recv):
        me = lax.axis_index("tensor")
        side = lax.rem(me, 2)
        sibling = me + 1 - 2 * side
        signal_all([("tensor", [sibling])])
        copy = push(
            mixed_r.at[span((1 - side) * half, half)], near, send.at[0], recv.at[0], "tensor", sibling
        )
        for c in range(width // chunk):
            cols = slice(c * chunk, (c + 1) * chunk)
            left = t_mm(hid[:, cols], low[...]).astype(BF16)
            right = t_mm(cot[:, cols], nor[...]).astype(BF16)
            for d in range(c * chunk // rows, (c + 1) * chunk // rows):
                at = slice(d * rows - c * chunk, (d + 1) * rows - c * chunk)
                place = slice((d // nx) * rows, (d // nx + 1) * rows)
                buf[d % nx, place, :inner] = left[at]
                buf[d % nx, place, inner:] = right[at]
        copy.wait()
        mine = mixed_r[span(side * half, half), :].astype(F32) + near[...].astype(F32)
        half_o[...] = mine.astype(BF16)

    vm = pl.BlockSpec(memory_space=pltpu.VMEM)
    return pl.pallas_call(
        body,
        in_specs=[vm] * 5,
        out_specs=[vm] * 2,
        out_shape=[
            jax.ShapeDtypeStruct((half, width), BF16),
            jax.ShapeDtypeStruct((nx, nz * rows, 2 * inner), BF16),
        ],
        scratch_shapes=[
            pltpu.VMEM((half, width), BF16),
            pltpu.SemaphoreType.DMA((1,)),
            pltpu.SemaphoreType.DMA((1,)),
        ],
        compiler_params=pltpu.CompilerParams(
            collective_id=collective_id, has_side_effects=True, vmem_limit_bytes=60 * 1024 * 1024
        ),
        cost_estimate=cost(micros),
        name="mid_step",
    )(mixed, hidden, gate_low, cotangent, normal)


def bwd_step(ins, outs, scratch, dw, mixed_half, blocks, collective_id, micros):
    nt, nd = lax.axis_size("tensor"), lax.axis_size("dp")
    chips = nt // 2
    nx, nz = split_dp(nd)
    part, cols = dw.shape[1:]
    rows = part // nz
    order = hops(nz)
    inside = nz - 2
    per = -(-inside // (blocks - 1))

    def body(*refs):
        refs = list(refs)

        def take(n):
            out = refs[:n]
            del refs[:n]
            return out

        plain_in = take(len(ins))
        dw_h, mix_h = take(2)
        plain_out = take(len(outs))
        sum_o, last_o, far_o = take(3)
        plain_scratch = take(len(scratch))
        keep, xslot, zsrc, zslot, loc, m_s, m_r, x_s, x_r, z_s, z_r = refs
        step = pl.program_id(0)
        me, md = lax.axis_index("tensor"), lax.axis_index("dp")
        side, chip = lax.rem(me, 2), me // 2
        x, z = lax.rem(md, nx), md // nx

        def remote(src, dst, send, recv, axis, peer):
            return pltpu.make_async_remote_copy(
                src_ref=src, dst_ref=dst, send_sem=send, recv_sem=recv, device_id={axis: peer},
                device_id_type=MESH,
            )

        def mate(q):
            return 2 * lax.rem(chip + q, chips) + side

        def x_peer(q):
            return z * nx + lax.rem(x + q, nx)

        def z_peer(k):
            return lax.rem(z + k, nz) * nx + x

        def place(p):
            return span(lax.rem(z + (order + [0])[p], nz) * rows, rows)

        def mix_copy(q):
            return remote(mix_h, far_o.at[q - 1], m_s.at[q - 1], m_r.at[q - 1], "tensor", mate(q))

        def x_copy(q, p):
            return remote(
                dw_h.at[lax.rem(x + q, nx), place(p)], xslot.at[q - 1, p], x_s.at[q - 1, p],
                x_r.at[q - 1, p], "dp", x_peer(q),
            )

        def z_copy(p):
            return remote(
                zsrc.at[p], zslot.at[p], z_s.at[p], z_r.at[p], "dp", z_peer(order[p])
            )

        def keep_copy():
            return pltpu.make_async_copy(dw_h.at[x], keep, loc.at[0])

        def gather_piece(p):
            for q in range(1, nx):
                x_copy(q, p).wait_recv()
            total = keep[place(p), :].astype(F32)
            for q in range(1, nx):
                total = total + xslot[q - 1, p].astype(F32)
            return total

        @pl.when(step == 0)
        def _():
            keep_copy().start()
            signal_all([
                ("tensor", [mate(q) for q in range(1, chips)]),
                ("dp", [x_peer(q) for q in range(1, nx)] + [z_peer(k) for k in range(1, nz)]),
            ])
            for p in range(nz):
                for q in range(1, nx):
                    x_copy(q, p).start()
            for q in range(1, chips):
                mix_copy(q).start()

        for s in range(1, blocks):

            @pl.when(step == s)
            def _(s=s):
                if s == 1:
                    keep_copy().wait()
                for p in range((s - 1) * per, min(s * per, inside)):
                    zsrc[p] = gather_piece(p).astype(BF16)
                    z_copy(p).start()

        bwd_kernel(*plain_in, *plain_out, *plain_scratch)

        @pl.when(step == blocks - 1)
        def _():
            last_o[...] = gather_piece(nz - 2).astype(BF16)
            total = gather_piece(nz - 1)
            for p in range(inside):
                z_copy(p).wait_recv()
                total = total + zslot[p].astype(F32)
            sum_o[...] = total
            for q in range(1, chips):
                mix_copy(q).wait()
            for p in range(inside):
                z_copy(p).wait_send()
            for p in range(nz):
                for q in range(1, nx):
                    x_copy(q, p).wait_send()

    spec = block_specs(blocks, True)
    hbm = pl.BlockSpec(memory_space=pl.ANY)
    dma = pltpu.SemaphoreType.DMA
    return pl.pallas_call(
        body,
        grid=(blocks,),
        in_specs=[spec(a.shape, kind) for a, kind in ins] + [hbm, hbm],
        out_specs=[spec(shape, kind) for shape, _, kind in outs] + [spec((rows, cols), "whole")] * 2 + [hbm],
        out_shape=[jax.ShapeDtypeStruct(shape, dtype) for shape, dtype, _ in outs]
        + [
            jax.ShapeDtypeStruct((rows, cols), F32),
            jax.ShapeDtypeStruct((rows, cols), BF16),
            jax.ShapeDtypeStruct((chips - 1,) + mixed_half.shape, BF16),
        ],
        scratch_shapes=scratch
        + [
            pltpu.VMEM((part, cols), BF16),
            pltpu.VMEM((nx - 1, nz, rows, cols), BF16),
            pltpu.VMEM((inside, rows, cols), BF16),
            pltpu.VMEM((inside, rows, cols), BF16),
            dma((1,)), dma((chips - 1,)), dma((chips - 1,)), dma((nx - 1, nz)), dma((nx - 1, nz)),
            dma((inside,)), dma((inside,)),
        ],
        compiler_params=pltpu.CompilerParams(
            dimension_semantics=("arbitrary",), collective_id=collective_id, has_side_effects=True,
            vmem_limit_bytes=60 * 1024 * 1024,
        ),
        cost_estimate=cost(micros),
        name="bwd_scan",
    )(*[a for a, _ in ins], dw, mixed_half)


def finish_kernel(
    heads, result, gtok, gate_out, last, value_step, shared, early, late,
    result_o, gtok_o, dgate_o, dvalue_o, dshared_o, dstep_o, dout_o,
    convv_o, biasv_o, convs_o, biass_o, h0_o, h1_o, h2_o, gain_o, norm_o,
):
    inner = dgate_o.shape[1]
    result_o[...] = result[...]
    gtok_o[...] = gtok[...]

    @pl.when(pl.program_id(0) == 0)
    def _():
        dgate_o[...] = gate_out[:, :inner] + last[:, :inner].astype(F32)
        dout_o[...] = gate_out[:, inner:] + last[:, inner:].astype(F32)
        dvalue_o[...] = value_step[:, :inner]
        dstep_o[...] = jnp.transpose(value_step[:, inner : inner + LANES])[:heads, :]
        dshared_o[...] = shared[...]
        convv_o[...] = early[0:4, :inner]
        biasv_o[...] = early[4:5, :inner]
        gain_o[...] = early[5:6, :inner]
        h0_o[...] = early[0:1, inner : inner + heads]
        h1_o[...] = early[1:2, inner : inner + heads]
        h2_o[...] = early[2:3, inner : inner + heads]
        convs_o[...] = late[0:4, :]
        biass_o[...] = late[4:5, :]
        norm_o[...] = late[5:6, : norm_o.shape[1]]


def tail_step(
    heads_part, dbc_part, hidden, value_low, step_low, shared_conv, shared_pre, aux, tokens, cotangent,
    ng, shared_proj, shp, mixed_half, mixed_far, last, ch_grads, head_grads, gain_part,
    collective_id, micros,
):
    length, width = tokens.shape
    inner = value_low.shape[1]
    shared_width = shared_proj.shape[1]
    nt, nd = lax.axis_size("tensor"), lax.axis_size("dp")
    ng_chips = nt // 2
    nx, nz = split_dp(nd)
    rows = width // nd
    quarter, half = length // nt, length // 2
    piece = quarter // PIECES
    part = nz * rows
    low_width = inner + LANES
    norm_width = width // nt
    early_width = inner + LANES
    late_width = shared_width
    blocks = length // SPAN
    chunk = 256
    path = hops(nz) + [0]
    n_mixed = ng_chips - 1
    n_late = 9 + n_mixed

    def body(*refs):
        refs = list(refs)

        def take(n):
            out = refs[:n]
            del refs[:n]
            return out

        heads_r, dbc, aux_r, ng_r, ws, shp_r, chg, hg, gain = take(9)
        hid_h, vlow_h, slow_h, scv_h, spre_h, tok_h, cot_h, mix_h, mixfar_h, last_h = take(10)
        result_o, gtok_o, value_o, shared_o, early_o, late_o, last_o = take(7)
        hid, low, scv, spre, tokh, tokq, cotq, mix, mixfar = take(9)
        (
            dnear, dslots, dtot, dbuf, shlow, hnear, fsrc, ffar, hacc, vbuf, vslot, sbuf, sslot,
            zv, zvslot, zs, zsslot, eslots, lslots, nbuf, nslot,
        ) = take(21)
        (
            loc, a_s, a_r, d_s, d_r, n_s, n_r, f_s, f_r, g_s, g_r, h_s, h_r, r_s, r_r,
            zv_s, zv_r, zs_s, zs_r, xv_s, xv_r, w_s, w_r, xs_s, xs_r, e_s, e_r, l_s, l_r, m_s, m_r,
        ) = take(31)

        me = lax.axis_index("tensor")
        side, chip = lax.rem(me, 2), me // 2
        sibling = 2 * chip + 1 - side
        md = lax.axis_index("dp")
        x, z = lax.rem(md, nx), md // nx

        def chip_at(q):
            return lax.rem(chip + q, ng_chips)

        def mate(q):
            return 2 * chip_at(q) + side

        def x_peer(q):
            return z * nx + lax.rem(x + q, nx)

        def z_peer(k):
            return lax.rem(z + k, nz) * nx + x

        count = [0]

        def fetch(src, dst):
            copy = pltpu.make_async_copy(src, dst, loc.at[count[0]])
            count[0] += 1
            copy.start()
            return copy

        my_rows = span(me * quarter, quarter)
        my_half = span(side * half, half)
        sib_half = span((1 - side) * half, half)
        got_low = [
            fetch(hid_h, hid), fetch(vlow_h, low.at[:, 0:inner]),
            fetch(slow_h, low.at[:, inner : inner + LANES]),
        ]
        got_mix = [fetch(mix_h, mix), fetch(tok_h.at[my_half], tokh)]
        got_mix += [fetch(mixfar_h.at[q], mixfar.at[q]) for q in range(n_mixed)]
        got_shared = [fetch(scv_h, scv), fetch(spre_h, spre)]
        got_end = [fetch(tok_h.at[my_rows], tokq), fetch(cot_h.at[my_rows], cotq)]

        signal_all([
            ("tensor", [lax.rem(me + k, nt) for k in range(1, nt)]),
            ("dp", [lax.rem(md + k, nd) for k in range(1, nd)]),
        ])
        sent = []

        def send(*args):
            copy = push(*args)
            sent.append(copy)
            return copy

        dn = send(dbc.at[sib_half], dnear, a_s.at[0], a_r.at[0], "tensor", sibling)
        last_copy = send(last_h, last_o, w_s.at[0], w_r.at[0], "dp", z_peer(path[nz - 2]))
        order = list(range(1, ng_chips)) + [0]
        near = {}
        for q in order:
            for p in range(PIECES):
                at = (2 * chip_at(q) + 1 - side) * quarter + p * piece
                near[q, p] = send(
                    heads_r.at[span(at, piece)], hnear.at[q, p], n_s.at[q, p], n_r.at[q, p],
                    "tensor", sibling,
                )
        eslots[md, :, :inner] = jnp.concatenate(
            [chg[0:5, :], gain[0:1, :], jnp.zeros((2, inner), F32)], axis=0
        )
        eslots[md, :, inner:] = hg[...]

        dn.wait_recv()
        dslots[chip] = (dbc[my_half, :] + dnear[...]).astype(BF16)
        dmates = [
            send(dslots.at[chip], dslots.at[chip], d_s.at[q], d_r.at[q], "tensor", mate(q))
            for q in range(1, ng_chips)
        ]
        fwd = {}
        for q in order:
            for p in range(PIECES):
                near[q, p].wait_recv()
                at = (2 * chip_at(q) + side) * quarter + p * piece
                both = heads_r[span(at, piece), :].astype(F32) + hnear[q, p].astype(F32)
                if q:
                    fsrc[q, p] = both.astype(BF16)
                    fwd[q, p] = send(
                        fsrc.at[q, p], ffar.at[q, p], f_s.at[q, p], f_r.at[q, p], "tensor", mate(q)
                    )
                else:
                    hacc[p * piece : (p + 1) * piece, :] = both
        es = [
            send(
                eslots.at[md], eslots.at[md], e_s.at[k], e_r.at[k], "dp", lax.rem(md + k, nd)
            )
            for k in range(1, nd)
        ]

        for copy in got_low:
            copy.wait()
        xvs = {}
        for p in range(nz):
            cols = span(lax.rem(z + path[p], nz) * (nx * rows), nx * rows)
            prod = t_mm(hid[:, cols], low[...]).astype(BF16)
            for k in range(nx):
                vbuf[p, k] = prod[k * rows : (k + 1) * rows]
            for q in range(1, nx):
                xvs[q, p] = send(
                    vbuf.at[p, lax.rem(x + q, nx)], vslot.at[q - 1, p], xv_s.at[q - 1, p],
                    xv_r.at[q - 1, p], "dp", x_peer(q),
                )
        zvs = []

        def own_piece(p):
            total = vbuf[p, x].astype(F32)
            for q in range(1, nx):
                xvs[q, p].wait_recv()
                total = total + vslot[q - 1, p].astype(F32)
            return total

        def pass_on(p):
            zv[p] = own_piece(p).astype(BF16)
            zvs.append(
                send(zv.at[p], zvslot.at[p], zv_s.at[p], zv_r.at[p], "dp", z_peer(path[p]))
            )

        for copy in got_shared:
            copy.wait()
        for copy in dmates:
            copy.wait_recv()
        total = dslots[0].astype(F32)
        for g in range(1, ng_chips):
            total = total + dslots[g].astype(F32)
        dtot[my_half, :] = total
        dt_copy = send(
            dtot.at[my_half], dtot.at[my_half], a_s.at[1], a_r.at[1], "tensor", sibling
        )

        pass_on(0)
        for copy in got_mix:
            copy.wait()
        mixed = mix[...].astype(F32)
        if n_mixed == 1:
            mixed = mixed + mixfar[0].astype(F32)
        else:
            terms = [mix] + [mixfar.at[q] for q in range(n_mixed)]
            mixed = jnp.zeros((half, width), F32)
            for g in range(ng_chips):
                for q in range(ng_chips):
                    mine = (lax.rem(chip - q + ng_chips, ng_chips) == g).astype(F32)
                    mixed = mixed + terms[q][...].astype(F32) * mine
        result_o[my_half, :] = (tokh[...].astype(F32) + mixed).astype(BF16)
        res = send(
            result_o.at[my_half], result_o.at[my_half], r_s.at[0], r_r.at[0], "tensor", sibling
        )

        if nz > 2:
            pass_on(1)
        dt_copy.wait_recv()
        dbuf[length : length + 8, :] = jnp.zeros((8, shared_width), F32)
        sums = [jnp.zeros((1, shared_width), F32)] * 5
        for b in reversed(range(blocks)):
            base = b * SPAN
            at = slice(base, base + SPAN)
            sc = scv[at, :]
            csig = sigmoid(sc)
            dcv = dtot[at, :] * (csig * (1.0 + sc * (1.0 - csig)))
            dbuf[at, :] = dcv
            sp = spre[at, :]
            mask = aux_r[at, :]
            ds = dcv * shp_r[3:4, :]
            sums[3] = sums[3] + jnp.sum(dcv * sp, axis=0, keepdims=True)
            sums[4] = sums[4] + jnp.sum(dcv, axis=0, keepdims=True)
            for j in range(1, 4):
                moved = dbuf[base + j : base + j + SPAN, :] * mask[:, 8 + j : 9 + j]
                ds = ds + moved * shp_r[3 - j : 4 - j, :]
                sums[3 - j] = sums[3 - j] + jnp.sum(moved * sp, axis=0, keepdims=True)
            shlow[at, :] = ds.astype(BF16)
        for p in range(2, nz - 1):
            pass_on(p)
        for c in range(width // chunk):
            prod = t_mm(hid[:, c * chunk : (c + 1) * chunk], shlow[...]).astype(BF16)
            for d in range(c * chunk // rows, (c + 1) * chunk // rows):
                at = slice(d * rows - c * chunk, (d + 1) * rows - c * chunk)
                sbuf[d % nx, (d // nx) * rows : (d // nx + 1) * rows, :] = prod[at]
        xss = [
            send(
                sbuf.at[lax.rem(x + q, nx)], sslot.at[q], xs_s.at[q], xs_r.at[q], "dp", x_peer(q)
            )
            for q in range(1, nx)
        ]
        hacc[...] = hacc[...] + mm_t(shlow[my_rows, :], ws[...])

        for copy in got_end:
            copy.wait()
        norm = jnp.zeros((1, width), F32)
        gather, own = {}, []
        for p in range(PIECES):
            at = slice(p * piece, (p + 1) * piece)
            grad_hidden = hacc[at, :]
            for q in range(1, ng_chips):
                fwd[q, p].wait_recv()
                grad_hidden = grad_hidden + ffar[q, p].astype(F32)
            v = tokq[at, :].astype(F32)
            inv = lax.rsqrt(jnp.mean(v * v, axis=1, keepdims=True) + EPSILON)
            normed = v * inv
            scaled = grad_hidden * ng_r[...]
            norm = norm + jnp.sum(grad_hidden * normed, axis=0, keepdims=True)
            mean = jnp.mean(scaled * normed, axis=1, keepdims=True)
            place = span(me * quarter + p * piece, piece)
            gtok_o[place, :] = (inv * (scaled - normed * mean) + cotq[at, :].astype(F32)).astype(BF16)
            for q in range(1, ng_chips):
                gather[q, p] = send(
                    gtok_o.at[place], gtok_o.at[place], g_s.at[q, p], g_r.at[q, p], "tensor", mate(q)
                )
            own.append(
                send(gtok_o.at[place], gtok_o.at[place], h_s.at[0, p], h_r.at[0, p], "tensor", sibling)
            )
        for q in range(nt):
            nbuf[q] = norm[:, q * norm_width : (q + 1) * norm_width] + jnp.zeros((8, norm_width), F32)
        norms = [
            send(
                nbuf.at[lax.rem(me + k, nt)], nslot.at[k], m_s.at[k], m_r.at[k], "tensor",
                lax.rem(me + k, nt),
            )
            for k in range(1, nt)
        ]

        for copy in xss:
            copy.wait_recv()
        total = sbuf[x].astype(F32)
        for q in range(1, nx):
            total = total + sslot[q].astype(F32)
        zs[...] = total.astype(BF16)
        zss = [
            send(
                zs.at[span(lax.rem(z + k, nz) * rows, rows)], zsslot.at[k], zs_s.at[k], zs_r.at[k],
                "dp", z_peer(k),
            )
            for k in range(1, nz)
        ]

        for copy in norms:
            copy.wait_recv()
        total = nbuf[me]
        for k in range(1, nt):
            total = total + nslot[k]
        wide = jnp.concatenate(
            [total[0:1, :], jnp.zeros((1, shared_width - norm_width), F32)], axis=1
        ) if norm_width < shared_width else total[0:1, :]
        lslots[md] = jnp.concatenate(sums + [wide, jnp.zeros((2, shared_width), F32)], axis=0)
        ls = [
            send(
                lslots.at[md], lslots.at[md], l_s.at[k], l_r.at[k], "dp", lax.rem(md + k, nd)
            )
            for k in range(1, nd)
        ]

        for copy in es:
            copy.wait_recv()
        total = eslots[0]
        for s in range(1, nd):
            total = total + eslots[s]
        early_o[...] = total

        for p in range(PIECES):
            for q in range(1, ng_chips):
                gather[q, p].wait_recv()
                came = 2 * lax.rem(chip - q + ng_chips, ng_chips) + side
                place = span(came * quarter + p * piece, piece)
                own.append(
                    send(
                        gtok_o.at[place], gtok_o.at[place], h_s.at[q, p], h_r.at[q, p],
                        "tensor", sibling,
                    )
                )

        for copy in zvs:
            copy.wait_recv()
        total = own_piece(nz - 1)
        for p in range(nz - 1):
            total = total + zvslot[p].astype(F32)
        value_o[...] = total
        for copy in zss:
            copy.wait_recv()
        total = zs[span(z * rows, rows), :].astype(F32)
        for k in range(1, nz):
            total = total + zsslot[k].astype(F32)
        shared_o[...] = total

        for copy in ls:
            copy.wait_recv()
        total = lslots[0]
        for s in range(1, nd):
            total = total + lslots[s]
        late_o[...] = total

        res.wait_recv()
        last_copy.wait_recv()
        for copy in own:
            copy.wait_recv()
        for copy in sent:
            copy.wait_send()

    vm = pl.BlockSpec(memory_space=pltpu.VMEM)
    hbm = pl.BlockSpec(memory_space=pl.ANY)
    dma = pltpu.SemaphoreType.DMA

    def f32(*shape):
        return pltpu.VMEM(shape, F32)

    def bf16(*shape):
        return pltpu.VMEM(shape, BF16)

    def out(*shape):
        return jax.ShapeDtypeStruct(shape, F32)

    early = [heads_part, dbc_part, aux, ng, shared_proj, shp, ch_grads, head_grads, gain_part]
    late = [hidden, value_low, step_low, shared_conv, shared_pre, tokens, cotangent, mixed_half]
    late += [mixed_far, last]
    return pl.pallas_call(
        body,
        in_specs=[vm] * len(early) + [hbm] * len(late),
        out_specs=[vm] * 6 + [hbm],
        out_shape=[
            jax.ShapeDtypeStruct((length, width), BF16), jax.ShapeDtypeStruct((length, width), BF16),
            out(rows, low_width), out(rows, shared_width), out(8, early_width), out(8, late_width),
            jax.ShapeDtypeStruct(last.shape, last.dtype),
        ],
        scratch_shapes=[
            bf16(length, width), bf16(length, low_width), f32(length, shared_width),
            f32(length, shared_width), bf16(half, width), bf16(quarter, width), bf16(quarter, width),
            bf16(half, width), bf16(n_mixed, half, width),
            f32(half, shared_width), bf16(ng_chips, half, shared_width), f32(length, shared_width),
            f32(length + 8, shared_width), bf16(length, shared_width),
            bf16(ng_chips, PIECES, piece, width), bf16(ng_chips, PIECES, piece, width),
            bf16(ng_chips, PIECES, piece, width), f32(quarter, width),
            bf16(nz, nx, rows, low_width), bf16(nx - 1, nz, rows, low_width),
            bf16(nx, part, shared_width), bf16(nx, part, shared_width),
            bf16(nz - 1, rows, low_width), bf16(nz - 1, rows, low_width),
            bf16(part, shared_width), bf16(nz, rows, shared_width),
            f32(nd, 8, early_width), f32(nd, 8, late_width),
            f32(nt, 8, norm_width), f32(nt, 8, norm_width),
        ]
        + [dma((n_late + 1,)), dma((2,)), dma((2,)), dma((ng_chips,)), dma((ng_chips,))]
        + [dma((ng_chips, PIECES))] * 8
        + [dma((1,)), dma((1,))]
        + [dma((nz,))] * 4
        + [dma((nx - 1, nz))] * 2
        + [dma((1,))] * 2
        + [dma((nx,))] * 2
        + [dma((nd,))] * 4
        + [dma((nt,))] * 2,
        compiler_params=pltpu.CompilerParams(
            collective_id=collective_id, has_side_effects=True, vmem_limit_bytes=60 * 1024 * 1024
        ),
        cost_estimate=cost(micros),
        name="tail_step",
    )(*early, *late)


def per_device(
    tokens, cotangent, segments, norm_gain, gate_proj, value_proj, shared_proj, step_proj,
    conv_value, bias_value, conv_shared, bias_shared, step_bias, decay_log, skip_gain,
    gate_gain, out_proj,
):
    tp_count = lax.axis_size("tensor")
    dp_count = lax.axis_size("dp")
    length, width = tokens.shape
    inner = gate_proj.shape[1]
    heads = step_proj.shape[1]
    shared_width = shared_proj.shape[1]
    state_size = shared_width // 2
    blocks = length // SPAN
    aux, segr, wst, chp, shp, hp = pl.pallas_call(
        prep_kernel,
        out_shape=[
            jax.ShapeDtypeStruct((length, LANES), F32),
            jax.ShapeDtypeStruct((1, length), F32),
            jax.ShapeDtypeStruct((width, LANES), BF16),
            jax.ShapeDtypeStruct((8, inner), F32),
            jax.ShapeDtypeStruct((8, shared_width), F32),
            jax.ShapeDtypeStruct((8, LANES), F32),
        ],
        name="prep_step",
    )(
        segments, step_proj.T, conv_value, bias_value[None], gate_gain[None], skip_gain[None],
        conv_shared, bias_shared[None], step_bias[None], decay_log[None],
    )
    ng = norm_gain[None, :]

    (
        hidden, gate_pre, value_pre, conv_out, shared_pre, shared_conv, z, ld, ldt, yn, sin, gn, stat,
    ) = call(
        fwd_kernel,
        blocks,
        [
            (tokens, "rows"), (cotangent, "rows"), (aux, "rows"), (segr, "lanes"), (ng, "whole"),
            (gate_proj, "whole"), (value_proj, "whole"), (shared_proj, "whole"), (wst, "whole"),
            (out_proj, "whole"), (chp, "whole"), (shp, "whole"), (hp, "whole"),
        ],
        [
            ((length, width), BF16, "rows"),
            ((length, inner), F32, "rows"),
            ((length, inner), F32, "rows"),
            ((length, inner), F32, "rows"),
            ((length, shared_width), F32, "rows"),
            ((length, shared_width), F32, "rows"),
            ((length, LANES), F32, "rows"),
            ((length, LANES), F32, "rows"),
            ((8, length), F32, "lanes"),
            ((length, inner), F32, "rows"),
            ((blocks * state_size, inner), F32, "rows"),
            ((length, inner), F32, "rows"),
            ((8, length), F32, "lanes"),
        ],
        [
            pltpu.VMEM((SPAN + 8, inner), F32),
            pltpu.VMEM((SPAN + 8, shared_width), F32),
            pltpu.VMEM((state_size, inner), F32),
        ],
        False,
        "fwd_scan",
        20,
    )
    stat = small_sum(stat, "tensor", 0)
    total_inner = float(inner * tp_count)

    def gate_body(*refs):
        gate_kernel(total_inner, *refs)

    normal_out, dy, gate_low, gain_part, mixed_part = call(
        gate_body,
        blocks,
        [
            (gate_pre, "rows"), (conv_out, "rows"), (yn, "rows"), (gn, "rows"), (stat, "lanes"),
            (chp, "whole"), (out_proj, "whole"),
        ],
        [
            ((length, inner), BF16, "rows"),
            ((length, inner), F32, "rows"),
            ((length, inner), BF16, "rows"),
            ((8, inner), F32, "whole"),
            ((length, width), BF16, "rows"),
        ],
        [],
        False,
        "gate_step",
        9,
    )
    mixed_half, dw = mid_step(mixed_part, hidden, gate_low, cotangent, normal_out, 1, 6)
    value_low, step_low, heads_part, dbc_part, ch_grads, head_grads, gate_out, last, mixed_far = bwd_step(
        [
            (dy, "rows"), (conv_out, "rows"), (value_pre, "rows"), (shared_conv, "rows"),
            (z, "rows"), (ld, "rows"), (ldt, "lanes"), (yn, "rows"), (sin, "rows"),
            (aux, "rows"), (segr, "lanes"), (gate_low, "rows"), (gate_proj, "whole"),
            (value_proj, "whole"), (wst, "whole"), (chp, "whole"), (hp, "whole"),
        ],
        [
            ((length, inner), BF16, "rows"),
            ((length, LANES), BF16, "rows"),
            ((length, width), BF16, "rows"),
            ((length, shared_width), F32, "rows"),
            ((8, inner), F32, "whole"),
            ((8, LANES), F32, "whole"),
        ],
        [pltpu.VMEM((SPAN + 8, inner), F32), pltpu.VMEM((state_size, inner), F32)],
        dw, mixed_half, blocks, 3, 27,
    )
    result, grad_tokens, value_step, shared_sum, early, late, last = tail_step(
        heads_part, dbc_part, hidden, value_low, step_low, shared_conv, shared_pre, aux, tokens,
        cotangent, ng, shared_proj, shp, mixed_half, mixed_far, last, ch_grads, head_grads,
        gain_part, 2, 40,
    )

    def finish_body(*refs):
        finish_kernel(heads, *refs)

    rows = width // dp_count
    (
        result, grad_tokens, dgate, dvalue, dshared, dstep, dout,
        convv, biasv, convs, biass, h0, h1, h2, gain, norm,
    ) = call(
        finish_body,
        blocks,
        [
            (result, "rows"), (grad_tokens, "rows"), (gate_out, "whole"), (last, "whole"),
            (value_step, "whole"),
            (shared_sum, "whole"), (early, "whole"), (late, "whole"),
        ],
        [
            ((length, width), BF16, "rows"), ((length, width), BF16, "rows"),
            ((rows, inner), F32, "whole"), ((rows, inner), F32, "whole"),
            ((rows, shared_width), F32, "whole"), ((heads, rows), F32, "whole"),
            ((rows, inner), F32, "whole"), ((4, inner), F32, "whole"), ((1, inner), F32, "whole"),
            ((4, shared_width), F32, "whole"), ((1, shared_width), F32, "whole"),
            ((1, heads), F32, "whole"), ((1, heads), F32, "whole"), ((1, heads), F32, "whole"),
            ((1, inner), F32, "whole"), ((1, width // tp_count), F32, "whole"),
        ],
        [],
        False,
        "finish_step",
        3,
    )
    return (
        result, grad_tokens, norm[0], dgate, dvalue, dshared, dstep.T, convv, biasv[0], convs, biass[0],
        h0[0], h1[0], h2[0], gain[0], dout,
    )


def solution(mesh):
    rows, cols, vec = P("dp", None), P(None, "tensor"), P("tensor")
    return jax.shard_map(
        per_device,
        mesh=mesh,
        in_specs=(
            rows, rows, rows, P(), cols, cols, P(), cols, cols, vec, P(), P(), vec, vec, vec, vec, cols,
        ),
        out_specs=(
            rows, rows, vec, P("dp", "tensor"), P("dp", "tensor"), rows, P("dp", "tensor"), cols, vec,
            P(), P(), vec, vec, vec, vec, P("dp", "tensor"),
        ),
        check_vma=False,
    )
```

```python
import jax
import jax.numpy as jnp
from jax import lax
from jax.experimental import pallas as pl
from jax.experimental.pallas import tpu as pltpu
from jax.sharding import PartitionSpec as P

SPAN = 256
HSIZE = 64
LANES = 128
EPSILON = 1e-05
NEG_FILL = -1e30
EXACT = lax.Precision.HIGHEST
F32 = jnp.float32
BF16 = jnp.bfloat16


def mm(left, right):
    return jnp.dot(left, right, preferred_element_type=F32)


def mm_t(left, right):
    return lax.dot_general(left, right, (((1,), (1,)), ((), ())), preferred_element_type=F32)


def t_mm(left, right):
    return lax.dot_general(left, right, (((0,), (0,)), ((), ())), preferred_element_type=F32)


def exact(left, right):
    return jnp.dot(left, right, precision=EXACT, preferred_element_type=F32)


def sigmoid(v):
    return 1.0 / (1.0 + jnp.exp(-v))


def spread(cols, pairs):
    low = lax.broadcasted_iota(jnp.int32, (cols.shape[0], LANES), 1) < HSIZE
    parts = [
        jnp.where(low, cols[:, 2 * p : 2 * p + 1], cols[:, 2 * p + 1 : 2 * p + 2])
        for p in range(pairs)
    ]
    return jnp.concatenate(parts, axis=1)


def gather_mat(inner):
    channel = lax.broadcasted_iota(jnp.int32, (inner, LANES), 0) // HSIZE
    head = lax.broadcasted_iota(jnp.int32, (inner, LANES), 1)
    return (channel == head).astype(F32)


def grid_masks():
    row = lax.broadcasted_iota(jnp.int32, (SPAN, SPAN), 0)
    col = lax.broadcasted_iota(jnp.int32, (SPAN, SPAN), 1)
    return row, col


def conv_fwd(buf, pack, aux):
    out = pack[4:5, :] + buf[8 : 8 + SPAN, :] * pack[3:4, :]
    for j in range(1, 4):
        out = out + buf[8 - j : 8 - j + SPAN, :] * (aux[:, j : j + 1] * pack[3 - j : 4 - j, :])
    return out


def fwd_kernel(
    tok, cot, aux_ref, segr, ng, wg, wv, ws, wst, wo, chp, shp, hp,
    hidden_o, gate_o, vpre_o, cv_o, spre_o, scv_o, z_o, ld_o, ldt_o, yn_o, sin_o, gn_o, stat_o,
    vbuf, sbuf, state,
):
    inner = wg.shape[1]
    pairs = inner // LANES
    state_size = ws.shape[1] // 2

    @pl.when(pl.program_id(0) == 0)
    def _():
        vbuf[0:8, :] = jnp.zeros((8, inner), F32)
        sbuf[0:8, :] = jnp.zeros((8, 2 * state_size), F32)
        state[...] = jnp.zeros_like(state)

    aux = aux_ref[...]
    x = tok[...].astype(F32)
    inv = lax.rsqrt(jnp.mean(x * x, axis=1, keepdims=True) + EPSILON)
    hid = (x * inv * ng[...]).astype(BF16)
    hidden_o[...] = hid
    gate = mm(hid, wg[...])
    gate_o[...] = gate
    vp = mm(hid, wv[...])
    vpre_o[...] = vp
    vbuf[8 : 8 + SPAN, :] = vp
    sp = mm(hid, ws[...])
    spre_o[...] = sp
    sbuf[8 : 8 + SPAN, :] = sp
    z = mm(hid, wst[...]) + hp[0:1, :]
    z_o[...] = z
    gn = mm(cot[...], wo[...])
    gn_o[...] = gn
    scv = conv_fwd(sbuf, shp, aux)
    scv_o[...] = scv
    bc = (scv * sigmoid(scv)).astype(BF16)
    b_low, c_low = bc[:, :state_size], bc[:, state_size:]
    cv = conv_fwd(vbuf, chp, aux)
    cv_o[...] = cv
    vbuf[0:8, :] = vbuf[SPAN : SPAN + 8, :]
    sbuf[0:8, :] = sbuf[SPAN : SPAN + 8, :]
    values = cv * sigmoid(cv)
    dt = jnp.maximum(z, 0.0) + jnp.log1p(jnp.exp(-jnp.abs(z)))
    row, col = grid_masks()
    tri = (row >= col).astype(F32)
    ld = exact(tri, dt * hp[1:2, :])
    ld_o[...] = ld
    ldt = jnp.transpose(ld)[0:8, :]
    ldt_o[...] = ldt
    allowed = (row >= col) & (aux[:, 0:1] == segr[...])
    scores = jnp.where(allowed, mm_t(c_low, b_low), 0.0)
    xs = values * spread(dt, pairs)
    xs_low = xs.astype(BF16)
    ein = jnp.exp(ld) * aux[:, 4:5]
    eout = jnp.exp(ld[SPAN - 1 : SPAN, :] - ld) * aux[:, 5:6]
    ein_x = spread(ein, pairs)
    eout_x = spread(eout, pairs)
    old = state[...]
    sin_o[...] = old
    carried = mm(c_low, old.astype(BF16)) * ein_x
    state[...] = old * ein_x[SPAN - 1 : SPAN, :] + t_mm(b_low, (xs * eout_x).astype(BF16))
    low = lax.broadcasted_iota(jnp.int32, (SPAN, LANES), 1) < HSIZE
    parts = []
    for p in range(pairs):
        pair = xs_low[:, p * LANES : (p + 1) * LANES]
        outs = []
        for h in (2 * p, 2 * p + 1):
            gap = jnp.minimum(ld[:, h : h + 1] - ldt[h : h + 1, :], 0.0)
            outs.append(mm((jnp.exp(gap) * scores).astype(BF16), pair))
        parts.append(jnp.where(low, outs[0], outs[1]))
    yn = jnp.concatenate(parts, axis=1) + carried
    yn_o[...] = yn
    gated = (yn + chp[6:7, :] * values) * (gate * sigmoid(gate))
    squares = jnp.sum(gated * gated, axis=1, keepdims=True)
    dots = jnp.sum(gn * chp[5:6, :] * gated, axis=1, keepdims=True)
    lane = lax.broadcasted_iota(jnp.int32, (SPAN, LANES), 1)
    both = jnp.where(lane == 0, squares, jnp.where(lane == 1, dots, 0.0))
    stat_o[...] = jnp.transpose(both)[0:8, :]


def gate_kernel(
    width, gate_ref, cv_ref, yn, gn_ref, stat, chp, wo, normal_o, dy_o, low_o, gain_o, mixed_o
):
    both = jnp.transpose(jnp.concatenate([stat[...]] * (LANES // 8), axis=0))
    inv = lax.rsqrt(both[:, 0:1] / width + EPSILON)
    mean_dots = both[:, 1:2] / width
    gate = gate_ref[...]
    cv = cv_ref[...]
    gn = gn_ref[...]
    sig = sigmoid(gate)
    act = gate * sig
    mixer = yn[...] + chp[6:7, :] * (cv * sigmoid(cv))
    gated = mixer * act
    normed = gated * inv
    normal = (normed * chp[5:6, :]).astype(BF16)
    normal_o[...] = normal
    mixed_o[...] = mm_t(normal, wo[...]).astype(BF16)
    part = jnp.sum(gn * normed, axis=0, keepdims=True)

    @pl.when(pl.program_id(0) == 0)
    def _():
        gain_o[...] = jnp.zeros_like(gain_o)

    gain_o[0:1, :] += part
    grad_gated = inv * (gn * chp[5:6, :]) - gated * (inv * inv * inv) * mean_dots
    dy_o[...] = grad_gated * act
    low_o[...] = (grad_gated * mixer * (sig * (1.0 + gate * (1.0 - sig)))).astype(BF16)


def bwd_kernel(
    dy_ref, cv_ref, vpre, scv_ref, z_ref, ld_ref, ldt_ref, yn, sin, aux_ref, segr, glow,
    wg, wv, wst, chp, hp,
    vlow_o, slow_o, heads_o, dbc_o, chg_o, hg_o,
    dbuf, dstate,
):
    inner = wg.shape[1]
    pairs = inner // LANES
    state_size = sin.shape[0]

    @pl.when(pl.program_id(0) == 0)
    def _():
        dbuf[SPAN : SPAN + 8, :] = jnp.zeros((8, inner), F32)
        dstate[...] = jnp.zeros_like(dstate)
        chg_o[...] = jnp.zeros_like(chg_o)
        hg_o[...] = jnp.zeros_like(hg_o)

    aux = aux_ref[...]
    dy = dy_ref[...]
    dy_low = dy.astype(BF16)
    scv = scv_ref[...]
    bc = (scv * sigmoid(scv)).astype(BF16)
    b_low, c_low = bc[:, :state_size], bc[:, state_size:]
    cv = cv_ref[...]
    csig = sigmoid(cv)
    values = cv * csig
    z = z_ref[...]
    dt = jnp.maximum(z, 0.0) + jnp.log1p(jnp.exp(-jnp.abs(z)))
    ld = ld_ref[...]
    ldt = ldt_ref[...]
    dt_x = spread(dt, pairs)
    xs = values * dt_x
    xs_low = xs.astype(BF16)
    ein = jnp.exp(ld) * aux[:, 4:5]
    eout = jnp.exp(ld[SPAN - 1 : SPAN, :] - ld) * aux[:, 5:6]
    ein_x = spread(ein, pairs)
    eout_x = spread(eout, pairs)
    row, col = grid_masks()
    allowed = (col >= row) & (aux[:, 0:1] == segr[...])
    mask = allowed.astype(F32)
    scores_t = mm_t(b_low, c_low) * mask
    low = lax.broadcasted_iota(jnp.int32, (SPAN, LANES), 1) < HSIZE
    parts = []
    dscores_t = jnp.zeros((SPAN, SPAN), F32)
    for p in range(pairs):
        cols = slice(p * LANES, (p + 1) * LANES)
        dy_pair = dy_low[:, cols]
        xs_pair = xs_low[:, cols]
        zero = jnp.zeros_like(xs_pair)
        outs = []
        for side, h in enumerate((2 * p, 2 * p + 1)):
            gap = jnp.minimum(ldt[h : h + 1, :] - ld[:, h : h + 1], 0.0)
            decay = jnp.exp(gap)
            outs.append(mm((decay * scores_t).astype(BF16), dy_pair))
            mine = jnp.where(low, xs_pair, zero) if side == 0 else jnp.where(low, zero, xs_pair)
            dscores_t = dscores_t + mm_t(mine, dy_pair) * decay
        parts.append(jnp.where(low, outs[0], outs[1]))
    inside = jnp.concatenate(parts, axis=1)
    dscores_low = (dscores_t * mask).astype(BF16)
    old = sin[...]
    dst = dstate[...]
    dst_low = dst.astype(BF16)
    dye_low = (dy * ein_x).astype(BF16)
    xse_low = (xs * eout_x).astype(BF16)
    db = mm(dscores_low, c_low) + mm_t(xse_low, dst_low)
    dc = t_mm(dscores_low, b_low) + mm_t(dye_low, old.astype(BF16))
    late = mm(b_low, dst_low) * eout_x
    keep = ein_x[SPAN - 1 : SPAN, :]
    dstate[...] = dst * keep + t_mm(c_low, dye_low)
    dxs = inside + late
    collect = gather_mat(inner)
    q = dy_low.astype(F32) * yn[...] - xs_low.astype(F32) * inside
    u = xs * late
    kappa = exact(jnp.sum(old * dst, axis=0, keepdims=True) * keep + jnp.zeros((8, inner), F32), collect)
    da = (
        exact((col >= row).astype(F32), exact(q, collect))
        + exact((row > col).astype(F32), exact(u, collect))
        + kappa[0:1, :]
    )
    rates = hp[1:2, :]
    ddt = da * rates + exact(dxs * values, collect)
    dz = ddt * sigmoid(z)
    slow = dz.astype(BF16)
    slow_o[...] = slow
    skip = exact(jnp.sum(dy * values, axis=0, keepdims=True) + jnp.zeros((8, inner), F32), collect)
    hg_o[0:1, :] += jnp.sum(dz, axis=0, keepdims=True)
    hg_o[1:2, :] += jnp.sum(da * dt, axis=0, keepdims=True) * rates
    hg_o[2:3, :] += skip[0:1, :]
    dcv = (dxs * dt_x + chp[6:7, :] * dy) * (csig * (1.0 + cv * (1.0 - csig)))
    dbuf[0:SPAN, :] = dcv
    vp = vpre[...]
    dv = dcv * chp[3:4, :]
    chg_o[3:4, :] += jnp.sum(dcv * vp, axis=0, keepdims=True)
    chg_o[4:5, :] += jnp.sum(dcv, axis=0, keepdims=True)
    for j in range(1, 4):
        moved = dbuf[j : j + SPAN, :] * aux[:, 8 + j : 9 + j]
        dv = dv + moved * chp[3 - j : 4 - j, :]
        chg_o[3 - j : 4 - j, :] += jnp.sum(moved * vp, axis=0, keepdims=True)
    dbuf[SPAN : SPAN + 8, :] = dbuf[0:8, :]
    vlow = dv.astype(BF16)
    vlow_o[...] = vlow
    back = mm_t(glow[...], wg[...]) + mm_t(vlow, wv[...]) + mm_t(slow, wst[...])
    heads_o[...] = back.astype(BF16)
    dbc_o[...] = jnp.concatenate([db, dc], axis=1)


MESH = pl.DeviceIdType.MESH
PIECES = 4


def prep_kernel(
    seg, stepw, conv_v, bias_v, gate_g, skip_g, conv_s, bias_s, step_b, decay,
    aux_o, segr_o, wst_o, chp_o, shp_o, hp_o,
):
    length = seg.shape[1]
    ids = seg[...].astype(F32)
    segr_o[...] = ids
    wide = ids + jnp.zeros((8, length), F32)
    lane = lax.broadcasted_iota(jnp.int32, (8, length), 1)
    row = lax.broadcasted_iota(jnp.int32, (8, length), 0)
    ends = [
        ids[:, start + SPAN - 1 : start + SPAN] + jnp.zeros((8, SPAN), F32)
        for start in range(0, length, SPAN)
    ]
    last = jnp.concatenate(ends, axis=1)
    before = jnp.concatenate([jnp.full((8, SPAN), -1.0, F32)] + ends[:-1], axis=1)
    first = jnp.where(row == 0, wide, 0.0)
    first = jnp.where((row == 4) & (wide == before), 1.0, first)
    first = jnp.where((row == 5) & (wide == last), 1.0, first)
    second = jnp.zeros((8, length), F32)
    for j in range(1, 4):
        back = (pltpu.roll(wide, j, 1) == wide) & (lane >= j)
        ahead = (pltpu.roll(wide, length - j, 1) == wide) & (lane < length - j)
        first = jnp.where((row == j) & back, 1.0, first)
        second = jnp.where((row == j) & ahead, 1.0, second)
    rest = jnp.zeros((LANES - 16, length), F32)
    aux_o[...] = jnp.transpose(jnp.concatenate([first, second, rest], axis=0))
    heads, width = stepw.shape
    steps = jnp.concatenate([stepw[...].astype(F32), jnp.zeros((LANES - heads, width), F32)], axis=0)
    wst_o[...] = jnp.transpose(steps).astype(BF16)
    hp_o[...] = jnp.zeros_like(hp_o)
    hp_o[0:1, 0:heads] = step_b[...]
    hp_o[1:2, 0:heads] = -jnp.exp(decay[...])
    hp_o[2:3, 0:heads] = skip_g[...]
    inner = chp_o.shape[1]
    repeated = lax.dot_general(
        hp_o[...], gather_mat(inner), (((1,), (1,)), ((), ())), precision=EXACT,
        preferred_element_type=F32,
    )
    chp_o[0:4, :] = conv_v[...]
    chp_o[4:5, :] = bias_v[...]
    chp_o[5:6, :] = gate_g[...]
    chp_o[6:7, :] = repeated[2:3, :]
    chp_o[7:8, :] = jnp.zeros((1, inner), F32)
    shp_o[...] = jnp.zeros_like(shp_o)
    shp_o[0:4, :] = conv_s[...]
    shp_o[4:5, :] = bias_s[...]


def small_sum(x, axis, collective_id):
    count = lax.axis_size(axis)

    def body(x_ref, out_ref, slots, send, recv):
        me = lax.axis_index(axis)
        barrier = pltpu.get_barrier_semaphore()
        for k in range(1, count):
            peer = lax.rem(me + k, count)
            pl.semaphore_signal(barrier, inc=1, device_id={axis: peer}, device_id_type=MESH)
        pl.semaphore_wait(barrier, count - 1)
        copies = []
        for k in range(1, count):
            copies.append(
                pltpu.make_async_remote_copy(
                    src_ref=x_ref,
                    dst_ref=slots.at[k],
                    send_sem=send.at[k],
                    recv_sem=recv.at[k],
                    device_id={axis: lax.rem(me + k, count)},
                    device_id_type=MESH,
                )
            )
            copies[-1].start()
        slots[0] = x_ref[...]
        for copy in copies:
            copy.wait()
        total = slots[me]
        for source in range(1, count):
            total = total + slots[lax.rem(me - source + count, count)]
        out_ref[...] = total

    return pl.pallas_call(
        body,
        in_specs=[pl.BlockSpec(memory_space=pltpu.VMEM)],
        out_specs=pl.BlockSpec(memory_space=pltpu.VMEM),
        out_shape=jax.ShapeDtypeStruct(x.shape, x.dtype),
        scratch_shapes=[
            pltpu.VMEM((count,) + x.shape, x.dtype),
            pltpu.SemaphoreType.DMA((count,)),
            pltpu.SemaphoreType.DMA((count,)),
        ],
        compiler_params=pltpu.CompilerParams(collective_id=collective_id, has_side_effects=True),
        name="small_sum_" + axis,
    )(x)


def cost(micros):
    return pl.CostEstimate(
        flops=int(micros * 1e9), bytes_accessed=int(micros * 3.6e6), transcendentals=0
    )


def block_specs(blocks, backward):
    def spec(shape, kind):
        if kind == "whole":
            return pl.BlockSpec(shape, lambda i: (0,) * len(shape))
        if kind == "lanes":
            block = (shape[0], shape[1] // blocks)
            return pl.BlockSpec(block, (lambda i: (0, blocks - 1 - i)) if backward else (lambda i: (0, i)))
        block = (shape[0] // blocks, shape[1])
        return pl.BlockSpec(block, (lambda i: (blocks - 1 - i, 0)) if backward else (lambda i: (i, 0)))

    return spec


def call(body, blocks, ins, outs, scratch, backward, name, micros):
    spec = block_specs(blocks, backward)
    return pl.pallas_call(
        body,
        grid=(blocks,),
        in_specs=[spec(a.shape, kind) for a, kind in ins],
        out_specs=[spec(shape, kind) for shape, _, kind in outs],
        out_shape=[jax.ShapeDtypeStruct(shape, dtype) for shape, dtype, _ in outs],
        scratch_shapes=scratch,
        compiler_params=pltpu.CompilerParams(
            dimension_semantics=("arbitrary",), vmem_limit_bytes=60 * 1024 * 1024
        ),
        cost_estimate=cost(micros),
        name=name,
    )(*[a for a, _ in ins])


def signal_all(groups):
    barrier = pltpu.get_barrier_semaphore()
    for axis, peers in groups:
        for peer in peers:
            pl.semaphore_signal(barrier, inc=1, device_id={axis: peer}, device_id_type=MESH)
    pl.semaphore_wait(barrier, sum(len(peers) for _, peers in groups))


def push(src, dst, send, recv, axis, peer):
    copy = pltpu.make_async_remote_copy(
        src_ref=src, dst_ref=dst, send_sem=send, recv_sem=recv, device_id={axis: peer},
        device_id_type=MESH,
    )
    copy.start()
    return copy


def span(start, size):
    return pl.ds(pl.multiple_of(start, size), size)


def split_dp(count):
    small = 1
    while 2 * small * 2 * small * 2 <= count:
        small *= 2
    return small, count // small


def hops(count):
    return [count // 2] + [k for k in range(1, count) if k != count // 2]


def bwd_step(
    ins, outs, scratch, mixed, hidden, gate_low, cotangent, normal, blocks, collective_id, micros
):
    nt, nd = lax.axis_size("tensor"), lax.axis_size("dp")
    chips = nt // 2
    nx, nz = split_dp(nd)
    length, width = mixed.shape
    inner = gate_low.shape[1]
    half = length // 2
    rows, cols = width // nd, 2 * inner
    order = hops(nz)
    inside = nz - 2
    per = -(-inside // (blocks - 1))

    def body(*refs):
        refs = list(refs)

        def take(n):
            out = refs[:n]
            del refs[:n]
            return out

        plain_in = take(len(ins))
        mixed_h, hid_h, low_h, cot_h, nor_h = take(5)
        plain_out = take(len(outs))
        sum_o, last_o, half_o, far_o = take(4)
        plain_scratch = take(len(scratch))
        mine, near, mix, hid, low, cot, nor, dw, xslot, zsrc, zslot = take(11)
        loc, n_s, n_r, m_s, m_r, x_s, x_r, z_s, z_r = refs
        step = pl.program_id(0)
        me, md = lax.axis_index("tensor"), lax.axis_index("dp")
        side, chip = lax.rem(me, 2), me // 2
        x, z = lax.rem(md, nx), md // nx

        def remote(src, dst, send, recv, axis, peer):
            return pltpu.make_async_remote_copy(
                src_ref=src, dst_ref=dst, send_sem=send, recv_sem=recv, device_id={axis: peer},
                device_id_type=MESH,
            )

        def mate(q):
            return 2 * lax.rem(chip + q, chips) + side

        def x_peer(q):
            return z * nx + lax.rem(x + q, nx)

        def z_peer(k):
            return lax.rem(z + k, nz) * nx + x

        def mix_copy(q):
            return remote(mix, far_o.at[q - 1], m_s.at[q - 1], m_r.at[q - 1], "tensor", mate(q))

        def x_copy(q, p):
            return remote(
                dw.at[p, lax.rem(x + q, nx)], xslot.at[q - 1, p], x_s.at[q - 1, p],
                x_r.at[q - 1, p], "dp", x_peer(q),
            )

        def z_copy(p):
            return remote(
                zsrc.at[p], zslot.at[p], z_s.at[p], z_r.at[p], "dp", z_peer(order[p])
            )

        def gather_piece(p):
            for q in range(1, nx):
                x_copy(q, p).wait_recv()
            total = dw[p, x].astype(F32)
            for q in range(1, nx):
                total = total + xslot[q - 1, p].astype(F32)
            return total

        @pl.when(step == 0)
        def _():
            sibling = 2 * chip + 1 - side
            pairs = [
                (hid_h, hid), (low_h, low), (cot_h, cot), (nor_h, nor),
                (mixed_h.at[span(side * half, half)], mine),
            ]
            fetched = [
                pltpu.make_async_copy(src, dst, loc.at[n]) for n, (src, dst) in enumerate(pairs)
            ]
            for copy in fetched:
                copy.start()
            signal_all([
                ("tensor", [sibling] + [mate(q) for q in range(1, chips)]),
                ("dp", [x_peer(q) for q in range(1, nx)] + [z_peer(k) for k in range(1, nz)]),
            ])
            near_copy = remote(
                mixed_h.at[span((1 - side) * half, half)], near, n_s.at[0], n_r.at[0], "tensor",
                sibling,
            )
            near_copy.start()
            for copy in fetched[:4]:
                copy.wait()
            for p in range(nz):
                at = span(lax.rem(z + (order + [0])[p], nz) * (nx * rows), nx * rows)
                left = t_mm(hid[:, at], low[...]).astype(BF16)
                right = t_mm(cot[:, at], nor[...]).astype(BF16)
                for k in range(nx):
                    dw[p, k, :, :inner] = left[k * rows : (k + 1) * rows]
                    dw[p, k, :, inner:] = right[k * rows : (k + 1) * rows]
                for q in range(1, nx):
                    x_copy(q, p).start()
                if p == 0:
                    fetched[4].wait()
                    near_copy.wait_recv()
                    both = (mine[...].astype(F32) + near[...].astype(F32)).astype(BF16)
                    mix[...] = both
                    half_o[...] = both
                    for q in range(1, chips):
                        mix_copy(q).start()
            near_copy.wait_send()

        for s in range(1, blocks):

            @pl.when(step == s)
            def _(s=s):
                for p in range((s - 1) * per, min(s * per, inside)):
                    zsrc[p] = gather_piece(p).astype(BF16)
                    z_copy(p).start()

        bwd_kernel(*plain_in, *plain_out, *plain_scratch)

        @pl.when(step == blocks - 1)
        def _():
            last_o[...] = gather_piece(nz - 2).astype(BF16)
            total = gather_piece(nz - 1)
            for p in range(inside):
                z_copy(p).wait_recv()
                total = total + zslot[p].astype(F32)
            sum_o[...] = total
            for q in range(1, chips):
                mix_copy(q).wait()
            for p in range(inside):
                z_copy(p).wait_send()
            for p in range(nz):
                for q in range(1, nx):
                    x_copy(q, p).wait_send()

    spec = block_specs(blocks, True)
    hbm = pl.BlockSpec(memory_space=pl.ANY)
    dma = pltpu.SemaphoreType.DMA
    return pl.pallas_call(
        body,
        grid=(blocks,),
        in_specs=[spec(a.shape, kind) for a, kind in ins] + [hbm] * 5,
        out_specs=[spec(shape, kind) for shape, _, kind in outs]
        + [spec((rows, cols), "whole")] * 2
        + [spec((half, width), "whole"), hbm],
        out_shape=[jax.ShapeDtypeStruct(shape, dtype) for shape, dtype, _ in outs]
        + [
            jax.ShapeDtypeStruct((rows, cols), F32),
            jax.ShapeDtypeStruct((rows, cols), BF16),
            jax.ShapeDtypeStruct((half, width), BF16),
            jax.ShapeDtypeStruct((chips - 1, half, width), BF16),
        ],
        scratch_shapes=scratch
        + [
            pltpu.VMEM((half, width), BF16),
            pltpu.VMEM((half, width), BF16),
            pltpu.VMEM((half, width), BF16),
            pltpu.VMEM((length, width), BF16),
            pltpu.VMEM((length, inner), BF16),
            pltpu.VMEM((length, width), BF16),
            pltpu.VMEM((length, inner), BF16),
            pltpu.VMEM((nz, nx, rows, cols), BF16),
            pltpu.VMEM((nx - 1, nz, rows, cols), BF16),
            pltpu.VMEM((inside, rows, cols), BF16),
            pltpu.VMEM((inside, rows, cols), BF16),
            dma((5,)), dma((1,)), dma((1,)), dma((chips - 1,)), dma((chips - 1,)), dma((nx - 1, nz)), dma((nx - 1, nz)),
            dma((inside,)), dma((inside,)),
        ],
        compiler_params=pltpu.CompilerParams(
            dimension_semantics=("arbitrary",), collective_id=collective_id, has_side_effects=True,
            vmem_limit_bytes=60 * 1024 * 1024,
        ),
        cost_estimate=cost(micros),
        name="bwd_scan",
    )(*[a for a, _ in ins], mixed, hidden, gate_low, cotangent, normal)


def finish_kernel(
    heads, result, gtok, gate_out, last, value_step, shared, early, late,
    result_o, gtok_o, dgate_o, dvalue_o, dshared_o, dstep_o, dout_o,
    convv_o, biasv_o, convs_o, biass_o, h0_o, h1_o, h2_o, gain_o, norm_o,
):
    inner = dgate_o.shape[1]
    result_o[...] = result[...]
    gtok_o[...] = gtok[...]

    @pl.when(pl.program_id(0) == 0)
    def _():
        dgate_o[...] = gate_out[:, :inner] + last[:, :inner].astype(F32)
        dout_o[...] = gate_out[:, inner:] + last[:, inner:].astype(F32)
        dvalue_o[...] = value_step[:, :inner]
        dstep_o[...] = jnp.transpose(value_step[:, inner : inner + LANES])[:heads, :]
        dshared_o[...] = shared[...]
        convv_o[...] = early[0:4, :inner]
        biasv_o[...] = early[4:5, :inner]
        gain_o[...] = early[5:6, :inner]
        h0_o[...] = early[0:1, inner : inner + heads]
        h1_o[...] = early[1:2, inner : inner + heads]
        h2_o[...] = early[2:3, inner : inner + heads]
        convs_o[...] = late[0:4, :]
        biass_o[...] = late[4:5, :]
        norm_o[...] = late[5:6, : norm_o.shape[1]]


def tail_step(
    heads_part, dbc_part, hidden, value_low, step_low, shared_conv, shared_pre, aux, tokens, cotangent,
    ng, shared_proj, shp, mixed_half, mixed_far, last, ch_grads, head_grads, gain_part,
    collective_id, micros,
):
    length, width = tokens.shape
    inner = value_low.shape[1]
    shared_width = shared_proj.shape[1]
    nt, nd = lax.axis_size("tensor"), lax.axis_size("dp")
    ng_chips = nt // 2
    nx, nz = split_dp(nd)
    rows = width // nd
    quarter, half = length // nt, length // 2
    piece = quarter // PIECES
    part = nz * rows
    low_width = inner + LANES
    norm_width = width // nt
    early_width = inner + LANES
    late_width = shared_width
    blocks = length // SPAN
    chunk = 256
    path = hops(nz) + [0]
    n_mixed = ng_chips - 1
    n_late = 9 + n_mixed

    def body(*refs):
        refs = list(refs)

        def take(n):
            out = refs[:n]
            del refs[:n]
            return out

        heads_r, dbc, aux_r, ng_r, ws, shp_r, chg, hg, gain = take(9)
        hid_h, vlow_h, slow_h, scv_h, spre_h, tok_h, cot_h, mix_h, mixfar_h, last_h = take(10)
        result_o, gtok_o, value_o, shared_o, early_o, late_o, last_o = take(7)
        hid, low, scv, spre, tokh, tokq, cotq, mix, mixfar = take(9)
        (
            dnear, dslots, dtot, dbuf, shlow, hnear, fsrc, ffar, hacc, vbuf, vslot, sbuf, sslot,
            zv, zvslot, zs, zsslot, eslots, lslots, nbuf, nslot,
        ) = take(21)
        (
            loc, a_s, a_r, d_s, d_r, n_s, n_r, f_s, f_r, g_s, g_r, h_s, h_r, r_s, r_r,
            zv_s, zv_r, zs_s, zs_r, xv_s, xv_r, w_s, w_r, xs_s, xs_r, e_s, e_r, l_s, l_r, m_s, m_r,
        ) = take(31)

        me = lax.axis_index("tensor")
        side, chip = lax.rem(me, 2), me // 2
        sibling = 2 * chip + 1 - side
        md = lax.axis_index("dp")
        x, z = lax.rem(md, nx), md // nx

        def chip_at(q):
            return lax.rem(chip + q, ng_chips)

        def mate(q):
            return 2 * chip_at(q) + side

        def x_peer(q):
            return z * nx + lax.rem(x + q, nx)

        def z_peer(k):
            return lax.rem(z + k, nz) * nx + x

        count = [0]

        def fetch(src, dst):
            copy = pltpu.make_async_copy(src, dst, loc.at[count[0]])
            count[0] += 1
            copy.start()
            return copy

        my_rows = span(me * quarter, quarter)
        my_half = span(side * half, half)
        sib_half = span((1 - side) * half, half)
        got_low = [
            fetch(hid_h, hid), fetch(vlow_h, low.at[:, 0:inner]),
            fetch(slow_h, low.at[:, inner : inner + LANES]),
        ]
        got_mix = [fetch(mix_h, mix), fetch(tok_h.at[my_half], tokh)]
        got_mix += [fetch(mixfar_h.at[q], mixfar.at[q]) for q in range(n_mixed)]
        got_shared = [fetch(scv_h, scv), fetch(spre_h, spre)]
        got_end = [fetch(tok_h.at[my_rows], tokq), fetch(cot_h.at[my_rows], cotq)]

        signal_all([
            ("tensor", [lax.rem(me + k, nt) for k in range(1, nt)]),
            ("dp", [lax.rem(md + k, nd) for k in range(1, nd)]),
        ])
        sent = []

        def send(*args):
            copy = push(*args)
            sent.append(copy)
            return copy

        dn = send(dbc.at[sib_half], dnear, a_s.at[0], a_r.at[0], "tensor", sibling)
        last_copy = send(last_h, last_o, w_s.at[0], w_r.at[0], "dp", z_peer(path[nz - 2]))
        order = list(range(1, ng_chips)) + [0]
        near = {}
        for q in order:
            for p in range(PIECES):
                at = (2 * chip_at(q) + 1 - side) * quarter + p * piece
                near[q, p] = send(
                    heads_r.at[span(at, piece)], hnear.at[q, p], n_s.at[q, p], n_r.at[q, p],
                    "tensor", sibling,
                )
        eslots[md, :, :inner] = jnp.concatenate(
            [chg[0:5, :], gain[0:1, :], jnp.zeros((2, inner), F32)], axis=0
        )
        eslots[md, :, inner:] = hg[...]

        dn.wait_recv()
        dslots[chip] = (dbc[my_half, :] + dnear[...]).astype(BF16)
        dmates = [
            send(dslots.at[chip], dslots.at[chip], d_s.at[q], d_r.at[q], "tensor", mate(q))
            for q in range(1, ng_chips)
        ]
        fwd = {}
        for q in order:
            for p in range(PIECES):
                near[q, p].wait_recv()
                at = (2 * chip_at(q) + side) * quarter + p * piece
                both = heads_r[span(at, piece), :].astype(F32) + hnear[q, p].astype(F32)
                if q:
                    fsrc[q, p] = both.astype(BF16)
                    fwd[q, p] = send(
                        fsrc.at[q, p], ffar.at[q, p], f_s.at[q, p], f_r.at[q, p], "tensor", mate(q)
                    )
                else:
                    hacc[p * piece : (p + 1) * piece, :] = both
        es = [
            send(
                eslots.at[md], eslots.at[md], e_s.at[k], e_r.at[k], "dp", lax.rem(md + k, nd)
            )
            for k in range(1, nd)
        ]

        for copy in got_low:
            copy.wait()
        xvs = {}
        for p in range(nz):
            cols = span(lax.rem(z + path[p], nz) * (nx * rows), nx * rows)
            prod = t_mm(hid[:, cols], low[...]).astype(BF16)
            for k in range(nx):
                vbuf[p, k] = prod[k * rows : (k + 1) * rows]
            for q in range(1, nx):
                xvs[q, p] = send(
                    vbuf.at[p, lax.rem(x + q, nx)], vslot.at[q - 1, p], xv_s.at[q - 1, p],
                    xv_r.at[q - 1, p], "dp", x_peer(q),
                )
        zvs = []

        def own_piece(p):
            total = vbuf[p, x].astype(F32)
            for q in range(1, nx):
                xvs[q, p].wait_recv()
                total = total + vslot[q - 1, p].astype(F32)
            return total

        def pass_on(p):
            zv[p] = own_piece(p).astype(BF16)
            zvs.append(
                send(zv.at[p], zvslot.at[p], zv_s.at[p], zv_r.at[p], "dp", z_peer(path[p]))
            )

        for copy in got_shared:
            copy.wait()
        for copy in dmates:
            copy.wait_recv()
        total = dslots[0].astype(F32)
        for g in range(1, ng_chips):
            total = total + dslots[g].astype(F32)
        dtot[my_half, :] = total
        dt_copy = send(
            dtot.at[my_half], dtot.at[my_half], a_s.at[1], a_r.at[1], "tensor", sibling
        )

        pass_on(0)
        for copy in got_mix:
            copy.wait()
        mixed = mix[...].astype(F32)
        if n_mixed == 1:
            mixed = mixed + mixfar[0].astype(F32)
        else:
            terms = [mix] + [mixfar.at[q] for q in range(n_mixed)]
            mixed = jnp.zeros((half, width), F32)
            for g in range(ng_chips):
                for q in range(ng_chips):
                    mine = (lax.rem(chip - q + ng_chips, ng_chips) == g).astype(F32)
                    mixed = mixed + terms[q][...].astype(F32) * mine
        result_o[my_half, :] = (tokh[...].astype(F32) + mixed).astype(BF16)
        res = send(
            result_o.at[my_half], result_o.at[my_half], r_s.at[0], r_r.at[0], "tensor", sibling
        )

        if nz > 2:
            pass_on(1)
        dt_copy.wait_recv()
        dbuf[length : length + 8, :] = jnp.zeros((8, shared_width), F32)
        sums = [jnp.zeros((1, shared_width), F32)] * 5
        for b in reversed(range(blocks)):
            base = b * SPAN
            at = slice(base, base + SPAN)
            sc = scv[at, :]
            csig = sigmoid(sc)
            dcv = dtot[at, :] * (csig * (1.0 + sc * (1.0 - csig)))
            dbuf[at, :] = dcv
            sp = spre[at, :]
            mask = aux_r[at, :]
            ds = dcv * shp_r[3:4, :]
            sums[3] = sums[3] + jnp.sum(dcv * sp, axis=0, keepdims=True)
            sums[4] = sums[4] + jnp.sum(dcv, axis=0, keepdims=True)
            for j in range(1, 4):
                moved = dbuf[base + j : base + j + SPAN, :] * mask[:, 8 + j : 9 + j]
                ds = ds + moved * shp_r[3 - j : 4 - j, :]
                sums[3 - j] = sums[3 - j] + jnp.sum(moved * sp, axis=0, keepdims=True)
            shlow[at, :] = ds.astype(BF16)
        for p in range(2, nz - 1):
            pass_on(p)
        for c in range(width // chunk):
            prod = t_mm(hid[:, c * chunk : (c + 1) * chunk], shlow[...]).astype(BF16)
            for d in range(c * chunk // rows, (c + 1) * chunk // rows):
                at = slice(d * rows - c * chunk, (d + 1) * rows - c * chunk)
                sbuf[d % nx, (d // nx) * rows : (d // nx + 1) * rows, :] = prod[at]
        xss = [
            send(
                sbuf.at[lax.rem(x + q, nx)], sslot.at[q], xs_s.at[q], xs_r.at[q], "dp", x_peer(q)
            )
            for q in range(1, nx)
        ]
        hacc[...] = hacc[...] + mm_t(shlow[my_rows, :], ws[...])

        for copy in got_end:
            copy.wait()
        norm = jnp.zeros((1, width), F32)
        gather, own = {}, []
        for p in range(PIECES):
            at = slice(p * piece, (p + 1) * piece)
            grad_hidden = hacc[at, :]
            for q in range(1, ng_chips):
                fwd[q, p].wait_recv()
                grad_hidden = grad_hidden + ffar[q, p].astype(F32)
            v = tokq[at, :].astype(F32)
            inv = lax.rsqrt(jnp.mean(v * v, axis=1, keepdims=True) + EPSILON)
            normed = v * inv
            scaled = grad_hidden * ng_r[...]
            norm = norm + jnp.sum(grad_hidden * normed, axis=0, keepdims=True)
            mean = jnp.mean(scaled * normed, axis=1, keepdims=True)
            place = span(me * quarter + p * piece, piece)
            gtok_o[place, :] = (inv * (scaled - normed * mean) + cotq[at, :].astype(F32)).astype(BF16)
            for q in range(1, ng_chips):
                gather[q, p] = send(
                    gtok_o.at[place], gtok_o.at[place], g_s.at[q, p], g_r.at[q, p], "tensor", mate(q)
                )
            own.append(
                send(gtok_o.at[place], gtok_o.at[place], h_s.at[0, p], h_r.at[0, p], "tensor", sibling)
            )
        for q in range(nt):
            nbuf[q] = norm[:, q * norm_width : (q + 1) * norm_width] + jnp.zeros((8, norm_width), F32)
        norms = [
            send(
                nbuf.at[lax.rem(me + k, nt)], nslot.at[k], m_s.at[k], m_r.at[k], "tensor",
                lax.rem(me + k, nt),
            )
            for k in range(1, nt)
        ]

        for copy in xss:
            copy.wait_recv()
        total = sbuf[x].astype(F32)
        for q in range(1, nx):
            total = total + sslot[q].astype(F32)
        zs[...] = total.astype(BF16)
        zss = [
            send(
                zs.at[span(lax.rem(z + k, nz) * rows, rows)], zsslot.at[k], zs_s.at[k], zs_r.at[k],
                "dp", z_peer(k),
            )
            for k in range(1, nz)
        ]

        for copy in norms:
            copy.wait_recv()
        total = nbuf[me]
        for k in range(1, nt):
            total = total + nslot[k]
        wide = jnp.concatenate(
            [total[0:1, :], jnp.zeros((1, shared_width - norm_width), F32)], axis=1
        ) if norm_width < shared_width else total[0:1, :]
        lslots[md] = jnp.concatenate(sums + [wide, jnp.zeros((2, shared_width), F32)], axis=0)
        ls = [
            send(
                lslots.at[md], lslots.at[md], l_s.at[k], l_r.at[k], "dp", lax.rem(md + k, nd)
            )
            for k in range(1, nd)
        ]

        for copy in es:
            copy.wait_recv()
        total = eslots[0]
        for s in range(1, nd):
            total = total + eslots[s]
        early_o[...] = total

        for p in range(PIECES):
            for q in range(1, ng_chips):
                gather[q, p].wait_recv()
                came = 2 * lax.rem(chip - q + ng_chips, ng_chips) + side
                place = span(came * quarter + p * piece, piece)
                own.append(
                    send(
                        gtok_o.at[place], gtok_o.at[place], h_s.at[q, p], h_r.at[q, p],
                        "tensor", sibling,
                    )
                )

        for copy in zvs:
            copy.wait_recv()
        total = own_piece(nz - 1)
        for p in range(nz - 1):
            total = total + zvslot[p].astype(F32)
        value_o[...] = total
        for copy in zss:
            copy.wait_recv()
        total = zs[span(z * rows, rows), :].astype(F32)
        for k in range(1, nz):
            total = total + zsslot[k].astype(F32)
        shared_o[...] = total

        for copy in ls:
            copy.wait_recv()
        total = lslots[0]
        for s in range(1, nd):
            total = total + lslots[s]
        late_o[...] = total

        res.wait_recv()
        last_copy.wait_recv()
        for copy in own:
            copy.wait_recv()
        for copy in sent:
            copy.wait_send()

    vm = pl.BlockSpec(memory_space=pltpu.VMEM)
    hbm = pl.BlockSpec(memory_space=pl.ANY)
    dma = pltpu.SemaphoreType.DMA

    def f32(*shape):
        return pltpu.VMEM(shape, F32)

    def bf16(*shape):
        return pltpu.VMEM(shape, BF16)

    def out(*shape):
        return jax.ShapeDtypeStruct(shape, F32)

    early = [heads_part, dbc_part, aux, ng, shared_proj, shp, ch_grads, head_grads, gain_part]
    late = [hidden, value_low, step_low, shared_conv, shared_pre, tokens, cotangent, mixed_half]
    late += [mixed_far, last]
    return pl.pallas_call(
        body,
        in_specs=[vm] * len(early) + [hbm] * len(late),
        out_specs=[vm] * 6 + [hbm],
        out_shape=[
            jax.ShapeDtypeStruct((length, width), BF16), jax.ShapeDtypeStruct((length, width), BF16),
            out(rows, low_width), out(rows, shared_width), out(8, early_width), out(8, late_width),
            jax.ShapeDtypeStruct(last.shape, last.dtype),
        ],
        scratch_shapes=[
            bf16(length, width), bf16(length, low_width), f32(length, shared_width),
            f32(length, shared_width), bf16(half, width), bf16(quarter, width), bf16(quarter, width),
            bf16(half, width), bf16(n_mixed, half, width),
            f32(half, shared_width), bf16(ng_chips, half, shared_width), f32(length, shared_width),
            f32(length + 8, shared_width), bf16(length, shared_width),
            bf16(ng_chips, PIECES, piece, width), bf16(ng_chips, PIECES, piece, width),
            bf16(ng_chips, PIECES, piece, width), f32(quarter, width),
            bf16(nz, nx, rows, low_width), bf16(nx - 1, nz, rows, low_width),
            bf16(nx, part, shared_width), bf16(nx, part, shared_width),
            bf16(nz - 1, rows, low_width), bf16(nz - 1, rows, low_width),
            bf16(part, shared_width), bf16(nz, rows, shared_width),
            f32(nd, 8, early_width), f32(nd, 8, late_width),
            f32(nt, 8, norm_width), f32(nt, 8, norm_width),
        ]
        + [dma((n_late + 1,)), dma((2,)), dma((2,)), dma((ng_chips,)), dma((ng_chips,))]
        + [dma((ng_chips, PIECES))] * 8
        + [dma((1,)), dma((1,))]
        + [dma((nz,))] * 4
        + [dma((nx - 1, nz))] * 2
        + [dma((1,))] * 2
        + [dma((nx,))] * 2
        + [dma((nd,))] * 4
        + [dma((nt,))] * 2,
        compiler_params=pltpu.CompilerParams(
            collective_id=collective_id, has_side_effects=True, vmem_limit_bytes=60 * 1024 * 1024
        ),
        cost_estimate=cost(micros),
        name="tail_step",
    )(*early, *late)


def per_device(
    tokens, cotangent, segments, norm_gain, gate_proj, value_proj, shared_proj, step_proj,
    conv_value, bias_value, conv_shared, bias_shared, step_bias, decay_log, skip_gain,
    gate_gain, out_proj,
):
    tp_count = lax.axis_size("tensor")
    dp_count = lax.axis_size("dp")
    length, width = tokens.shape
    inner = gate_proj.shape[1]
    heads = step_proj.shape[1]
    shared_width = shared_proj.shape[1]
    state_size = shared_width // 2
    blocks = length // SPAN
    aux, segr, wst, chp, shp, hp = pl.pallas_call(
        prep_kernel,
        out_shape=[
            jax.ShapeDtypeStruct((length, LANES), F32),
            jax.ShapeDtypeStruct((1, length), F32),
            jax.ShapeDtypeStruct((width, LANES), BF16),
            jax.ShapeDtypeStruct((8, inner), F32),
            jax.ShapeDtypeStruct((8, shared_width), F32),
            jax.ShapeDtypeStruct((8, LANES), F32),
        ],
        name="prep_step",
    )(
        segments, step_proj.T, conv_value, bias_value[None], gate_gain[None], skip_gain[None],
        conv_shared, bias_shared[None], step_bias[None], decay_log[None],
    )
    ng = norm_gain[None, :]

    (
        hidden, gate_pre, value_pre, conv_out, shared_pre, shared_conv, z, ld, ldt, yn, sin, gn, stat,
    ) = call(
        fwd_kernel,
        blocks,
        [
            (tokens, "rows"), (cotangent, "rows"), (aux, "rows"), (segr, "lanes"), (ng, "whole"),
            (gate_proj, "whole"), (value_proj, "whole"), (shared_proj, "whole"), (wst, "whole"),
            (out_proj, "whole"), (chp, "whole"), (shp, "whole"), (hp, "whole"),
        ],
        [
            ((length, width), BF16, "rows"),
            ((length, inner), F32, "rows"),
            ((length, inner), F32, "rows"),
            ((length, inner), F32, "rows"),
            ((length, shared_width), F32, "rows"),
            ((length, shared_width), F32, "rows"),
            ((length, LANES), F32, "rows"),
            ((length, LANES), F32, "rows"),
            ((8, length), F32, "lanes"),
            ((length, inner), F32, "rows"),
            ((blocks * state_size, inner), F32, "rows"),
            ((length, inner), F32, "rows"),
            ((8, length), F32, "lanes"),
        ],
        [
            pltpu.VMEM((SPAN + 8, inner), F32),
            pltpu.VMEM((SPAN + 8, shared_width), F32),
            pltpu.VMEM((state_size, inner), F32),
        ],
        False,
        "fwd_scan",
        20,
    )
    stat = small_sum(stat, "tensor", 0)
    total_inner = float(inner * tp_count)

    def gate_body(*refs):
        gate_kernel(total_inner, *refs)

    normal_out, dy, gate_low, gain_part, mixed_part = call(
        gate_body,
        blocks,
        [
            (gate_pre, "rows"), (conv_out, "rows"), (yn, "rows"), (gn, "rows"), (stat, "lanes"),
            (chp, "whole"), (out_proj, "whole"),
        ],
        [
            ((length, inner), BF16, "rows"),
            ((length, inner), F32, "rows"),
            ((length, inner), BF16, "rows"),
            ((8, inner), F32, "whole"),
            ((length, width), BF16, "rows"),
        ],
        [],
        False,
        "gate_step",
        9,
    )
    (
        value_low, step_low, heads_part, dbc_part, ch_grads, head_grads, gate_out, last, mixed_half,
        mixed_far,
    ) = bwd_step(
        [
            (dy, "rows"), (conv_out, "rows"), (value_pre, "rows"), (shared_conv, "rows"),
            (z, "rows"), (ld, "rows"), (ldt, "lanes"), (yn, "rows"), (sin, "rows"),
            (aux, "rows"), (segr, "lanes"), (gate_low, "rows"), (gate_proj, "whole"),
            (value_proj, "whole"), (wst, "whole"), (chp, "whole"), (hp, "whole"),
        ],
        [
            ((length, inner), BF16, "rows"),
            ((length, LANES), BF16, "rows"),
            ((length, width), BF16, "rows"),
            ((length, shared_width), F32, "rows"),
            ((8, inner), F32, "whole"),
            ((8, LANES), F32, "whole"),
        ],
        [pltpu.VMEM((SPAN + 8, inner), F32), pltpu.VMEM((state_size, inner), F32)],
        mixed_part, hidden, gate_low, cotangent, normal_out, blocks, 3, 30,
    )
    result, grad_tokens, value_step, shared_sum, early, late, last = tail_step(
        heads_part, dbc_part, hidden, value_low, step_low, shared_conv, shared_pre, aux, tokens,
        cotangent, ng, shared_proj, shp, mixed_half, mixed_far, last, ch_grads, head_grads,
        gain_part, 2, 40,
    )

    def finish_body(*refs):
        finish_kernel(heads, *refs)

    rows = width // dp_count
    (
        result, grad_tokens, dgate, dvalue, dshared, dstep, dout,
        convv, biasv, convs, biass, h0, h1, h2, gain, norm,
    ) = call(
        finish_body,
        blocks,
        [
            (result, "rows"), (grad_tokens, "rows"), (gate_out, "whole"), (last, "whole"),
            (value_step, "whole"),
            (shared_sum, "whole"), (early, "whole"), (late, "whole"),
        ],
        [
            ((length, width), BF16, "rows"), ((length, width), BF16, "rows"),
            ((rows, inner), F32, "whole"), ((rows, inner), F32, "whole"),
            ((rows, shared_width), F32, "whole"), ((heads, rows), F32, "whole"),
            ((rows, inner), F32, "whole"), ((4, inner), F32, "whole"), ((1, inner), F32, "whole"),
            ((4, shared_width), F32, "whole"), ((1, shared_width), F32, "whole"),
            ((1, heads), F32, "whole"), ((1, heads), F32, "whole"), ((1, heads), F32, "whole"),
            ((1, inner), F32, "whole"), ((1, width // tp_count), F32, "whole"),
        ],
        [],
        False,
        "finish_step",
        3,
    )
    return (
        result, grad_tokens, norm[0], dgate, dvalue, dshared, dstep.T, convv, biasv[0], convs, biass[0],
        h0[0], h1[0], h2[0], gain[0], dout,
    )


def solution(mesh):
    rows, cols, vec = P("dp", None), P(None, "tensor"), P("tensor")
    return jax.shard_map(
        per_device,
        mesh=mesh,
        in_specs=(
            rows, rows, rows, P(), cols, cols, P(), cols, cols, vec, P(), P(), vec, vec, vec, vec, cols,
        ),
        out_specs=(
            rows, rows, vec, P("dp", "tensor"), P("dp", "tensor"), rows, P("dp", "tensor"), cols, vec,
            P(), P(), vec, vec, vec, vec, P("dp", "tensor"),
        ),
        check_vma=False,
    )
```

```python
import jax
import jax.numpy as jnp
from jax import lax
from jax.experimental import pallas as pl
from jax.experimental.pallas import tpu as pltpu
from jax.sharding import PartitionSpec as P

SPAN = 256
HSIZE = 64
LANES = 128
EPSILON = 1e-05
NEG_FILL = -1e30
EXACT = lax.Precision.HIGHEST
F32 = jnp.float32
BF16 = jnp.bfloat16


def mm(left, right):
    return jnp.dot(left, right, preferred_element_type=F32)


def mm_t(left, right):
    return lax.dot_general(left, right, (((1,), (1,)), ((), ())), preferred_element_type=F32)


def t_mm(left, right):
    return lax.dot_general(left, right, (((0,), (0,)), ((), ())), preferred_element_type=F32)


def exact(left, right):
    return jnp.dot(left, right, precision=EXACT, preferred_element_type=F32)


def sigmoid(v):
    return 1.0 / (1.0 + jnp.exp(-v))


def spread(cols, pairs):
    low = lax.broadcasted_iota(jnp.int32, (cols.shape[0], LANES), 1) < HSIZE
    parts = [
        jnp.where(low, cols[:, 2 * p : 2 * p + 1], cols[:, 2 * p + 1 : 2 * p + 2])
        for p in range(pairs)
    ]
    return jnp.concatenate(parts, axis=1)


def gather_mat(inner):
    channel = lax.broadcasted_iota(jnp.int32, (inner, LANES), 0) // HSIZE
    head = lax.broadcasted_iota(jnp.int32, (inner, LANES), 1)
    return (channel == head).astype(F32)


def grid_masks():
    row = lax.broadcasted_iota(jnp.int32, (SPAN, SPAN), 0)
    col = lax.broadcasted_iota(jnp.int32, (SPAN, SPAN), 1)
    return row, col


def conv_fwd(buf, pack, aux):
    out = pack[4:5, :] + buf[8 : 8 + SPAN, :] * pack[3:4, :]
    for j in range(1, 4):
        out = out + buf[8 - j : 8 - j + SPAN, :] * (aux[:, j : j + 1] * pack[3 - j : 4 - j, :])
    return out


def fwd_kernel(
    tok, cot, aux_ref, segr, ng, wg, wv, ws, wst, wo, chp, shp, hp,
    hidden_o, gate_o, vpre_o, cv_o, spre_o, scv_o, z_o, ld_o, ldt_o, yn_o, sin_o, gn_o, stat_o,
    vbuf, sbuf, state,
):
    inner = wg.shape[1]
    pairs = inner // LANES
    state_size = ws.shape[1] // 2

    @pl.when(pl.program_id(0) == 0)
    def _():
        vbuf[0:8, :] = jnp.zeros((8, inner), F32)
        sbuf[0:8, :] = jnp.zeros((8, 2 * state_size), F32)
        state[...] = jnp.zeros_like(state)

    aux = aux_ref[...]
    x = tok[...].astype(F32)
    inv = lax.rsqrt(jnp.mean(x * x, axis=1, keepdims=True) + EPSILON)
    hid = (x * inv * ng[...]).astype(BF16)
    hidden_o[...] = hid
    gate = mm(hid, wg[...])
    gate_o[...] = gate
    vp = mm(hid, wv[...])
    vpre_o[...] = vp
    vbuf[8 : 8 + SPAN, :] = vp
    sp = mm(hid, ws[...])
    spre_o[...] = sp
    sbuf[8 : 8 + SPAN, :] = sp
    z = mm(hid, wst[...]) + hp[0:1, :]
    z_o[...] = z
    gn = mm(cot[...], wo[...])
    gn_o[...] = gn
    scv = conv_fwd(sbuf, shp, aux)
    scv_o[...] = scv
    bc = (scv * sigmoid(scv)).astype(BF16)
    b_low, c_low = bc[:, :state_size], bc[:, state_size:]
    cv = conv_fwd(vbuf, chp, aux)
    cv_o[...] = cv
    vbuf[0:8, :] = vbuf[SPAN : SPAN + 8, :]
    sbuf[0:8, :] = sbuf[SPAN : SPAN + 8, :]
    values = cv * sigmoid(cv)
    dt = jnp.maximum(z, 0.0) + jnp.log1p(jnp.exp(-jnp.abs(z)))
    row, col = grid_masks()
    tri = (row >= col).astype(F32)
    ld = exact(tri, dt * hp[1:2, :])
    ld_o[...] = ld
    ldt = jnp.transpose(ld)[0:8, :]
    ldt_o[...] = ldt
    allowed = (row >= col) & (aux[:, 0:1] == segr[...])
    scores = jnp.where(allowed, mm_t(c_low, b_low), 0.0)
    xs = values * spread(dt, pairs)
    xs_low = xs.astype(BF16)
    ein = jnp.exp(ld) * aux[:, 4:5]
    eout = jnp.exp(ld[SPAN - 1 : SPAN, :] - ld) * aux[:, 5:6]
    ein_x = spread(ein, pairs)
    eout_x = spread(eout, pairs)
    old = state[...]
    sin_o[...] = old
    carried = mm(c_low, old.astype(BF16)) * ein_x
    state[...] = old * ein_x[SPAN - 1 : SPAN, :] + t_mm(b_low, (xs * eout_x).astype(BF16))
    low = lax.broadcasted_iota(jnp.int32, (SPAN, LANES), 1) < HSIZE
    parts = []
    for p in range(pairs):
        pair = xs_low[:, p * LANES : (p + 1) * LANES]
        outs = []
        for h in (2 * p, 2 * p + 1):
            gap = jnp.minimum(ld[:, h : h + 1] - ldt[h : h + 1, :], 0.0)
            outs.append(mm((jnp.exp(gap) * scores).astype(BF16), pair))
        parts.append(jnp.where(low, outs[0], outs[1]))
    yn = jnp.concatenate(parts, axis=1) + carried
    yn_o[...] = yn
    gated = (yn + chp[6:7, :] * values) * (gate * sigmoid(gate))
    squares = jnp.sum(gated * gated, axis=1, keepdims=True)
    dots = jnp.sum(gn * chp[5:6, :] * gated, axis=1, keepdims=True)
    lane = lax.broadcasted_iota(jnp.int32, (SPAN, LANES), 1)
    both = jnp.where(lane == 0, squares, jnp.where(lane == 1, dots, 0.0))
    stat_o[...] = jnp.transpose(both)[0:8, :]


def gate_kernel(
    width, first, gate_ref, cv_ref, yn, gn_ref, stat, chp, wo, normal_o, dy_o, low_o, gain_o, mixed_o
):
    both = jnp.transpose(jnp.concatenate([stat[...]] * (LANES // 8), axis=0))
    inv = lax.rsqrt(both[:, 0:1] / width + EPSILON)
    mean_dots = both[:, 1:2] / width
    gate = gate_ref[...]
    cv = cv_ref[...]
    gn = gn_ref[...]
    sig = sigmoid(gate)
    act = gate * sig
    mixer = yn[...] + chp[6:7, :] * (cv * sigmoid(cv))
    gated = mixer * act
    normed = gated * inv
    normal = (normed * chp[5:6, :]).astype(BF16)
    normal_o[...] = normal
    mixed_o[...] = mm_t(normal, wo[...]).astype(BF16)
    part = jnp.sum(gn * normed, axis=0, keepdims=True)

    @pl.when(first)
    def _():
        gain_o[...] = jnp.zeros_like(gain_o)

    gain_o[0:1, :] += part
    grad_gated = inv * (gn * chp[5:6, :]) - gated * (inv * inv * inv) * mean_dots
    dy_o[...] = grad_gated * act
    low_o[...] = (grad_gated * mixer * (sig * (1.0 + gate * (1.0 - sig)))).astype(BF16)


def bwd_kernel(
    dy_ref, cv_ref, vpre, scv_ref, z_ref, ld_ref, ldt_ref, yn, sin, aux_ref, segr, glow,
    wg, wv, wst, chp, hp,
    vlow_o, slow_o, heads_o, dbc_o, chg_o, hg_o,
    dbuf, dstate,
):
    inner = wg.shape[1]
    pairs = inner // LANES
    state_size = sin.shape[0]

    @pl.when(pl.program_id(0) == 0)
    def _():
        dbuf[SPAN : SPAN + 8, :] = jnp.zeros((8, inner), F32)
        dstate[...] = jnp.zeros_like(dstate)
        chg_o[...] = jnp.zeros_like(chg_o)
        hg_o[...] = jnp.zeros_like(hg_o)

    aux = aux_ref[...]
    dy = dy_ref[...]
    dy_low = dy.astype(BF16)
    scv = scv_ref[...]
    bc = (scv * sigmoid(scv)).astype(BF16)
    b_low, c_low = bc[:, :state_size], bc[:, state_size:]
    cv = cv_ref[...]
    csig = sigmoid(cv)
    values = cv * csig
    z = z_ref[...]
    dt = jnp.maximum(z, 0.0) + jnp.log1p(jnp.exp(-jnp.abs(z)))
    ld = ld_ref[...]
    ldt = ldt_ref[...]
    dt_x = spread(dt, pairs)
    xs = values * dt_x
    xs_low = xs.astype(BF16)
    ein = jnp.exp(ld) * aux[:, 4:5]
    eout = jnp.exp(ld[SPAN - 1 : SPAN, :] - ld) * aux[:, 5:6]
    ein_x = spread(ein, pairs)
    eout_x = spread(eout, pairs)
    row, col = grid_masks()
    allowed = (col >= row) & (aux[:, 0:1] == segr[...])
    mask = allowed.astype(F32)
    scores_t = mm_t(b_low, c_low) * mask
    low = lax.broadcasted_iota(jnp.int32, (SPAN, LANES), 1) < HSIZE
    parts = []
    dscores_t = jnp.zeros((SPAN, SPAN), F32)
    for p in range(pairs):
        cols = slice(p * LANES, (p + 1) * LANES)
        dy_pair = dy_low[:, cols]
        xs_pair = xs_low[:, cols]
        zero = jnp.zeros_like(xs_pair)
        outs = []
        for side, h in enumerate((2 * p, 2 * p + 1)):
            gap = jnp.minimum(ldt[h : h + 1, :] - ld[:, h : h + 1], 0.0)
            decay = jnp.exp(gap)
            outs.append(mm((decay * scores_t).astype(BF16), dy_pair))
            mine = jnp.where(low, xs_pair, zero) if side == 0 else jnp.where(low, zero, xs_pair)
            dscores_t = dscores_t + mm_t(mine, dy_pair) * decay
        parts.append(jnp.where(low, outs[0], outs[1]))
    inside = jnp.concatenate(parts, axis=1)
    dscores_low = (dscores_t * mask).astype(BF16)
    old = sin[...]
    dst = dstate[...]
    dst_low = dst.astype(BF16)
    dye_low = (dy * ein_x).astype(BF16)
    xse_low = (xs * eout_x).astype(BF16)
    db = mm(dscores_low, c_low) + mm_t(xse_low, dst_low)
    dc = t_mm(dscores_low, b_low) + mm_t(dye_low, old.astype(BF16))
    late = mm(b_low, dst_low) * eout_x
    keep = ein_x[SPAN - 1 : SPAN, :]
    dstate[...] = dst * keep + t_mm(c_low, dye_low)
    dxs = inside + late
    collect = gather_mat(inner)
    q = dy_low.astype(F32) * yn[...] - xs_low.astype(F32) * inside
    u = xs * late
    kappa = exact(jnp.sum(old * dst, axis=0, keepdims=True) * keep + jnp.zeros((8, inner), F32), collect)
    da = (
        exact((col >= row).astype(F32), exact(q, collect))
        + exact((row > col).astype(F32), exact(u, collect))
        + kappa[0:1, :]
    )
    rates = hp[1:2, :]
    ddt = da * rates + exact(dxs * values, collect)
    dz = ddt * sigmoid(z)
    slow = dz.astype(BF16)
    slow_o[...] = slow
    skip = exact(jnp.sum(dy * values, axis=0, keepdims=True) + jnp.zeros((8, inner), F32), collect)
    hg_o[0:1, :] += jnp.sum(dz, axis=0, keepdims=True)
    hg_o[1:2, :] += jnp.sum(da * dt, axis=0, keepdims=True) * rates
    hg_o[2:3, :] += skip[0:1, :]
    dcv = (dxs * dt_x + chp[6:7, :] * dy) * (csig * (1.0 + cv * (1.0 - csig)))
    dbuf[0:SPAN, :] = dcv
    vp = vpre[...]
    dv = dcv * chp[3:4, :]
    chg_o[3:4, :] += jnp.sum(dcv * vp, axis=0, keepdims=True)
    chg_o[4:5, :] += jnp.sum(dcv, axis=0, keepdims=True)
    for j in range(1, 4):
        moved = dbuf[j : j + SPAN, :] * aux[:, 8 + j : 9 + j]
        dv = dv + moved * chp[3 - j : 4 - j, :]
        chg_o[3 - j : 4 - j, :] += jnp.sum(moved * vp, axis=0, keepdims=True)
    dbuf[SPAN : SPAN + 8, :] = dbuf[0:8, :]
    vlow = dv.astype(BF16)
    vlow_o[...] = vlow
    back = mm_t(glow[...], wg[...]) + mm_t(vlow, wv[...]) + mm_t(slow, wst[...])
    heads_o[...] = back.astype(BF16)
    dbc_o[...] = jnp.concatenate([db, dc], axis=1)


MESH = pl.DeviceIdType.MESH
PIECES = 4


def prep_kernel(
    seg, stepw, conv_v, bias_v, gate_g, skip_g, conv_s, bias_s, step_b, decay,
    aux_o, segr_o, wst_o, chp_o, shp_o, hp_o,
):
    length = seg.shape[1]
    ids = seg[...].astype(F32)
    segr_o[...] = ids
    wide = ids + jnp.zeros((8, length), F32)
    lane = lax.broadcasted_iota(jnp.int32, (8, length), 1)
    row = lax.broadcasted_iota(jnp.int32, (8, length), 0)
    ends = [
        ids[:, start + SPAN - 1 : start + SPAN] + jnp.zeros((8, SPAN), F32)
        for start in range(0, length, SPAN)
    ]
    last = jnp.concatenate(ends, axis=1)
    before = jnp.concatenate([jnp.full((8, SPAN), -1.0, F32)] + ends[:-1], axis=1)
    first = jnp.where(row == 0, wide, 0.0)
    first = jnp.where((row == 4) & (wide == before), 1.0, first)
    first = jnp.where((row == 5) & (wide == last), 1.0, first)
    second = jnp.zeros((8, length), F32)
    for j in range(1, 4):
        back = (pltpu.roll(wide, j, 1) == wide) & (lane >= j)
        ahead = (pltpu.roll(wide, length - j, 1) == wide) & (lane < length - j)
        first = jnp.where((row == j) & back, 1.0, first)
        second = jnp.where((row == j) & ahead, 1.0, second)
    rest = jnp.zeros((LANES - 16, length), F32)
    aux_o[...] = jnp.transpose(jnp.concatenate([first, second, rest], axis=0))
    heads, width = stepw.shape
    steps = jnp.concatenate([stepw[...].astype(F32), jnp.zeros((LANES - heads, width), F32)], axis=0)
    wst_o[...] = jnp.transpose(steps).astype(BF16)
    hp_o[...] = jnp.zeros_like(hp_o)
    hp_o[0:1, 0:heads] = step_b[...]
    hp_o[1:2, 0:heads] = -jnp.exp(decay[...])
    hp_o[2:3, 0:heads] = skip_g[...]
    inner = chp_o.shape[1]
    repeated = lax.dot_general(
        hp_o[...], gather_mat(inner), (((1,), (1,)), ((), ())), precision=EXACT,
        preferred_element_type=F32,
    )
    chp_o[0:4, :] = conv_v[...]
    chp_o[4:5, :] = bias_v[...]
    chp_o[5:6, :] = gate_g[...]
    chp_o[6:7, :] = repeated[2:3, :]
    chp_o[7:8, :] = jnp.zeros((1, inner), F32)
    shp_o[...] = jnp.zeros_like(shp_o)
    shp_o[0:4, :] = conv_s[...]
    shp_o[4:5, :] = bias_s[...]


def cost(micros):
    return pl.CostEstimate(
        flops=int(micros * 1e9), bytes_accessed=int(micros * 3.6e6), transcendentals=0
    )


def block_specs(blocks, backward):
    def spec(shape, kind):
        if kind == "whole":
            return pl.BlockSpec(shape, lambda i: (0,) * len(shape))
        if kind == "lanes":
            block = (shape[0], shape[1] // blocks)
            return pl.BlockSpec(block, (lambda i: (0, blocks - 1 - i)) if backward else (lambda i: (0, i)))
        block = (shape[0] // blocks, shape[1])
        return pl.BlockSpec(block, (lambda i: (blocks - 1 - i, 0)) if backward else (lambda i: (i, 0)))

    return spec


def call(body, blocks, ins, outs, scratch, backward, name, micros):
    spec = block_specs(blocks, backward)
    return pl.pallas_call(
        body,
        grid=(blocks,),
        in_specs=[spec(a.shape, kind) for a, kind in ins],
        out_specs=[spec(shape, kind) for shape, _, kind in outs],
        out_shape=[jax.ShapeDtypeStruct(shape, dtype) for shape, dtype, _ in outs],
        scratch_shapes=scratch,
        compiler_params=pltpu.CompilerParams(
            dimension_semantics=("arbitrary",), vmem_limit_bytes=60 * 1024 * 1024
        ),
        cost_estimate=cost(micros),
        name=name,
    )(*[a for a, _ in ins])


def signal_all(groups):
    barrier = pltpu.get_barrier_semaphore()
    for axis, peers in groups:
        for peer in peers:
            pl.semaphore_signal(barrier, inc=1, device_id={axis: peer}, device_id_type=MESH)
    pl.semaphore_wait(barrier, sum(len(peers) for _, peers in groups))


def push(src, dst, send, recv, axis, peer):
    copy = pltpu.make_async_remote_copy(
        src_ref=src, dst_ref=dst, send_sem=send, recv_sem=recv, device_id={axis: peer},
        device_id_type=MESH,
    )
    copy.start()
    return copy


def span(start, size):
    return pl.ds(pl.multiple_of(start, size), size)


def split_dp(count):
    small = 1
    while 2 * small * 2 * small * 2 <= count:
        small *= 2
    return small, count // small


def hops(count):
    return [count // 2] + [k for k in range(1, count) if k != count // 2]


class Both:
    def __init__(self, *refs):
        self.refs = refs

    def __setitem__(self, index, value):
        for ref in self.refs:
            ref[index] = value


def front_step(ins, outs, late_outs, scratch, inner, blocks, collective_id, micros):
    nt = lax.axis_size("tensor")
    length = blocks * SPAN
    total_inner = float(inner * nt)

    def body(*refs):
        refs = list(refs)

        def take(n):
            out = refs[:n]
            del refs[:n]
            return out

        plain_in = take(len(ins))
        hidden_o, vpre_o, cv_o, spre_o, scv_o, z_o, ld_o, ldt_o, yn_o, sin_o = take(len(outs))
        gate_out = take(len(late_outs))
        plain_scratch = take(len(scratch))
        gate_s, cv_s, yn_s, gn_s, slots, send, recv = refs
        wo, chp = plain_in[9], plain_in[10]
        step = pl.program_id(0)
        me = lax.axis_index("tensor")

        def peer(k):
            return lax.rem(me + k, nt)

        def copy(k, b):
            return pltpu.make_async_remote_copy(
                src_ref=slots.at[me, b], dst_ref=slots.at[me, b], send_sem=send.at[k - 1, b],
                recv_sem=recv.at[k - 1, b], device_id={"tensor": peer(k)}, device_id_type=MESH,
            )

        @pl.when(step == 0)
        def _():
            signal_all([("tensor", [peer(k) for k in range(1, nt)])])

        @pl.when(step < blocks)
        def _():
            at = span(step * SPAN, SPAN)
            fwd_kernel(
                *plain_in, hidden_o, gate_s.at[at], vpre_o, Both(cv_o, cv_s.at[at]), spre_o, scv_o,
                z_o, ld_o, ldt_o, Both(yn_o, yn_s.at[at]), sin_o, gn_s.at[at], slots.at[me, step],
                *plain_scratch,
            )
            for k in range(1, nt):
                copy(k, step).start()

        @pl.when(step >= blocks)
        def _():
            b = step - blocks
            at = span(b * SPAN, SPAN)
            for k in range(1, nt):
                copy(k, b).wait()
            total = slots[0, b]
            for source in range(1, nt):
                total = total + slots[source, b]
            gate_kernel(
                total_inner, step == blocks, gate_s.at[at], cv_s.at[at], yn_s.at[at], gn_s.at[at],
                total, chp, wo, *gate_out,
            )

    def spec(shape, kind, late):
        if kind == "whole":
            return pl.BlockSpec(shape, lambda i: (0,) * len(shape))

        def at(i):
            return (i // blocks) * (i - blocks) if late else i - (i // blocks) * (i - blocks + 1)

        if kind == "lanes":
            return pl.BlockSpec((shape[0], shape[1] // blocks), lambda i: (0, at(i)))
        return pl.BlockSpec((shape[0] // blocks, shape[1]), lambda i: (at(i), 0))

    dma = pltpu.SemaphoreType.DMA
    full = pltpu.VMEM((length, inner), F32)
    return pl.pallas_call(
        body,
        grid=(2 * blocks,),
        in_specs=[spec(a.shape, kind, False) for a, kind in ins],
        out_specs=[spec(shape, kind, False) for shape, _, kind in outs]
        + [spec(shape, kind, True) for shape, _, kind in late_outs],
        out_shape=[jax.ShapeDtypeStruct(shape, dtype) for shape, dtype, _ in outs + late_outs],
        scratch_shapes=scratch
        + [
            full, full, full, full, pltpu.VMEM((nt, blocks, 8, SPAN), F32), dma((nt - 1, blocks)),
            dma((nt - 1, blocks)),
        ],
        compiler_params=pltpu.CompilerParams(
            dimension_semantics=("arbitrary",), collective_id=collective_id, has_side_effects=True,
            vmem_limit_bytes=60 * 1024 * 1024,
        ),
        cost_estimate=cost(micros),
        name="front_scan",
    )(*[a for a, _ in ins])


def bwd_step(
    ins, outs, scratch, mixed, hidden, gate_low, cotangent, normal, blocks, collective_id, micros
):
    nt, nd = lax.axis_size("tensor"), lax.axis_size("dp")
    chips = nt // 2
    nx, nz = split_dp(nd)
    length, width = mixed.shape
    inner = gate_low.shape[1]
    half = length // 2
    rows, cols = width // nd, 2 * inner
    order = hops(nz)
    inside = nz - 2
    per = -(-inside // (blocks - 1))

    def body(*refs):
        refs = list(refs)

        def take(n):
            out = refs[:n]
            del refs[:n]
            return out

        plain_in = take(len(ins))
        mixed_h, hid_h, low_h, cot_h, nor_h = take(5)
        plain_out = take(len(outs))
        sum_o, last_o, half_o, far_o = take(4)
        plain_scratch = take(len(scratch))
        mine, near, mix, hid, low, cot, nor, dw, xslot, zsrc, zslot = take(11)
        loc, n_s, n_r, m_s, m_r, x_s, x_r, z_s, z_r = refs
        step = pl.program_id(0)
        me, md = lax.axis_index("tensor"), lax.axis_index("dp")
        side, chip = lax.rem(me, 2), me // 2
        x, z = lax.rem(md, nx), md // nx

        def remote(src, dst, send, recv, axis, peer):
            return pltpu.make_async_remote_copy(
                src_ref=src, dst_ref=dst, send_sem=send, recv_sem=recv, device_id={axis: peer},
                device_id_type=MESH,
            )

        def mate(q):
            return 2 * lax.rem(chip + q, chips) + side

        def x_peer(q):
            return z * nx + lax.rem(x + q, nx)

        def z_peer(k):
            return lax.rem(z + k, nz) * nx + x

        def mix_copy(q):
            return remote(mix, far_o.at[q - 1], m_s.at[q - 1], m_r.at[q - 1], "tensor", mate(q))

        def x_copy(q, p):
            return remote(
                dw.at[p, lax.rem(x + q, nx)], xslot.at[q - 1, p], x_s.at[q - 1, p],
                x_r.at[q - 1, p], "dp", x_peer(q),
            )

        def z_copy(p):
            return remote(
                zsrc.at[p], zslot.at[p], z_s.at[p], z_r.at[p], "dp", z_peer(order[p])
            )

        def gather_piece(p):
            for q in range(1, nx):
                x_copy(q, p).wait_recv()
            total = dw[p, x].astype(F32)
            for q in range(1, nx):
                total = total + xslot[q - 1, p].astype(F32)
            return total

        @pl.when(step == 0)
        def _():
            sibling = 2 * chip + 1 - side
            pairs = [
                (hid_h, hid), (low_h, low), (cot_h, cot), (nor_h, nor),
                (mixed_h.at[span(side * half, half)], mine),
            ]
            fetched = [
                pltpu.make_async_copy(src, dst, loc.at[n]) for n, (src, dst) in enumerate(pairs)
            ]
            for copy in fetched:
                copy.start()
            signal_all([
                ("tensor", [sibling] + [mate(q) for q in range(1, chips)]),
                ("dp", [x_peer(q) for q in range(1, nx)] + [z_peer(k) for k in range(1, nz)]),
            ])
            near_copy = remote(
                mixed_h.at[span((1 - side) * half, half)], near, n_s.at[0], n_r.at[0], "tensor",
                sibling,
            )
            near_copy.start()
            for copy in fetched[:4]:
                copy.wait()
            for p in range(nz):
                at = span(lax.rem(z + (order + [0])[p], nz) * (nx * rows), nx * rows)
                left = t_mm(hid[:, at], low[...]).astype(BF16)
                right = t_mm(cot[:, at], nor[...]).astype(BF16)
                for k in range(nx):
                    dw[p, k, :, :inner] = left[k * rows : (k + 1) * rows]
                    dw[p, k, :, inner:] = right[k * rows : (k + 1) * rows]
                for q in range(1, nx):
                    x_copy(q, p).start()
                if p == 0:
                    fetched[4].wait()
                    near_copy.wait_recv()
                    both = (mine[...].astype(F32) + near[...].astype(F32)).astype(BF16)
                    mix[...] = both
                    half_o[...] = both
                    for q in range(1, chips):
                        mix_copy(q).start()
            near_copy.wait_send()

        for s in range(1, blocks):

            @pl.when(step == s)
            def _(s=s):
                for p in range((s - 1) * per, min(s * per, inside)):
                    zsrc[p] = gather_piece(p).astype(BF16)
                    z_copy(p).start()

        bwd_kernel(*plain_in, *plain_out, *plain_scratch)

        @pl.when(step == blocks - 1)
        def _():
            last_o[...] = gather_piece(nz - 2).astype(BF16)
            total = gather_piece(nz - 1)
            for p in range(inside):
                z_copy(p).wait_recv()
                total = total + zslot[p].astype(F32)
            sum_o[...] = total
            for q in range(1, chips):
                mix_copy(q).wait()
            for p in range(inside):
                z_copy(p).wait_send()
            for p in range(nz):
                for q in range(1, nx):
                    x_copy(q, p).wait_send()

    spec = block_specs(blocks, True)
    hbm = pl.BlockSpec(memory_space=pl.ANY)
    dma = pltpu.SemaphoreType.DMA
    return pl.pallas_call(
        body,
        grid=(blocks,),
        in_specs=[spec(a.shape, kind) for a, kind in ins] + [hbm] * 5,
        out_specs=[spec(shape, kind) for shape, _, kind in outs]
        + [spec((rows, cols), "whole")] * 2
        + [spec((half, width), "whole"), hbm],
        out_shape=[jax.ShapeDtypeStruct(shape, dtype) for shape, dtype, _ in outs]
        + [
            jax.ShapeDtypeStruct((rows, cols), F32),
            jax.ShapeDtypeStruct((rows, cols), BF16),
            jax.ShapeDtypeStruct((half, width), BF16),
            jax.ShapeDtypeStruct((chips - 1, half, width), BF16),
        ],
        scratch_shapes=scratch
        + [
            pltpu.VMEM((half, width), BF16),
            pltpu.VMEM((half, width), BF16),
            pltpu.VMEM((half, width), BF16),
            pltpu.VMEM((length, width), BF16),
            pltpu.VMEM((length, inner), BF16),
            pltpu.VMEM((length, width), BF16),
            pltpu.VMEM((length, inner), BF16),
            pltpu.VMEM((nz, nx, rows, cols), BF16),
            pltpu.VMEM((nx - 1, nz, rows, cols), BF16),
            pltpu.VMEM((inside, rows, cols), BF16),
            pltpu.VMEM((inside, rows, cols), BF16),
            dma((5,)), dma((1,)), dma((1,)), dma((chips - 1,)), dma((chips - 1,)), dma((nx - 1, nz)), dma((nx - 1, nz)),
            dma((inside,)), dma((inside,)),
        ],
        compiler_params=pltpu.CompilerParams(
            dimension_semantics=("arbitrary",), collective_id=collective_id, has_side_effects=True,
            vmem_limit_bytes=60 * 1024 * 1024,
        ),
        cost_estimate=cost(micros),
        name="bwd_scan",
    )(*[a for a, _ in ins], mixed, hidden, gate_low, cotangent, normal)


def finish_kernel(
    heads, result, gtok, gate_out, last, value_step, shared, early, late,
    result_o, gtok_o, dgate_o, dvalue_o, dshared_o, dstep_o, dout_o,
    convv_o, biasv_o, convs_o, biass_o, h0_o, h1_o, h2_o, gain_o, norm_o,
):
    inner = dgate_o.shape[1]
    result_o[...] = result[...]
    gtok_o[...] = gtok[...]

    @pl.when(pl.program_id(0) == 0)
    def _():
        dgate_o[...] = gate_out[:, :inner] + last[:, :inner].astype(F32)
        dout_o[...] = gate_out[:, inner:] + last[:, inner:].astype(F32)
        dvalue_o[...] = value_step[:, :inner]
        dstep_o[...] = jnp.transpose(value_step[:, inner : inner + LANES])[:heads, :]
        dshared_o[...] = shared[...]
        convv_o[...] = early[0:4, :inner]
        biasv_o[...] = early[4:5, :inner]
        gain_o[...] = early[5:6, :inner]
        h0_o[...] = early[0:1, inner : inner + heads]
        h1_o[...] = early[1:2, inner : inner + heads]
        h2_o[...] = early[2:3, inner : inner + heads]
        convs_o[...] = late[0:4, :]
        biass_o[...] = late[4:5, :]
        norm_o[...] = late[5:6, : norm_o.shape[1]]


def tail_step(
    heads_part, dbc_part, hidden, value_low, step_low, shared_conv, shared_pre, aux, tokens, cotangent,
    ng, shared_proj, shp, mixed_half, mixed_far, last, ch_grads, head_grads, gain_part,
    collective_id, micros,
):
    length, width = tokens.shape
    inner = value_low.shape[1]
    shared_width = shared_proj.shape[1]
    nt, nd = lax.axis_size("tensor"), lax.axis_size("dp")
    ng_chips = nt // 2
    nx, nz = split_dp(nd)
    rows = width // nd
    quarter, half = length // nt, length // 2
    piece = quarter // PIECES
    part = nz * rows
    low_width = inner + LANES
    norm_width = width // nt
    early_width = inner + LANES
    late_width = shared_width
    blocks = length // SPAN
    chunk = 256
    path = hops(nz) + [0]
    n_mixed = ng_chips - 1
    n_late = 9 + n_mixed

    def body(*refs):
        refs = list(refs)

        def take(n):
            out = refs[:n]
            del refs[:n]
            return out

        heads_r, dbc, aux_r, ng_r, ws, shp_r, chg, hg, gain = take(9)
        hid_h, vlow_h, slow_h, scv_h, spre_h, tok_h, cot_h, mix_h, mixfar_h, last_h = take(10)
        result_o, gtok_o, value_o, shared_o, early_o, late_o, last_o = take(7)
        hid, low, scv, spre, tokh, tokq, cotq, mix, mixfar = take(9)
        (
            dnear, dslots, dtot, dbuf, shlow, hnear, fsrc, ffar, hacc, vbuf, vslot, sbuf, sslot,
            zv, zvslot, zs, zsslot, eslots, lslots, nbuf, nslot,
        ) = take(21)
        (
            loc, a_s, a_r, d_s, d_r, n_s, n_r, f_s, f_r, g_s, g_r, h_s, h_r, r_s, r_r,
            zv_s, zv_r, zs_s, zs_r, xv_s, xv_r, w_s, w_r, xs_s, xs_r, e_s, e_r, l_s, l_r, m_s, m_r,
        ) = take(31)

        me = lax.axis_index("tensor")
        side, chip = lax.rem(me, 2), me // 2
        sibling = 2 * chip + 1 - side
        md = lax.axis_index("dp")
        x, z = lax.rem(md, nx), md // nx

        def chip_at(q):
            return lax.rem(chip + q, ng_chips)

        def mate(q):
            return 2 * chip_at(q) + side

        def x_peer(q):
            return z * nx + lax.rem(x + q, nx)

        def z_peer(k):
            return lax.rem(z + k, nz) * nx + x

        count = [0]

        def fetch(src, dst):
            copy = pltpu.make_async_copy(src, dst, loc.at[count[0]])
            count[0] += 1
            copy.start()
            return copy

        my_rows = span(me * quarter, quarter)
        my_half = span(side * half, half)
        sib_half = span((1 - side) * half, half)
        got_low = [
            fetch(hid_h, hid), fetch(vlow_h, low.at[:, 0:inner]),
            fetch(slow_h, low.at[:, inner : inner + LANES]),
        ]
        got_mix = [fetch(mix_h, mix), fetch(tok_h.at[my_half], tokh)]
        got_mix += [fetch(mixfar_h.at[q], mixfar.at[q]) for q in range(n_mixed)]
        got_shared = [fetch(scv_h, scv), fetch(spre_h, spre)]
        got_end = [fetch(tok_h.at[my_rows], tokq), fetch(cot_h.at[my_rows], cotq)]

        signal_all([
            ("tensor", [lax.rem(me + k, nt) for k in range(1, nt)]),
            ("dp", [lax.rem(md + k, nd) for k in range(1, nd)]),
        ])
        sent = []

        def send(*args):
            copy = push(*args)
            sent.append(copy)
            return copy

        dn = send(dbc.at[sib_half], dnear, a_s.at[0], a_r.at[0], "tensor", sibling)
        last_copy = send(last_h, last_o, w_s.at[0], w_r.at[0], "dp", z_peer(path[nz - 2]))
        order = list(range(1, ng_chips)) + [0]
        near = {}
        for q in order:
            for p in range(PIECES):
                at = (2 * chip_at(q) + 1 - side) * quarter + p * piece
                near[q, p] = send(
                    heads_r.at[span(at, piece)], hnear.at[q, p], n_s.at[q, p], n_r.at[q, p],
                    "tensor", sibling,
                )
        eslots[md, :, :inner] = jnp.concatenate(
            [chg[0:5, :], gain[0:1, :], jnp.zeros((2, inner), F32)], axis=0
        )
        eslots[md, :, inner:] = hg[...]

        dn.wait_recv()
        dslots[chip] = (dbc[my_half, :] + dnear[...]).astype(BF16)
        dmates = [
            send(dslots.at[chip], dslots.at[chip], d_s.at[q], d_r.at[q], "tensor", mate(q))
            for q in range(1, ng_chips)
        ]
        fwd = {}
        for q in order:
            for p in range(PIECES):
                near[q, p].wait_recv()
                at = (2 * chip_at(q) + side) * quarter + p * piece
                both = heads_r[span(at, piece), :].astype(F32) + hnear[q, p].astype(F32)
                if q:
                    fsrc[q, p] = both.astype(BF16)
                    fwd[q, p] = send(
                        fsrc.at[q, p], ffar.at[q, p], f_s.at[q, p], f_r.at[q, p], "tensor", mate(q)
                    )
                else:
                    hacc[p * piece : (p + 1) * piece, :] = both
        es = [
            send(
                eslots.at[md], eslots.at[md], e_s.at[k], e_r.at[k], "dp", lax.rem(md + k, nd)
            )
            for k in range(1, nd)
        ]

        for copy in got_low:
            copy.wait()
        xvs = {}
        for p in range(nz):
            cols = span(lax.rem(z + path[p], nz) * (nx * rows), nx * rows)
            prod = t_mm(hid[:, cols], low[...]).astype(BF16)
            for k in range(nx):
                vbuf[p, k] = prod[k * rows : (k + 1) * rows]
            for q in range(1, nx):
                xvs[q, p] = send(
                    vbuf.at[p, lax.rem(x + q, nx)], vslot.at[q - 1, p], xv_s.at[q - 1, p],
                    xv_r.at[q - 1, p], "dp", x_peer(q),
                )
        zvs = []

        def own_piece(p):
            total = vbuf[p, x].astype(F32)
            for q in range(1, nx):
                xvs[q, p].wait_recv()
                total = total + vslot[q - 1, p].astype(F32)
            return total

        def pass_on(p):
            zv[p] = own_piece(p).astype(BF16)
            zvs.append(
                send(zv.at[p], zvslot.at[p], zv_s.at[p], zv_r.at[p], "dp", z_peer(path[p]))
            )

        for copy in got_shared:
            copy.wait()
        for copy in dmates:
            copy.wait_recv()
        total = dslots[0].astype(F32)
        for g in range(1, ng_chips):
            total = total + dslots[g].astype(F32)
        dtot[my_half, :] = total
        dt_copy = send(
            dtot.at[my_half], dtot.at[my_half], a_s.at[1], a_r.at[1], "tensor", sibling
        )

        pass_on(0)
        for copy in got_mix:
            copy.wait()
        mixed = mix[...].astype(F32)
        if n_mixed == 1:
            mixed = mixed + mixfar[0].astype(F32)
        else:
            terms = [mix] + [mixfar.at[q] for q in range(n_mixed)]
            mixed = jnp.zeros((half, width), F32)
            for g in range(ng_chips):
                for q in range(ng_chips):
                    mine = (lax.rem(chip - q + ng_chips, ng_chips) == g).astype(F32)
                    mixed = mixed + terms[q][...].astype(F32) * mine
        result_o[my_half, :] = (tokh[...].astype(F32) + mixed).astype(BF16)
        res = send(
            result_o.at[my_half], result_o.at[my_half], r_s.at[0], r_r.at[0], "tensor", sibling
        )

        if nz > 2:
            pass_on(1)
        dt_copy.wait_recv()
        dbuf[length : length + 8, :] = jnp.zeros((8, shared_width), F32)
        sums = [jnp.zeros((1, shared_width), F32)] * 5
        for b in reversed(range(blocks)):
            base = b * SPAN
            at = slice(base, base + SPAN)
            sc = scv[at, :]
            csig = sigmoid(sc)
            dcv = dtot[at, :] * (csig * (1.0 + sc * (1.0 - csig)))
            dbuf[at, :] = dcv
            sp = spre[at, :]
            mask = aux_r[at, :]
            ds = dcv * shp_r[3:4, :]
            sums[3] = sums[3] + jnp.sum(dcv * sp, axis=0, keepdims=True)
            sums[4] = sums[4] + jnp.sum(dcv, axis=0, keepdims=True)
            for j in range(1, 4):
                moved = dbuf[base + j : base + j + SPAN, :] * mask[:, 8 + j : 9 + j]
                ds = ds + moved * shp_r[3 - j : 4 - j, :]
                sums[3 - j] = sums[3 - j] + jnp.sum(moved * sp, axis=0, keepdims=True)
            shlow[at, :] = ds.astype(BF16)
        for p in range(2, nz - 1):
            pass_on(p)
        for c in range(width // chunk):
            prod = t_mm(hid[:, c * chunk : (c + 1) * chunk], shlow[...]).astype(BF16)
            for d in range(c * chunk // rows, (c + 1) * chunk // rows):
                at = slice(d * rows - c * chunk, (d + 1) * rows - c * chunk)
                sbuf[d % nx, (d // nx) * rows : (d // nx + 1) * rows, :] = prod[at]
        xss = [
            send(
                sbuf.at[lax.rem(x + q, nx)], sslot.at[q], xs_s.at[q], xs_r.at[q], "dp", x_peer(q)
            )
            for q in range(1, nx)
        ]
        hacc[...] = hacc[...] + mm_t(shlow[my_rows, :], ws[...])

        for copy in got_end:
            copy.wait()
        norm = jnp.zeros((1, width), F32)
        gather, own = {}, []
        for p in range(PIECES):
            at = slice(p * piece, (p + 1) * piece)
            grad_hidden = hacc[at, :]
            for q in range(1, ng_chips):
                fwd[q, p].wait_recv()
                grad_hidden = grad_hidden + ffar[q, p].astype(F32)
            v = tokq[at, :].astype(F32)
            inv = lax.rsqrt(jnp.mean(v * v, axis=1, keepdims=True) + EPSILON)
            normed = v * inv
            scaled = grad_hidden * ng_r[...]
            norm = norm + jnp.sum(grad_hidden * normed, axis=0, keepdims=True)
            mean = jnp.mean(scaled * normed, axis=1, keepdims=True)
            place = span(me * quarter + p * piece, piece)
            gtok_o[place, :] = (inv * (scaled - normed * mean) + cotq[at, :].astype(F32)).astype(BF16)
            for q in range(1, ng_chips):
                gather[q, p] = send(
                    gtok_o.at[place], gtok_o.at[place], g_s.at[q, p], g_r.at[q, p], "tensor", mate(q)
                )
            own.append(
                send(gtok_o.at[place], gtok_o.at[place], h_s.at[0, p], h_r.at[0, p], "tensor", sibling)
            )
        for q in range(nt):
            nbuf[q] = norm[:, q * norm_width : (q + 1) * norm_width] + jnp.zeros((8, norm_width), F32)
        norms = [
            send(
                nbuf.at[lax.rem(me + k, nt)], nslot.at[k], m_s.at[k], m_r.at[k], "tensor",
                lax.rem(me + k, nt),
            )
            for k in range(1, nt)
        ]

        for copy in xss:
            copy.wait_recv()
        total = sbuf[x].astype(F32)
        for q in range(1, nx):
            total = total + sslot[q].astype(F32)
        zs[...] = total.astype(BF16)
        zss = [
            send(
                zs.at[span(lax.rem(z + k, nz) * rows, rows)], zsslot.at[k], zs_s.at[k], zs_r.at[k],
                "dp", z_peer(k),
            )
            for k in range(1, nz)
        ]

        for copy in norms:
            copy.wait_recv()
        total = nbuf[me]
        for k in range(1, nt):
            total = total + nslot[k]
        wide = jnp.concatenate(
            [total[0:1, :], jnp.zeros((1, shared_width - norm_width), F32)], axis=1
        ) if norm_width < shared_width else total[0:1, :]
        lslots[md] = jnp.concatenate(sums + [wide, jnp.zeros((2, shared_width), F32)], axis=0)
        ls = [
            send(
                lslots.at[md], lslots.at[md], l_s.at[k], l_r.at[k], "dp", lax.rem(md + k, nd)
            )
            for k in range(1, nd)
        ]

        for copy in es:
            copy.wait_recv()
        total = eslots[0]
        for s in range(1, nd):
            total = total + eslots[s]
        early_o[...] = total

        for p in range(PIECES):
            for q in range(1, ng_chips):
                gather[q, p].wait_recv()
                came = 2 * lax.rem(chip - q + ng_chips, ng_chips) + side
                place = span(came * quarter + p * piece, piece)
                own.append(
                    send(
                        gtok_o.at[place], gtok_o.at[place], h_s.at[q, p], h_r.at[q, p],
                        "tensor", sibling,
                    )
                )

        for copy in zvs:
            copy.wait_recv()
        total = own_piece(nz - 1)
        for p in range(nz - 1):
            total = total + zvslot[p].astype(F32)
        value_o[...] = total
        for copy in zss:
            copy.wait_recv()
        total = zs[span(z * rows, rows), :].astype(F32)
        for k in range(1, nz):
            total = total + zsslot[k].astype(F32)
        shared_o[...] = total

        for copy in ls:
            copy.wait_recv()
        total = lslots[0]
        for s in range(1, nd):
            total = total + lslots[s]
        late_o[...] = total

        res.wait_recv()
        last_copy.wait_recv()
        for copy in own:
            copy.wait_recv()
        for copy in sent:
            copy.wait_send()

    vm = pl.BlockSpec(memory_space=pltpu.VMEM)
    hbm = pl.BlockSpec(memory_space=pl.ANY)
    dma = pltpu.SemaphoreType.DMA

    def f32(*shape):
        return pltpu.VMEM(shape, F32)

    def bf16(*shape):
        return pltpu.VMEM(shape, BF16)

    def out(*shape):
        return jax.ShapeDtypeStruct(shape, F32)

    early = [heads_part, dbc_part, aux, ng, shared_proj, shp, ch_grads, head_grads, gain_part]
    late = [hidden, value_low, step_low, shared_conv, shared_pre, tokens, cotangent, mixed_half]
    late += [mixed_far, last]
    return pl.pallas_call(
        body,
        in_specs=[vm] * len(early) + [hbm] * len(late),
        out_specs=[vm] * 6 + [hbm],
        out_shape=[
            jax.ShapeDtypeStruct((length, width), BF16), jax.ShapeDtypeStruct((length, width), BF16),
            out(rows, low_width), out(rows, shared_width), out(8, early_width), out(8, late_width),
            jax.ShapeDtypeStruct(last.shape, last.dtype),
        ],
        scratch_shapes=[
            bf16(length, width), bf16(length, low_width), f32(length, shared_width),
            f32(length, shared_width), bf16(half, width), bf16(quarter, width), bf16(quarter, width),
            bf16(half, width), bf16(n_mixed, half, width),
            f32(half, shared_width), bf16(ng_chips, half, shared_width), f32(length, shared_width),
            f32(length + 8, shared_width), bf16(length, shared_width),
            bf16(ng_chips, PIECES, piece, width), bf16(ng_chips, PIECES, piece, width),
            bf16(ng_chips, PIECES, piece, width), f32(quarter, width),
            bf16(nz, nx, rows, low_width), bf16(nx - 1, nz, rows, low_width),
            bf16(nx, part, shared_width), bf16(nx, part, shared_width),
            bf16(nz - 1, rows, low_width), bf16(nz - 1, rows, low_width),
            bf16(part, shared_width), bf16(nz, rows, shared_width),
            f32(nd, 8, early_width), f32(nd, 8, late_width),
            f32(nt, 8, norm_width), f32(nt, 8, norm_width),
        ]
        + [dma((n_late + 1,)), dma((2,)), dma((2,)), dma((ng_chips,)), dma((ng_chips,))]
        + [dma((ng_chips, PIECES))] * 8
        + [dma((1,)), dma((1,))]
        + [dma((nz,))] * 4
        + [dma((nx - 1, nz))] * 2
        + [dma((1,))] * 2
        + [dma((nx,))] * 2
        + [dma((nd,))] * 4
        + [dma((nt,))] * 2,
        compiler_params=pltpu.CompilerParams(
            collective_id=collective_id, has_side_effects=True, vmem_limit_bytes=60 * 1024 * 1024
        ),
        cost_estimate=cost(micros),
        name="tail_step",
    )(*early, *late)


def per_device(
    tokens, cotangent, segments, norm_gain, gate_proj, value_proj, shared_proj, step_proj,
    conv_value, bias_value, conv_shared, bias_shared, step_bias, decay_log, skip_gain,
    gate_gain, out_proj,
):
    tp_count = lax.axis_size("tensor")
    dp_count = lax.axis_size("dp")
    length, width = tokens.shape
    inner = gate_proj.shape[1]
    heads = step_proj.shape[1]
    shared_width = shared_proj.shape[1]
    state_size = shared_width // 2
    blocks = length // SPAN
    aux, segr, wst, chp, shp, hp = pl.pallas_call(
        prep_kernel,
        out_shape=[
            jax.ShapeDtypeStruct((length, LANES), F32),
            jax.ShapeDtypeStruct((1, length), F32),
            jax.ShapeDtypeStruct((width, LANES), BF16),
            jax.ShapeDtypeStruct((8, inner), F32),
            jax.ShapeDtypeStruct((8, shared_width), F32),
            jax.ShapeDtypeStruct((8, LANES), F32),
        ],
        name="prep_step",
    )(
        segments, step_proj.T, conv_value, bias_value[None], gate_gain[None], skip_gain[None],
        conv_shared, bias_shared[None], step_bias[None], decay_log[None],
    )
    ng = norm_gain[None, :]

    (
        hidden, value_pre, conv_out, shared_pre, shared_conv, z, ld, ldt, yn, sin,
        normal_out, dy, gate_low, gain_part, mixed_part,
    ) = front_step(
        [
            (tokens, "rows"), (cotangent, "rows"), (aux, "rows"), (segr, "lanes"), (ng, "whole"),
            (gate_proj, "whole"), (value_proj, "whole"), (shared_proj, "whole"), (wst, "whole"),
            (out_proj, "whole"), (chp, "whole"), (shp, "whole"), (hp, "whole"),
        ],
        [
            ((length, width), BF16, "rows"),
            ((length, inner), F32, "rows"),
            ((length, inner), F32, "rows"),
            ((length, shared_width), F32, "rows"),
            ((length, shared_width), F32, "rows"),
            ((length, LANES), F32, "rows"),
            ((length, LANES), F32, "rows"),
            ((8, length), F32, "lanes"),
            ((length, inner), F32, "rows"),
            ((blocks * state_size, inner), F32, "rows"),
        ],
        [
            ((length, inner), BF16, "rows"),
            ((length, inner), F32, "rows"),
            ((length, inner), BF16, "rows"),
            ((8, inner), F32, "whole"),
            ((length, width), BF16, "rows"),
        ],
        [
            pltpu.VMEM((SPAN + 8, inner), F32),
            pltpu.VMEM((SPAN + 8, shared_width), F32),
            pltpu.VMEM((state_size, inner), F32),
        ],
        inner, blocks, 0, 29,
    )
    (
        value_low, step_low, heads_part, dbc_part, ch_grads, head_grads, gate_out, last, mixed_half,
        mixed_far,
    ) = bwd_step(
        [
            (dy, "rows"), (conv_out, "rows"), (value_pre, "rows"), (shared_conv, "rows"),
            (z, "rows"), (ld, "rows"), (ldt, "lanes"), (yn, "rows"), (sin, "rows"),
            (aux, "rows"), (segr, "lanes"), (gate_low, "rows"), (gate_proj, "whole"),
            (value_proj, "whole"), (wst, "whole"), (chp, "whole"), (hp, "whole"),
        ],
        [
            ((length, inner), BF16, "rows"),
            ((length, LANES), BF16, "rows"),
            ((length, width), BF16, "rows"),
            ((length, shared_width), F32, "rows"),
            ((8, inner), F32, "whole"),
            ((8, LANES), F32, "whole"),
        ],
        [pltpu.VMEM((SPAN + 8, inner), F32), pltpu.VMEM((state_size, inner), F32)],
        mixed_part, hidden, gate_low, cotangent, normal_out, blocks, 3, 30,
    )
    result, grad_tokens, value_step, shared_sum, early, late, last = tail_step(
        heads_part, dbc_part, hidden, value_low, step_low, shared_conv, shared_pre, aux, tokens,
        cotangent, ng, shared_proj, shp, mixed_half, mixed_far, last, ch_grads, head_grads,
        gain_part, 2, 40,
    )

    def finish_body(*refs):
        finish_kernel(heads, *refs)

    rows = width // dp_count
    (
        result, grad_tokens, dgate, dvalue, dshared, dstep, dout,
        convv, biasv, convs, biass, h0, h1, h2, gain, norm,
    ) = call(
        finish_body,
        blocks,
        [
            (result, "rows"), (grad_tokens, "rows"), (gate_out, "whole"), (last, "whole"),
            (value_step, "whole"),
            (shared_sum, "whole"), (early, "whole"), (late, "whole"),
        ],
        [
            ((length, width), BF16, "rows"), ((length, width), BF16, "rows"),
            ((rows, inner), F32, "whole"), ((rows, inner), F32, "whole"),
            ((rows, shared_width), F32, "whole"), ((heads, rows), F32, "whole"),
            ((rows, inner), F32, "whole"), ((4, inner), F32, "whole"), ((1, inner), F32, "whole"),
            ((4, shared_width), F32, "whole"), ((1, shared_width), F32, "whole"),
            ((1, heads), F32, "whole"), ((1, heads), F32, "whole"), ((1, heads), F32, "whole"),
            ((1, inner), F32, "whole"), ((1, width // tp_count), F32, "whole"),
        ],
        [],
        False,
        "finish_step",
        3,
    )
    return (
        result, grad_tokens, norm[0], dgate, dvalue, dshared, dstep.T, convv, biasv[0], convs, biass[0],
        h0[0], h1[0], h2[0], gain[0], dout,
    )


def solution(mesh):
    rows, cols, vec = P("dp", None), P(None, "tensor"), P("tensor")
    return jax.shard_map(
        per_device,
        mesh=mesh,
        in_specs=(
            rows, rows, rows, P(), cols, cols, P(), cols, cols, vec, P(), P(), vec, vec, vec, vec, cols,
        ),
        out_specs=(
            rows, rows, vec, P("dp", "tensor"), P("dp", "tensor"), rows, P("dp", "tensor"), cols, vec,
            P(), P(), vec, vec, vec, vec, P("dp", "tensor"),
        ),
        check_vma=False,
    )
```

```python
import jax
import jax.numpy as jnp
from jax import lax
from jax.experimental import pallas as pl
from jax.experimental.pallas import tpu as pltpu
from jax.sharding import PartitionSpec as P

SPAN = 256
HSIZE = 64
LANES = 128
EPSILON = 1e-05
NEG_FILL = -1e30
EXACT = lax.Precision.HIGHEST
F32 = jnp.float32
BF16 = jnp.bfloat16


def mm(left, right):
    return jnp.dot(left, right, preferred_element_type=F32)


def mm_t(left, right):
    return lax.dot_general(left, right, (((1,), (1,)), ((), ())), preferred_element_type=F32)


def t_mm(left, right):
    return lax.dot_general(left, right, (((0,), (0,)), ((), ())), preferred_element_type=F32)


def exact(left, right):
    return jnp.dot(left, right, precision=EXACT, preferred_element_type=F32)


def sigmoid(v):
    return 1.0 / (1.0 + jnp.exp(-v))


def spread(cols, pairs):
    low = lax.broadcasted_iota(jnp.int32, (cols.shape[0], LANES), 1) < HSIZE
    parts = [
        jnp.where(low, cols[:, 2 * p : 2 * p + 1], cols[:, 2 * p + 1 : 2 * p + 2])
        for p in range(pairs)
    ]
    return jnp.concatenate(parts, axis=1)


def gather_mat(inner):
    channel = lax.broadcasted_iota(jnp.int32, (inner, LANES), 0) // HSIZE
    head = lax.broadcasted_iota(jnp.int32, (inner, LANES), 1)
    return (channel == head).astype(F32)


def grid_masks():
    row = lax.broadcasted_iota(jnp.int32, (SPAN, SPAN), 0)
    col = lax.broadcasted_iota(jnp.int32, (SPAN, SPAN), 1)
    return row, col


def conv_fwd(buf, pack, aux):
    out = pack[4:5, :] + buf[8 : 8 + SPAN, :] * pack[3:4, :]
    for j in range(1, 4):
        out = out + buf[8 - j : 8 - j + SPAN, :] * (aux[:, j : j + 1] * pack[3 - j : 4 - j, :])
    return out


def fwd_kernel(
    tok, cot, aux_ref, segr, ng, wg, wv, ws, wst, wo, chp, shp, hp,
    hidden_o, gate_o, vpre_o, cv_o, spre_o, scv_o, z_o, ld_o, ldt_o, yn_o, sin_o, gn_o, stat_o,
    vbuf, sbuf, state,
):
    inner = wg.shape[1]
    pairs = inner // LANES
    state_size = ws.shape[1] // 2

    @pl.when(pl.program_id(0) == 0)
    def _():
        vbuf[0:8, :] = jnp.zeros((8, inner), F32)
        sbuf[0:8, :] = jnp.zeros((8, 2 * state_size), F32)
        state[...] = jnp.zeros_like(state)

    aux = aux_ref[...]
    x = tok[...].astype(F32)
    inv = lax.rsqrt(jnp.mean(x * x, axis=1, keepdims=True) + EPSILON)
    hid = (x * inv * ng[...]).astype(BF16)
    hidden_o[...] = hid
    gate = mm(hid, wg[...])
    gate_o[...] = gate
    vp = mm(hid, wv[...])
    vpre_o[...] = vp
    vbuf[8 : 8 + SPAN, :] = vp
    sp = mm(hid, ws[...])
    spre_o[...] = sp
    sbuf[8 : 8 + SPAN, :] = sp
    z = mm(hid, wst[...]) + hp[0:1, :]
    z_o[...] = z
    gn = mm(cot[...], wo[...])
    gn_o[...] = gn
    scv = conv_fwd(sbuf, shp, aux)
    scv_o[...] = scv
    bc = (scv * sigmoid(scv)).astype(BF16)
    b_low, c_low = bc[:, :state_size], bc[:, state_size:]
    cv = conv_fwd(vbuf, chp, aux)
    cv_o[...] = cv
    vbuf[0:8, :] = vbuf[SPAN : SPAN + 8, :]
    sbuf[0:8, :] = sbuf[SPAN : SPAN + 8, :]
    values = cv * sigmoid(cv)
    dt = jnp.maximum(z, 0.0) + jnp.log1p(jnp.exp(-jnp.abs(z)))
    row, col = grid_masks()
    tri = (row >= col).astype(F32)
    ld = exact(tri, dt * hp[1:2, :])
    ld_o[...] = ld
    ldt = jnp.transpose(ld)[0:8, :]
    ldt_o[...] = ldt
    allowed = (row >= col) & (aux[:, 0:1] == segr[...])
    scores = jnp.where(allowed, mm_t(c_low, b_low), 0.0)
    xs = values * spread(dt, pairs)
    xs_low = xs.astype(BF16)
    ein = jnp.exp(ld) * aux[:, 4:5]
    eout = jnp.exp(ld[SPAN - 1 : SPAN, :] - ld) * aux[:, 5:6]
    ein_x = spread(ein, pairs)
    eout_x = spread(eout, pairs)
    old = state[...]
    sin_o[...] = old
    carried = mm(c_low, old.astype(BF16)) * ein_x
    state[...] = old * ein_x[SPAN - 1 : SPAN, :] + t_mm(b_low, (xs * eout_x).astype(BF16))
    low = lax.broadcasted_iota(jnp.int32, (SPAN, LANES), 1) < HSIZE
    parts = []
    for p in range(pairs):
        pair = xs_low[:, p * LANES : (p + 1) * LANES]
        outs = []
        for h in (2 * p, 2 * p + 1):
            gap = jnp.minimum(ld[:, h : h + 1] - ldt[h : h + 1, :], 0.0)
            outs.append(mm((jnp.exp(gap) * scores).astype(BF16), pair))
        parts.append(jnp.where(low, outs[0], outs[1]))
    yn = jnp.concatenate(parts, axis=1) + carried
    yn_o[...] = yn
    gated = (yn + chp[6:7, :] * values) * (gate * sigmoid(gate))
    squares = jnp.sum(gated * gated, axis=1, keepdims=True)
    dots = jnp.sum(gn * chp[5:6, :] * gated, axis=1, keepdims=True)
    lane = lax.broadcasted_iota(jnp.int32, (SPAN, LANES), 1)
    both = jnp.where(lane == 0, squares, jnp.where(lane == 1, dots, 0.0))
    stat_o[...] = jnp.transpose(both)[0:8, :]


def gate_kernel(
    width, first, gate_ref, cv_ref, yn, gn_ref, stat, chp, wo, normal_o, dy_o, low_o, gain_o, mixed_o
):
    both = jnp.transpose(jnp.concatenate([stat[...]] * (LANES // 8), axis=0))
    inv = lax.rsqrt(both[:, 0:1] / width + EPSILON)
    mean_dots = both[:, 1:2] / width
    gate = gate_ref[...]
    cv = cv_ref[...]
    gn = gn_ref[...]
    sig = sigmoid(gate)
    act = gate * sig
    mixer = yn[...] + chp[6:7, :] * (cv * sigmoid(cv))
    gated = mixer * act
    normed = gated * inv
    normal = (normed * chp[5:6, :]).astype(BF16)
    normal_o[...] = normal
    mixed_o[...] = mm_t(normal, wo[...]).astype(BF16)
    part = jnp.sum(gn * normed, axis=0, keepdims=True)

    @pl.when(first)
    def _():
        gain_o[...] = jnp.zeros_like(gain_o)

    gain_o[0:1, :] += part
    grad_gated = inv * (gn * chp[5:6, :]) - gated * (inv * inv * inv) * mean_dots
    dy_o[...] = grad_gated * act
    low_o[...] = (grad_gated * mixer * (sig * (1.0 + gate * (1.0 - sig)))).astype(BF16)


def bwd_kernel(
    dy_ref, cv_ref, vpre, scv_ref, z_ref, ld_ref, ldt_ref, yn, sin, aux_ref, segr, glow,
    wg, wv, wst, chp, hp,
    vlow_o, slow_o, heads_o, dbc_o, chg_o, hg_o,
    dbuf, dstate,
):
    inner = wg.shape[1]
    pairs = inner // LANES
    state_size = sin.shape[0]

    @pl.when(pl.program_id(0) == 0)
    def _():
        dbuf[SPAN : SPAN + 8, :] = jnp.zeros((8, inner), F32)
        dstate[...] = jnp.zeros_like(dstate)
        chg_o[...] = jnp.zeros_like(chg_o)
        hg_o[...] = jnp.zeros_like(hg_o)

    aux = aux_ref[...]
    dy = dy_ref[...]
    dy_low = dy.astype(BF16)
    scv = scv_ref[...]
    bc = (scv * sigmoid(scv)).astype(BF16)
    b_low, c_low = bc[:, :state_size], bc[:, state_size:]
    cv = cv_ref[...]
    csig = sigmoid(cv)
    values = cv * csig
    z = z_ref[...]
    dt = jnp.maximum(z, 0.0) + jnp.log1p(jnp.exp(-jnp.abs(z)))
    ld = ld_ref[...]
    ldt = ldt_ref[...]
    dt_x = spread(dt, pairs)
    xs = values * dt_x
    xs_low = xs.astype(BF16)
    ein = jnp.exp(ld) * aux[:, 4:5]
    eout = jnp.exp(ld[SPAN - 1 : SPAN, :] - ld) * aux[:, 5:6]
    ein_x = spread(ein, pairs)
    eout_x = spread(eout, pairs)
    row, col = grid_masks()
    allowed = (col >= row) & (aux[:, 0:1] == segr[...])
    mask = allowed.astype(F32)
    scores_t = mm_t(b_low, c_low) * mask
    low = lax.broadcasted_iota(jnp.int32, (SPAN, LANES), 1) < HSIZE
    parts = []
    dscores_t = jnp.zeros((SPAN, SPAN), F32)
    for p in range(pairs):
        cols = slice(p * LANES, (p + 1) * LANES)
        dy_pair = dy_low[:, cols]
        xs_pair = xs_low[:, cols]
        zero = jnp.zeros_like(xs_pair)
        outs = []
        for side, h in enumerate((2 * p, 2 * p + 1)):
            gap = jnp.minimum(ldt[h : h + 1, :] - ld[:, h : h + 1], 0.0)
            decay = jnp.exp(gap)
            outs.append(mm((decay * scores_t).astype(BF16), dy_pair))
            mine = jnp.where(low, xs_pair, zero) if side == 0 else jnp.where(low, zero, xs_pair)
            dscores_t = dscores_t + mm_t(mine, dy_pair) * decay
        parts.append(jnp.where(low, outs[0], outs[1]))
    inside = jnp.concatenate(parts, axis=1)
    dscores_low = (dscores_t * mask).astype(BF16)
    old = sin[...]
    dst = dstate[...]
    dst_low = dst.astype(BF16)
    dye_low = (dy * ein_x).astype(BF16)
    xse_low = (xs * eout_x).astype(BF16)
    db = mm(dscores_low, c_low) + mm_t(xse_low, dst_low)
    dc = t_mm(dscores_low, b_low) + mm_t(dye_low, old.astype(BF16))
    late = mm(b_low, dst_low) * eout_x
    keep = ein_x[SPAN - 1 : SPAN, :]
    dstate[...] = dst * keep + t_mm(c_low, dye_low)
    dxs = inside + late
    collect = gather_mat(inner)
    q = dy_low.astype(F32) * yn[...] - xs_low.astype(F32) * inside
    u = xs * late
    kappa = exact(jnp.sum(old * dst, axis=0, keepdims=True) * keep + jnp.zeros((8, inner), F32), collect)
    da = (
        exact((col >= row).astype(F32), exact(q, collect))
        + exact((row > col).astype(F32), exact(u, collect))
        + kappa[0:1, :]
    )
    rates = hp[1:2, :]
    ddt = da * rates + exact(dxs * values, collect)
    dz = ddt * sigmoid(z)
    slow = dz.astype(BF16)
    slow_o[...] = slow
    skip = exact(jnp.sum(dy * values, axis=0, keepdims=True) + jnp.zeros((8, inner), F32), collect)
    hg_o[0:1, :] += jnp.sum(dz, axis=0, keepdims=True)
    hg_o[1:2, :] += jnp.sum(da * dt, axis=0, keepdims=True) * rates
    hg_o[2:3, :] += skip[0:1, :]
    dcv = (dxs * dt_x + chp[6:7, :] * dy) * (csig * (1.0 + cv * (1.0 - csig)))
    dbuf[0:SPAN, :] = dcv
    vp = vpre[...]
    dv = dcv * chp[3:4, :]
    chg_o[3:4, :] += jnp.sum(dcv * vp, axis=0, keepdims=True)
    chg_o[4:5, :] += jnp.sum(dcv, axis=0, keepdims=True)
    for j in range(1, 4):
        moved = dbuf[j : j + SPAN, :] * aux[:, 8 + j : 9 + j]
        dv = dv + moved * chp[3 - j : 4 - j, :]
        chg_o[3 - j : 4 - j, :] += jnp.sum(moved * vp, axis=0, keepdims=True)
    dbuf[SPAN : SPAN + 8, :] = dbuf[0:8, :]
    vlow = dv.astype(BF16)
    vlow_o[...] = vlow
    back = mm_t(glow[...], wg[...]) + mm_t(vlow, wv[...]) + mm_t(slow, wst[...])
    heads_o[...] = back.astype(BF16)
    dbc_o[...] = jnp.concatenate([db, dc], axis=1)


MESH = pl.DeviceIdType.MESH
PIECES = 4


def prep_kernel(
    seg, stepw, conv_v, bias_v, gate_g, skip_g, conv_s, bias_s, step_b, decay,
    aux_o, segr_o, wst_o, chp_o, shp_o, hp_o,
):
    length = seg.shape[1]
    ids = seg[...].astype(F32)
    segr_o[...] = ids
    wide = ids + jnp.zeros((8, length), F32)
    lane = lax.broadcasted_iota(jnp.int32, (8, length), 1)
    row = lax.broadcasted_iota(jnp.int32, (8, length), 0)
    ends = [
        ids[:, start + SPAN - 1 : start + SPAN] + jnp.zeros((8, SPAN), F32)
        for start in range(0, length, SPAN)
    ]
    last = jnp.concatenate(ends, axis=1)
    before = jnp.concatenate([jnp.full((8, SPAN), -1.0, F32)] + ends[:-1], axis=1)
    first = jnp.where(row == 0, wide, 0.0)
    first = jnp.where((row == 4) & (wide == before), 1.0, first)
    first = jnp.where((row == 5) & (wide == last), 1.0, first)
    second = jnp.zeros((8, length), F32)
    for j in range(1, 4):
        back = (pltpu.roll(wide, j, 1) == wide) & (lane >= j)
        ahead = (pltpu.roll(wide, length - j, 1) == wide) & (lane < length - j)
        first = jnp.where((row == j) & back, 1.0, first)
        second = jnp.where((row == j) & ahead, 1.0, second)
    rest = jnp.zeros((LANES - 16, length), F32)
    aux_o[...] = jnp.transpose(jnp.concatenate([first, second, rest], axis=0))
    heads, width = stepw.shape
    steps = jnp.concatenate([stepw[...].astype(F32), jnp.zeros((LANES - heads, width), F32)], axis=0)
    wst_o[...] = jnp.transpose(steps).astype(BF16)
    hp_o[...] = jnp.zeros_like(hp_o)
    hp_o[0:1, 0:heads] = step_b[...]
    hp_o[1:2, 0:heads] = -jnp.exp(decay[...])
    hp_o[2:3, 0:heads] = skip_g[...]
    inner = chp_o.shape[1]
    repeated = lax.dot_general(
        hp_o[...], gather_mat(inner), (((1,), (1,)), ((), ())), precision=EXACT,
        preferred_element_type=F32,
    )
    chp_o[0:4, :] = conv_v[...]
    chp_o[4:5, :] = bias_v[...]
    chp_o[5:6, :] = gate_g[...]
    chp_o[6:7, :] = repeated[2:3, :]
    chp_o[7:8, :] = jnp.zeros((1, inner), F32)
    shp_o[...] = jnp.zeros_like(shp_o)
    shp_o[0:4, :] = conv_s[...]
    shp_o[4:5, :] = bias_s[...]


def cost(micros):
    return pl.CostEstimate(
        flops=int(micros * 1e9), bytes_accessed=int(micros * 3.6e6), transcendentals=0
    )


def block_specs(blocks, backward):
    def spec(shape, kind):
        if kind == "whole":
            return pl.BlockSpec(shape, lambda i: (0,) * len(shape))
        if kind == "lanes":
            block = (shape[0], shape[1] // blocks)
            return pl.BlockSpec(block, (lambda i: (0, blocks - 1 - i)) if backward else (lambda i: (0, i)))
        block = (shape[0] // blocks, shape[1])
        return pl.BlockSpec(block, (lambda i: (blocks - 1 - i, 0)) if backward else (lambda i: (i, 0)))

    return spec


def call(body, blocks, ins, outs, scratch, backward, name, micros):
    spec = block_specs(blocks, backward)
    return pl.pallas_call(
        body,
        grid=(blocks,),
        in_specs=[spec(a.shape, kind) for a, kind in ins],
        out_specs=[spec(shape, kind) for shape, _, kind in outs],
        out_shape=[jax.ShapeDtypeStruct(shape, dtype) for shape, dtype, _ in outs],
        scratch_shapes=scratch,
        compiler_params=pltpu.CompilerParams(
            dimension_semantics=("arbitrary",), vmem_limit_bytes=60 * 1024 * 1024
        ),
        cost_estimate=cost(micros),
        name=name,
    )(*[a for a, _ in ins])


def signal_all(groups):
    barrier = pltpu.get_barrier_semaphore()
    for axis, peers in groups:
        for peer in peers:
            pl.semaphore_signal(barrier, inc=1, device_id={axis: peer}, device_id_type=MESH)
    pl.semaphore_wait(barrier, sum(len(peers) for _, peers in groups))


def push(src, dst, send, recv, axis, peer):
    copy = pltpu.make_async_remote_copy(
        src_ref=src, dst_ref=dst, send_sem=send, recv_sem=recv, device_id={axis: peer},
        device_id_type=MESH,
    )
    copy.start()
    return copy


def span(start, size):
    return pl.ds(pl.multiple_of(start, size), size)


def split_dp(count):
    small = 1
    while 2 * small * 2 * small * 2 <= count:
        small *= 2
    return small, count // small


def hops(count):
    return [count // 2] + [k for k in range(1, count) if k != count // 2]


class Both:
    def __init__(self, *refs):
        self.refs = refs

    def __setitem__(self, index, value):
        for ref in self.refs:
            ref[index] = value


def front_step(ins, outs, late_outs, scratch, inner, blocks, collective_id, micros):
    nt = lax.axis_size("tensor")
    length = blocks * SPAN
    total_inner = float(inner * nt)

    def body(*refs):
        refs = list(refs)

        def take(n):
            out = refs[:n]
            del refs[:n]
            return out

        plain_in = take(len(ins))
        hidden_o, vpre_o, cv_o, spre_o, scv_o, z_o, ld_o, ldt_o, yn_o, sin_o = take(len(outs))
        gate_out = take(len(late_outs))
        plain_scratch = take(len(scratch))
        gate_s, cv_s, yn_s, gn_s, slots, send, recv = refs
        wo, chp = plain_in[9], plain_in[10]
        step = pl.program_id(0)
        me = lax.axis_index("tensor")

        def peer(k):
            return lax.rem(me + k, nt)

        def copy(k, b):
            return pltpu.make_async_remote_copy(
                src_ref=slots.at[me, b], dst_ref=slots.at[me, b], send_sem=send.at[k - 1, b],
                recv_sem=recv.at[k - 1, b], device_id={"tensor": peer(k)}, device_id_type=MESH,
            )

        @pl.when(step == 0)
        def _():
            signal_all([("tensor", [peer(k) for k in range(1, nt)])])

        @pl.when(step < blocks)
        def _():
            at = span(step * SPAN, SPAN)
            fwd_kernel(
                *plain_in, hidden_o, gate_s.at[at], vpre_o, Both(cv_o, cv_s.at[at]), spre_o, scv_o,
                z_o, ld_o, ldt_o, Both(yn_o, yn_s.at[at]), sin_o, gn_s.at[at], slots.at[me, step],
                *plain_scratch,
            )
            for k in range(1, nt):
                copy(k, step).start()

        @pl.when(step >= blocks)
        def _():
            b = step - blocks
            at = span(b * SPAN, SPAN)
            for k in range(1, nt):
                copy(k, b).wait()
            total = slots[0, b]
            for source in range(1, nt):
                total = total + slots[source, b]
            gate_kernel(
                total_inner, step == blocks, gate_s.at[at], cv_s.at[at], yn_s.at[at], gn_s.at[at],
                total, chp, wo, *gate_out,
            )

    def spec(shape, kind, late):
        if kind == "whole":
            return pl.BlockSpec(shape, lambda i: (0,) * len(shape))

        def at(i):
            return (i // blocks) * (i - blocks) if late else i - (i // blocks) * (i - blocks + 1)

        if kind == "lanes":
            return pl.BlockSpec((shape[0], shape[1] // blocks), lambda i: (0, at(i)))
        return pl.BlockSpec((shape[0] // blocks, shape[1]), lambda i: (at(i), 0))

    dma = pltpu.SemaphoreType.DMA
    full = pltpu.VMEM((length, inner), F32)
    return pl.pallas_call(
        body,
        grid=(2 * blocks,),
        in_specs=[spec(a.shape, kind, False) for a, kind in ins],
        out_specs=[spec(shape, kind, False) for shape, _, kind in outs]
        + [spec(shape, kind, True) for shape, _, kind in late_outs],
        out_shape=[jax.ShapeDtypeStruct(shape, dtype) for shape, dtype, _ in outs + late_outs],
        scratch_shapes=scratch
        + [
            full, full, full, full, pltpu.VMEM((nt, blocks, 8, SPAN), F32), dma((nt - 1, blocks)),
            dma((nt - 1, blocks)),
        ],
        compiler_params=pltpu.CompilerParams(
            dimension_semantics=("arbitrary",), collective_id=collective_id, has_side_effects=True,
            vmem_limit_bytes=60 * 1024 * 1024,
        ),
        cost_estimate=cost(micros),
        name="front_scan",
    )(*[a for a, _ in ins])


def bwd_step(
    ins, outs, scratch, mixed, hidden, gate_low, cotangent, normal, blocks, collective_id, micros
):
    nt, nd = lax.axis_size("tensor"), lax.axis_size("dp")
    chips = nt // 2
    nx, nz = split_dp(nd)
    length, width = mixed.shape
    inner = gate_low.shape[1]
    half = length // 2
    rows, cols = width // nd, 2 * inner
    order = hops(nz)
    inside = nz - 2
    per = -(-inside // (blocks - 1))

    def body(*refs):
        refs = list(refs)

        def take(n):
            out = refs[:n]
            del refs[:n]
            return out

        plain_in = take(len(ins))
        mixed_h, hid_h, low_h, cot_h, nor_h = take(5)
        plain_out = take(len(outs))
        sum_o, last_o, half_o, far_o = take(4)
        plain_scratch = take(len(scratch))
        mine, near, mix, hid, low, cot, nor, dw, xslot, zsrc, zslot = take(11)
        loc, n_s, n_r, m_s, m_r, x_s, x_r, z_s, z_r = refs
        step = pl.program_id(0)
        me, md = lax.axis_index("tensor"), lax.axis_index("dp")
        side, chip = lax.rem(me, 2), me // 2
        x, z = lax.rem(md, nx), md // nx

        def remote(src, dst, send, recv, axis, peer):
            return pltpu.make_async_remote_copy(
                src_ref=src, dst_ref=dst, send_sem=send, recv_sem=recv, device_id={axis: peer},
                device_id_type=MESH,
            )

        def mate(q):
            return 2 * lax.rem(chip + q, chips) + side

        def x_peer(q):
            return z * nx + lax.rem(x + q, nx)

        def z_peer(k):
            return lax.rem(z + k, nz) * nx + x

        def mix_copy(q):
            return remote(mix, far_o.at[q - 1], m_s.at[q - 1], m_r.at[q - 1], "tensor", mate(q))

        def x_copy(q, p):
            return remote(
                dw.at[p, lax.rem(x + q, nx)], xslot.at[q - 1, p], x_s.at[q - 1, p],
                x_r.at[q - 1, p], "dp", x_peer(q),
            )

        def z_copy(p):
            return remote(
                zsrc.at[p], zslot.at[p], z_s.at[p], z_r.at[p], "dp", z_peer(order[p])
            )

        def gather_piece(p):
            for q in range(1, nx):
                x_copy(q, p).wait_recv()
            total = dw[p, x].astype(F32)
            for q in range(1, nx):
                total = total + xslot[q - 1, p].astype(F32)
            return total

        @pl.when(step == 0)
        def _():
            sibling = 2 * chip + 1 - side
            pairs = [
                (hid_h, hid), (low_h, low), (cot_h, cot), (nor_h, nor),
                (mixed_h.at[span(side * half, half)], mine),
            ]
            fetched = [
                pltpu.make_async_copy(src, dst, loc.at[n]) for n, (src, dst) in enumerate(pairs)
            ]
            for copy in fetched:
                copy.start()
            signal_all([
                ("tensor", [sibling] + [mate(q) for q in range(1, chips)]),
                ("dp", [x_peer(q) for q in range(1, nx)] + [z_peer(k) for k in range(1, nz)]),
            ])
            near_copy = remote(
                mixed_h.at[span((1 - side) * half, half)], near, n_s.at[0], n_r.at[0], "tensor",
                sibling,
            )
            near_copy.start()
            for copy in fetched[:4]:
                copy.wait()
            for p in range(nz):
                at = span(lax.rem(z + (order + [0])[p], nz) * (nx * rows), nx * rows)
                left = t_mm(hid[:, at], low[...]).astype(BF16)
                right = t_mm(cot[:, at], nor[...]).astype(BF16)
                for k in range(nx):
                    dw[p, k, :, :inner] = left[k * rows : (k + 1) * rows]
                    dw[p, k, :, inner:] = right[k * rows : (k + 1) * rows]
                for q in range(1, nx):
                    x_copy(q, p).start()
                if p == 0:
                    fetched[4].wait()
                    near_copy.wait_recv()
                    both = (mine[...].astype(F32) + near[...].astype(F32)).astype(BF16)
                    mix[...] = both
                    half_o[...] = both
                    for q in range(1, chips):
                        mix_copy(q).start()
            near_copy.wait_send()

        for s in range(1, blocks):

            @pl.when(step == s)
            def _(s=s):
                for p in range((s - 1) * per, min(s * per, inside)):
                    zsrc[p] = gather_piece(p).astype(BF16)
                    z_copy(p).start()

        bwd_kernel(*plain_in, *plain_out, *plain_scratch)

        @pl.when(step == blocks - 1)
        def _():
            last_o[...] = gather_piece(nz - 2).astype(BF16)
            total = gather_piece(nz - 1)
            for p in range(inside):
                z_copy(p).wait_recv()
                total = total + zslot[p].astype(F32)
            sum_o[...] = total
            for q in range(1, chips):
                mix_copy(q).wait()
            for p in range(inside):
                z_copy(p).wait_send()
            for p in range(nz):
                for q in range(1, nx):
                    x_copy(q, p).wait_send()

    spec = block_specs(blocks, True)
    hbm = pl.BlockSpec(memory_space=pl.ANY)
    dma = pltpu.SemaphoreType.DMA
    return pl.pallas_call(
        body,
        grid=(blocks,),
        in_specs=[spec(a.shape, kind) for a, kind in ins] + [hbm] * 5,
        out_specs=[spec(shape, kind) for shape, _, kind in outs]
        + [spec((rows, cols), "whole")] * 2
        + [spec((half, width), "whole"), hbm],
        out_shape=[jax.ShapeDtypeStruct(shape, dtype) for shape, dtype, _ in outs]
        + [
            jax.ShapeDtypeStruct((rows, cols), F32),
            jax.ShapeDtypeStruct((rows, cols), BF16),
            jax.ShapeDtypeStruct((half, width), BF16),
            jax.ShapeDtypeStruct((chips - 1, half, width), BF16),
        ],
        scratch_shapes=scratch
        + [
            pltpu.VMEM((half, width), BF16),
            pltpu.VMEM((half, width), BF16),
            pltpu.VMEM((half, width), BF16),
            pltpu.VMEM((length, width), BF16),
            pltpu.VMEM((length, inner), BF16),
            pltpu.VMEM((length, width), BF16),
            pltpu.VMEM((length, inner), BF16),
            pltpu.VMEM((nz, nx, rows, cols), BF16),
            pltpu.VMEM((nx - 1, nz, rows, cols), BF16),
            pltpu.VMEM((inside, rows, cols), BF16),
            pltpu.VMEM((inside, rows, cols), BF16),
            dma((5,)), dma((1,)), dma((1,)), dma((chips - 1,)), dma((chips - 1,)), dma((nx - 1, nz)), dma((nx - 1, nz)),
            dma((inside,)), dma((inside,)),
        ],
        compiler_params=pltpu.CompilerParams(
            dimension_semantics=("arbitrary",), collective_id=collective_id, has_side_effects=True,
            vmem_limit_bytes=60 * 1024 * 1024,
        ),
        cost_estimate=cost(micros),
        name="bwd_scan",
    )(*[a for a, _ in ins], mixed, hidden, gate_low, cotangent, normal)


def finish_kernel(
    heads, result, gtok, gate_out, last, value_step, shared, early, late,
    result_o, gtok_o, dgate_o, dvalue_o, dshared_o, dstep_o, dout_o,
    convv_o, biasv_o, convs_o, biass_o, h0_o, h1_o, h2_o, gain_o, norm_o,
):
    inner = dgate_o.shape[1]
    result_o[...] = result[...]
    gtok_o[...] = gtok[...]

    @pl.when(pl.program_id(0) == 0)
    def _():
        dgate_o[...] = gate_out[:, :inner] + last[:, :inner].astype(F32)
        dout_o[...] = gate_out[:, inner:] + last[:, inner:].astype(F32)
        dvalue_o[...] = value_step[:, :inner]
        dstep_o[...] = jnp.transpose(value_step[:, inner : inner + LANES])[:heads, :]
        dshared_o[...] = shared[...]
        convv_o[...] = early[0:4, :inner]
        biasv_o[...] = early[4:5, :inner]
        gain_o[...] = early[5:6, :inner]
        h0_o[...] = early[0:1, inner : inner + heads]
        h1_o[...] = early[1:2, inner : inner + heads]
        h2_o[...] = early[2:3, inner : inner + heads]
        convs_o[...] = late[0:4, :]
        biass_o[...] = late[4:5, :]
        norm_o[...] = late[5:6, : norm_o.shape[1]]


def tail_step(
    heads_part, dbc_part, hidden, value_low, step_low, shared_conv, shared_pre, aux, tokens, cotangent,
    ng, shared_proj, shp, mixed_half, mixed_far, last, ch_grads, head_grads, gain_part,
    collective_id, micros,
):
    length, width = tokens.shape
    inner = value_low.shape[1]
    shared_width = shared_proj.shape[1]
    nt, nd = lax.axis_size("tensor"), lax.axis_size("dp")
    ng_chips = nt // 2
    nx, nz = split_dp(nd)
    rows = width // nd
    quarter, half = length // nt, length // 2
    piece = quarter // PIECES
    part = nz * rows
    low_width = inner + LANES
    norm_width = width // nt
    early_width = inner + LANES
    late_width = shared_width
    blocks = length // SPAN
    chunk = 256
    path = hops(nz) + [0]
    n_mixed = ng_chips - 1
    n_late = 9 + n_mixed

    def body(*refs):
        refs = list(refs)

        def take(n):
            out = refs[:n]
            del refs[:n]
            return out

        heads_r, dbc, aux_r, ng_r, ws, shp_r, chg, hg, gain = take(9)
        hid_h, vlow_h, slow_h, scv_h, spre_h, tok_h, cot_h, mix_h, mixfar_h, last_h = take(10)
        result_o, gtok_o, value_o, shared_o, early_o, late_o, last_o = take(7)
        hid, low, scv, spre, tokh, tokq, cotq, mix, mixfar = take(9)
        (
            dnear, dslots, dtot, dbuf, shlow, hnear, fsrc, ffar, hacc, vbuf, vslot, sbuf, sslot,
            zv, zvslot, zs, zsslot, eslots, lslots, nbuf, nslot,
        ) = take(21)
        (
            loc, a_s, a_r, d_s, d_r, n_s, n_r, f_s, f_r, g_s, g_r, h_s, h_r, r_s, r_r,
            zv_s, zv_r, zs_s, zs_r, xv_s, xv_r, w_s, w_r, xs_s, xs_r, e_s, e_r, l_s, l_r, m_s, m_r,
        ) = take(31)

        me = lax.axis_index("tensor")
        side, chip = lax.rem(me, 2), me // 2
        sibling = 2 * chip + 1 - side
        md = lax.axis_index("dp")
        x, z = lax.rem(md, nx), md // nx

        def chip_at(q):
            return lax.rem(chip + q, ng_chips)

        def mate(q):
            return 2 * chip_at(q) + side

        def x_peer(q):
            return z * nx + lax.rem(x + q, nx)

        def z_peer(k):
            return lax.rem(z + k, nz) * nx + x

        count = [0]

        def fetch(src, dst):
            copy = pltpu.make_async_copy(src, dst, loc.at[count[0]])
            count[0] += 1
            copy.start()
            return copy

        my_rows = span(me * quarter, quarter)
        my_half = span(side * half, half)
        sib_half = span((1 - side) * half, half)
        got_low = [
            fetch(hid_h, hid), fetch(vlow_h, low.at[:, 0:inner]),
            fetch(slow_h, low.at[:, inner : inner + LANES]),
        ]
        got_mix = [fetch(mix_h, mix), fetch(tok_h.at[my_half], tokh)]
        got_mix += [fetch(mixfar_h.at[q], mixfar.at[q]) for q in range(n_mixed)]
        got_shared = [fetch(scv_h, scv), fetch(spre_h, spre)]
        got_end = [fetch(tok_h.at[my_rows], tokq), fetch(cot_h.at[my_rows], cotq)]

        signal_all([
            ("tensor", [lax.rem(me + k, nt) for k in range(1, nt)]),
            ("dp", [lax.rem(md + k, nd) for k in range(1, nd)]),
        ])
        sent = []

        def send(*args):
            copy = push(*args)
            sent.append(copy)
            return copy

        dn = send(dbc.at[sib_half], dnear, a_s.at[0], a_r.at[0], "tensor", sibling)
        last_copy = send(last_h, last_o, w_s.at[0], w_r.at[0], "dp", z_peer(path[nz - 2]))
        order = list(range(1, ng_chips)) + [0]
        near = {}
        for q in order:
            for p in range(PIECES):
                at = (2 * chip_at(q) + 1 - side) * quarter + p * piece
                near[q, p] = send(
                    heads_r.at[span(at, piece)], hnear.at[q, p], n_s.at[q, p], n_r.at[q, p],
                    "tensor", sibling,
                )
        eslots[md, :, :inner] = jnp.concatenate(
            [chg[0:5, :], gain[0:1, :], jnp.zeros((2, inner), F32)], axis=0
        )
        eslots[md, :, inner:] = hg[...]

        for copy in got_low:
            copy.wait()
        xvs = {}

        def send_piece(p):
            cols = span(lax.rem(z + path[p], nz) * (nx * rows), nx * rows)
            prod = t_mm(hid[:, cols], low[...]).astype(BF16)
            for k in range(nx):
                vbuf[p, k] = prod[k * rows : (k + 1) * rows]
            for q in range(1, nx):
                xvs[q, p] = send(
                    vbuf.at[p, lax.rem(x + q, nx)], vslot.at[q - 1, p], xv_s.at[q - 1, p],
                    xv_r.at[q - 1, p], "dp", x_peer(q),
                )

        send_piece(0)
        dn.wait_recv()
        dslots[chip] = (dbc[my_half, :] + dnear[...]).astype(BF16)
        dmates = [
            send(dslots.at[chip], dslots.at[chip], d_s.at[q], d_r.at[q], "tensor", mate(q))
            for q in range(1, ng_chips)
        ]
        fwd = {}
        for q in order:
            for p in range(PIECES):
                near[q, p].wait_recv()
                at = (2 * chip_at(q) + side) * quarter + p * piece
                both = heads_r[span(at, piece), :].astype(F32) + hnear[q, p].astype(F32)
                if q:
                    fsrc[q, p] = both.astype(BF16)
                    fwd[q, p] = send(
                        fsrc.at[q, p], ffar.at[q, p], f_s.at[q, p], f_r.at[q, p], "tensor", mate(q)
                    )
                else:
                    hacc[p * piece : (p + 1) * piece, :] = both
        es = [
            send(
                eslots.at[md], eslots.at[md], e_s.at[k], e_r.at[k], "dp", lax.rem(md + k, nd)
            )
            for k in range(1, nd)
        ]

        for p in range(1, nz):
            send_piece(p)
        zvs = []

        def own_piece(p):
            total = vbuf[p, x].astype(F32)
            for q in range(1, nx):
                xvs[q, p].wait_recv()
                total = total + vslot[q - 1, p].astype(F32)
            return total

        def pass_on(p):
            zv[p] = own_piece(p).astype(BF16)
            zvs.append(
                send(zv.at[p], zvslot.at[p], zv_s.at[p], zv_r.at[p], "dp", z_peer(path[p]))
            )

        for copy in got_shared:
            copy.wait()
        for copy in dmates:
            copy.wait_recv()
        total = dslots[0].astype(F32)
        for g in range(1, ng_chips):
            total = total + dslots[g].astype(F32)
        dtot[my_half, :] = total
        dt_copy = send(
            dtot.at[my_half], dtot.at[my_half], a_s.at[1], a_r.at[1], "tensor", sibling
        )

        pass_on(0)
        for copy in got_mix:
            copy.wait()
        mixed = mix[...].astype(F32)
        if n_mixed == 1:
            mixed = mixed + mixfar[0].astype(F32)
        else:
            terms = [mix] + [mixfar.at[q] for q in range(n_mixed)]
            mixed = jnp.zeros((half, width), F32)
            for g in range(ng_chips):
                for q in range(ng_chips):
                    mine = (lax.rem(chip - q + ng_chips, ng_chips) == g).astype(F32)
                    mixed = mixed + terms[q][...].astype(F32) * mine
        result_o[my_half, :] = (tokh[...].astype(F32) + mixed).astype(BF16)
        res = send(
            result_o.at[my_half], result_o.at[my_half], r_s.at[0], r_r.at[0], "tensor", sibling
        )

        if nz > 2:
            pass_on(1)
        dt_copy.wait_recv()
        dbuf[length : length + 8, :] = jnp.zeros((8, shared_width), F32)
        sums = [jnp.zeros((1, shared_width), F32)] * 5
        for b in reversed(range(blocks)):
            base = b * SPAN
            at = slice(base, base + SPAN)
            sc = scv[at, :]
            csig = sigmoid(sc)
            dcv = dtot[at, :] * (csig * (1.0 + sc * (1.0 - csig)))
            dbuf[at, :] = dcv
            sp = spre[at, :]
            mask = aux_r[at, :]
            ds = dcv * shp_r[3:4, :]
            sums[3] = sums[3] + jnp.sum(dcv * sp, axis=0, keepdims=True)
            sums[4] = sums[4] + jnp.sum(dcv, axis=0, keepdims=True)
            for j in range(1, 4):
                moved = dbuf[base + j : base + j + SPAN, :] * mask[:, 8 + j : 9 + j]
                ds = ds + moved * shp_r[3 - j : 4 - j, :]
                sums[3 - j] = sums[3 - j] + jnp.sum(moved * sp, axis=0, keepdims=True)
            shlow[at, :] = ds.astype(BF16)
        for p in range(2, nz - 1):
            pass_on(p)
        for c in range(width // chunk):
            prod = t_mm(hid[:, c * chunk : (c + 1) * chunk], shlow[...]).astype(BF16)
            for d in range(c * chunk // rows, (c + 1) * chunk // rows):
                at = slice(d * rows - c * chunk, (d + 1) * rows - c * chunk)
                sbuf[d % nx, (d // nx) * rows : (d // nx + 1) * rows, :] = prod[at]
        xss = [
            send(
                sbuf.at[lax.rem(x + q, nx)], sslot.at[q], xs_s.at[q], xs_r.at[q], "dp", x_peer(q)
            )
            for q in range(1, nx)
        ]
        hacc[...] = hacc[...] + mm_t(shlow[my_rows, :], ws[...])

        for copy in got_end:
            copy.wait()
        norm = jnp.zeros((1, width), F32)
        gather, own = {}, []
        for p in range(PIECES):
            at = slice(p * piece, (p + 1) * piece)
            grad_hidden = hacc[at, :]
            for q in range(1, ng_chips):
                fwd[q, p].wait_recv()
                grad_hidden = grad_hidden + ffar[q, p].astype(F32)
            v = tokq[at, :].astype(F32)
            inv = lax.rsqrt(jnp.mean(v * v, axis=1, keepdims=True) + EPSILON)
            normed = v * inv
            scaled = grad_hidden * ng_r[...]
            norm = norm + jnp.sum(grad_hidden * normed, axis=0, keepdims=True)
            mean = jnp.mean(scaled * normed, axis=1, keepdims=True)
            place = span(me * quarter + p * piece, piece)
            gtok_o[place, :] = (inv * (scaled - normed * mean) + cotq[at, :].astype(F32)).astype(BF16)
            for q in range(1, ng_chips):
                gather[q, p] = send(
                    gtok_o.at[place], gtok_o.at[place], g_s.at[q, p], g_r.at[q, p], "tensor", mate(q)
                )
            own.append(
                send(gtok_o.at[place], gtok_o.at[place], h_s.at[0, p], h_r.at[0, p], "tensor", sibling)
            )
        for q in range(nt):
            nbuf[q] = norm[:, q * norm_width : (q + 1) * norm_width] + jnp.zeros((8, norm_width), F32)
        norms = [
            send(
                nbuf.at[lax.rem(me + k, nt)], nslot.at[k], m_s.at[k], m_r.at[k], "tensor",
                lax.rem(me + k, nt),
            )
            for k in range(1, nt)
        ]

        for copy in xss:
            copy.wait_recv()
        total = sbuf[x].astype(F32)
        for q in range(1, nx):
            total = total + sslot[q].astype(F32)
        zs[...] = total.astype(BF16)
        zss = [
            send(
                zs.at[span(lax.rem(z + k, nz) * rows, rows)], zsslot.at[k], zs_s.at[k], zs_r.at[k],
                "dp", z_peer(k),
            )
            for k in range(1, nz)
        ]

        for copy in norms:
            copy.wait_recv()
        total = nbuf[me]
        for k in range(1, nt):
            total = total + nslot[k]
        wide = jnp.concatenate(
            [total[0:1, :], jnp.zeros((1, shared_width - norm_width), F32)], axis=1
        ) if norm_width < shared_width else total[0:1, :]
        lslots[md] = jnp.concatenate(sums + [wide, jnp.zeros((2, shared_width), F32)], axis=0)
        ls = [
            send(
                lslots.at[md], lslots.at[md], l_s.at[k], l_r.at[k], "dp", lax.rem(md + k, nd)
            )
            for k in range(1, nd)
        ]

        for copy in es:
            copy.wait_recv()
        total = eslots[0]
        for s in range(1, nd):
            total = total + eslots[s]
        early_o[...] = total

        for p in range(PIECES):
            for q in range(1, ng_chips):
                gather[q, p].wait_recv()
                came = 2 * lax.rem(chip - q + ng_chips, ng_chips) + side
                place = span(came * quarter + p * piece, piece)
                own.append(
                    send(
                        gtok_o.at[place], gtok_o.at[place], h_s.at[q, p], h_r.at[q, p],
                        "tensor", sibling,
                    )
                )

        for copy in zvs:
            copy.wait_recv()
        total = own_piece(nz - 1)
        for p in range(nz - 1):
            total = total + zvslot[p].astype(F32)
        value_o[...] = total
        for copy in zss:
            copy.wait_recv()
        total = zs[span(z * rows, rows), :].astype(F32)
        for k in range(1, nz):
            total = total + zsslot[k].astype(F32)
        shared_o[...] = total

        for copy in ls:
            copy.wait_recv()
        total = lslots[0]
        for s in range(1, nd):
            total = total + lslots[s]
        late_o[...] = total

        res.wait_recv()
        last_copy.wait_recv()
        for copy in own:
            copy.wait_recv()
        for copy in sent:
            copy.wait_send()

    vm = pl.BlockSpec(memory_space=pltpu.VMEM)
    hbm = pl.BlockSpec(memory_space=pl.ANY)
    dma = pltpu.SemaphoreType.DMA

    def f32(*shape):
        return pltpu.VMEM(shape, F32)

    def bf16(*shape):
        return pltpu.VMEM(shape, BF16)

    def out(*shape):
        return jax.ShapeDtypeStruct(shape, F32)

    early = [heads_part, dbc_part, aux, ng, shared_proj, shp, ch_grads, head_grads, gain_part]
    late = [hidden, value_low, step_low, shared_conv, shared_pre, tokens, cotangent, mixed_half]
    late += [mixed_far, last]
    return pl.pallas_call(
        body,
        in_specs=[vm] * len(early) + [hbm] * len(late),
        out_specs=[vm] * 6 + [hbm],
        out_shape=[
            jax.ShapeDtypeStruct((length, width), BF16), jax.ShapeDtypeStruct((length, width), BF16),
            out(rows, low_width), out(rows, shared_width), out(8, early_width), out(8, late_width),
            jax.ShapeDtypeStruct(last.shape, last.dtype),
        ],
        scratch_shapes=[
            bf16(length, width), bf16(length, low_width), f32(length, shared_width),
            f32(length, shared_width), bf16(half, width), bf16(quarter, width), bf16(quarter, width),
            bf16(half, width), bf16(n_mixed, half, width),
            f32(half, shared_width), bf16(ng_chips, half, shared_width), f32(length, shared_width),
            f32(length + 8, shared_width), bf16(length, shared_width),
            bf16(ng_chips, PIECES, piece, width), bf16(ng_chips, PIECES, piece, width),
            bf16(ng_chips, PIECES, piece, width), f32(quarter, width),
            bf16(nz, nx, rows, low_width), bf16(nx - 1, nz, rows, low_width),
            bf16(nx, part, shared_width), bf16(nx, part, shared_width),
            bf16(nz - 1, rows, low_width), bf16(nz - 1, rows, low_width),
            bf16(part, shared_width), bf16(nz, rows, shared_width),
            f32(nd, 8, early_width), f32(nd, 8, late_width),
            f32(nt, 8, norm_width), f32(nt, 8, norm_width),
        ]
        + [dma((n_late + 1,)), dma((2,)), dma((2,)), dma((ng_chips,)), dma((ng_chips,))]
        + [dma((ng_chips, PIECES))] * 8
        + [dma((1,)), dma((1,))]
        + [dma((nz,))] * 4
        + [dma((nx - 1, nz))] * 2
        + [dma((1,))] * 2
        + [dma((nx,))] * 2
        + [dma((nd,))] * 4
        + [dma((nt,))] * 2,
        compiler_params=pltpu.CompilerParams(
            collective_id=collective_id, has_side_effects=True, vmem_limit_bytes=60 * 1024 * 1024
        ),
        cost_estimate=cost(micros),
        name="tail_step",
    )(*early, *late)


def per_device(
    tokens, cotangent, segments, norm_gain, gate_proj, value_proj, shared_proj, step_proj,
    conv_value, bias_value, conv_shared, bias_shared, step_bias, decay_log, skip_gain,
    gate_gain, out_proj,
):
    tp_count = lax.axis_size("tensor")
    dp_count = lax.axis_size("dp")
    length, width = tokens.shape
    inner = gate_proj.shape[1]
    heads = step_proj.shape[1]
    shared_width = shared_proj.shape[1]
    state_size = shared_width // 2
    blocks = length // SPAN
    aux, segr, wst, chp, shp, hp = pl.pallas_call(
        prep_kernel,
        out_shape=[
            jax.ShapeDtypeStruct((length, LANES), F32),
            jax.ShapeDtypeStruct((1, length), F32),
            jax.ShapeDtypeStruct((width, LANES), BF16),
            jax.ShapeDtypeStruct((8, inner), F32),
            jax.ShapeDtypeStruct((8, shared_width), F32),
            jax.ShapeDtypeStruct((8, LANES), F32),
        ],
        name="prep_step",
    )(
        segments, step_proj.T, conv_value, bias_value[None], gate_gain[None], skip_gain[None],
        conv_shared, bias_shared[None], step_bias[None], decay_log[None],
    )
    ng = norm_gain[None, :]

    (
        hidden, value_pre, conv_out, shared_pre, shared_conv, z, ld, ldt, yn, sin,
        normal_out, dy, gate_low, gain_part, mixed_part,
    ) = front_step(
        [
            (tokens, "rows"), (cotangent, "rows"), (aux, "rows"), (segr, "lanes"), (ng, "whole"),
            (gate_proj, "whole"), (value_proj, "whole"), (shared_proj, "whole"), (wst, "whole"),
            (out_proj, "whole"), (chp, "whole"), (shp, "whole"), (hp, "whole"),
        ],
        [
            ((length, width), BF16, "rows"),
            ((length, inner), F32, "rows"),
            ((length, inner), F32, "rows"),
            ((length, shared_width), F32, "rows"),
            ((length, shared_width), F32, "rows"),
            ((length, LANES), F32, "rows"),
            ((length, LANES), F32, "rows"),
            ((8, length), F32, "lanes"),
            ((length, inner), F32, "rows"),
            ((blocks * state_size, inner), F32, "rows"),
        ],
        [
            ((length, inner), BF16, "rows"),
            ((length, inner), F32, "rows"),
            ((length, inner), BF16, "rows"),
            ((8, inner), F32, "whole"),
            ((length, width), BF16, "rows"),
        ],
        [
            pltpu.VMEM((SPAN + 8, inner), F32),
            pltpu.VMEM((SPAN + 8, shared_width), F32),
            pltpu.VMEM((state_size, inner), F32),
        ],
        inner, blocks, 0, 29,
    )
    (
        value_low, step_low, heads_part, dbc_part, ch_grads, head_grads, gate_out, last, mixed_half,
        mixed_far,
    ) = bwd_step(
        [
            (dy, "rows"), (conv_out, "rows"), (value_pre, "rows"), (shared_conv, "rows"),
            (z, "rows"), (ld, "rows"), (ldt, "lanes"), (yn, "rows"), (sin, "rows"),
            (aux, "rows"), (segr, "lanes"), (gate_low, "rows"), (gate_proj, "whole"),
            (value_proj, "whole"), (wst, "whole"), (chp, "whole"), (hp, "whole"),
        ],
        [
            ((length, inner), BF16, "rows"),
            ((length, LANES), BF16, "rows"),
            ((length, width), BF16, "rows"),
            ((length, shared_width), F32, "rows"),
            ((8, inner), F32, "whole"),
            ((8, LANES), F32, "whole"),
        ],
        [pltpu.VMEM((SPAN + 8, inner), F32), pltpu.VMEM((state_size, inner), F32)],
        mixed_part, hidden, gate_low, cotangent, normal_out, blocks, 3, 30,
    )
    result, grad_tokens, value_step, shared_sum, early, late, last = tail_step(
        heads_part, dbc_part, hidden, value_low, step_low, shared_conv, shared_pre, aux, tokens,
        cotangent, ng, shared_proj, shp, mixed_half, mixed_far, last, ch_grads, head_grads,
        gain_part, 2, 40,
    )

    def finish_body(*refs):
        finish_kernel(heads, *refs)

    rows = width // dp_count
    (
        result, grad_tokens, dgate, dvalue, dshared, dstep, dout,
        convv, biasv, convs, biass, h0, h1, h2, gain, norm,
    ) = call(
        finish_body,
        blocks,
        [
            (result, "rows"), (grad_tokens, "rows"), (gate_out, "whole"), (last, "whole"),
            (value_step, "whole"),
            (shared_sum, "whole"), (early, "whole"), (late, "whole"),
        ],
        [
            ((length, width), BF16, "rows"), ((length, width), BF16, "rows"),
            ((rows, inner), F32, "whole"), ((rows, inner), F32, "whole"),
            ((rows, shared_width), F32, "whole"), ((heads, rows), F32, "whole"),
            ((rows, inner), F32, "whole"), ((4, inner), F32, "whole"), ((1, inner), F32, "whole"),
            ((4, shared_width), F32, "whole"), ((1, shared_width), F32, "whole"),
            ((1, heads), F32, "whole"), ((1, heads), F32, "whole"), ((1, heads), F32, "whole"),
            ((1, inner), F32, "whole"), ((1, width // tp_count), F32, "whole"),
        ],
        [],
        False,
        "finish_step",
        3,
    )
    return (
        result, grad_tokens, norm[0], dgate, dvalue, dshared, dstep.T, convv, biasv[0], convs, biass[0],
        h0[0], h1[0], h2[0], gain[0], dout,
    )


def solution(mesh):
    rows, cols, vec = P("dp", None), P(None, "tensor"), P("tensor")
    return jax.shard_map(
        per_device,
        mesh=mesh,
        in_specs=(
            rows, rows, rows, P(), cols, cols, P(), cols, cols, vec, P(), P(), vec, vec, vec, vec, cols,
        ),
        out_specs=(
            rows, rows, vec, P("dp", "tensor"), P("dp", "tensor"), rows, P("dp", "tensor"), cols, vec,
            P(), P(), vec, vec, vec, vec, P("dp", "tensor"),
        ),
        check_vma=False,
    )
```
